32 devices in a mesh: wide: 16 (over z, x, core), narrow: 2 (over y).
Axes of the slice: x: 2, y: 2, z: 4, core: 2. Of those that a mesh axis runs over, the one named last changes fastest.
Arguments:
- question_word_vectors: bfloat16 [32, 64, 768], P(('wide', 'narrow')), may hold values from -6 to 6
- question_numbers: int32 [32, 64], P(('wide', 'narrow')), may hold values from 0 to 2, never falling along the last dimension, each value on 1 to 40 neighbouring positions
- document_word_vectors: bfloat16 [32, 256, 768], P(('wide', 'narrow')), may hold values from -6 to 6
- document_numbers: int32 [32, 256], P(('wide', 'narrow')), may hold values from 0 to 3, never falling along the last dimension, each value on 1 to 106 neighbouring positions
- matching_document: int32 [96], P(('wide', 'narrow')), may hold values from 0 to 127
- distance_class_lookup: int32 [511], replicated, may hold values from 0 to 31
- softness_scalar: float32 [1], replicated, may hold values from 0.01 to 0.04
- distance_shift_grid: float32 [32, 12], replicated, may hold values from -4 to 4
- rescale_factors: float32 [3, 768], replicated, may hold values from 0.5 to 1.5
- asking_matrix: bfloat16 [768, 768], replicated, may hold values from -0.109375 to 0.109375
- addressing_matrix: bfloat16 [768, 768], replicated, may hold values from -0.109375 to 0.109375
- content_matrix: bfloat16 [768, 768], replicated, may hold values from -0.21875 to 0.21875
- attention_merge_matrix: bfloat16 [768, 768], replicated, may hold values from -1.75 to 1.75
- gating_matrix: bfloat16 [768, 2048], replicated, may hold values from -0.21875 to 0.21875
- expansion_matrix: bfloat16 [768, 2048], replicated, may hold values from -0.21875 to 0.21875
- contraction_matrix: bfloat16 [2048, 768], replicated, may hold values from -0.1875 to 0.1875
- pooling_matrix: bfloat16 [768, 768], replicated, may hold values from -0.21875 to 0.21875
Outputs:
- loss: float32 [1], replicated
- query_vectors: float32 [96, 768], P(('wide', 'narrow'))
- passage_vectors: float32 [128, 768], P(('wide', 'narrow'))
- query_grads: float32 [32, 64, 768], P(('wide', 'narrow'))
- passage_grads: float32 [32, 256, 768], P(('wide', 'narrow'))
- gain_grads: float32 [3, 768], replicated
- bias_grads: float32 [32, 12], replicated
- grad_query_w: float32 [768, 768], P('narrow', 'wide')
- grad_key_w: float32 [768, 768], P('narrow', 'wide')
- grad_value_w: float32 [768, 768], P('narrow', 'wide')
- grad_out_w: float32 [768, 768], P('narrow', 'wide')
- grad_gate_w: float32 [768, 2048], P('narrow', 'wide')
- grad_up_w: float32 [768, 2048], P('narrow', 'wide')
- grad_down_w: float32 [2048, 768], P('narrow', 'wide')
- grad_proj_w: float32 [768, 768], P('narrow', 'wide')
The draws below stay inside these ranges and needn't reach their ends.
Inputs may be any that keep to these rules, and one draw needn't show every extreme that they name: `question_numbers`: query ids of a row never fall, every query has at least one token and at most 40. `document_numbers`: passage ids of a row never fall, every passage has at least one token and at most 106. `matching_document`: passages numbered over all passage rows, row by row. `distance_class_lookup`: entry j - i + 255 is the bucket of key j seen from token i.
All inputs are finite; a program needn't handle non-finite values.
Results may differ from the reference program's by a relative error of at most 0.03.
Values may be sent and summed in bfloat16 or wider, within the bound.
No kernel may reach another device: no remote copies, remote signals or barrier semaphores. Data moves between devices by JAX's collectives and lax.ppermute only.
A program may use at most 192 MiB of HBM per device.

```python
import math
from functools import partial
import jax
import jax.numpy as jnp
import numpy as np
from jax import lax

D = 768
HEADS = 12
HDIM = 64
FF = 2048
BUCKETS = 32
LAYERS = 2
QLEN = 64
PLEN = 256
QSEGS = 3
PSEGS = 4
NQROWS = 32
NPROWS = 32
NQ = 96
NPASS = 128
QMOST = 40
PMOST = 106


def plant(result, key, smallest, top_value):
    shape = result.shape
    index_at = [jax.random.randint(jax.random.fold_in(key, axis), (), 0, shape[axis]) for axis in range(len(shape))]
    result = result.at[tuple(index_at)].set(smallest)
    longest = shape.index(max(shape))
    index_at[longest] = (index_at[longest] + 1) % shape[longest]
    return result.at[tuple(index_at)].set(top_value)


def level_of(rng, dims, shards, smallest, high):
    level = 1.0
    for dim, shards_of in shards:
        heights = jax.random.uniform(jax.random.fold_in(jax.random.fold_in(rng, 6), dim), (shards_of,), jnp.float32, smallest / len(shards), high / len(shards))
        level = level * jnp.repeat(jnp.exp(heights), dims[dim] // shards_of).reshape((-1,) + (1,) * (len(dims) - 1 - dim))
    return level


def split_up(count, total, limit, slope):
    portions = [(1 << 20) // math.isqrt(grade ** slope) + 1 for grade in range(2, count + 1)]
    spare, counts = total - limit - (count - 1), [1] * (count - 1)
    while spare > 0:
        movable = [i for i in range(count - 1) if counts[i] < limit]
        mass, budget = sum([portions[i] for i in movable]), spare
        for i in movable:
            more = min(limit - counts[i], max(1, budget * portions[i] // mass), spare)
            counts[i] = counts[i] + more
            spare = spare - more
    return np.array([limit] + counts)


def uneven(key, count, total, most, skew):
    if count == 2:
        one = jax.random.randint(key, (), max(1, total - most), min(most, total - 1) + 1)
        return jnp.stack([one, total - one])
    lengths = jnp.asarray(split_up(count, total, most, skew), jnp.int32)
    couples = (count - 1) // 2
    donor, sink = lengths[1:1 + 2 * couples:2], lengths[2:2 + 2 * couples:2]
    margin = jnp.minimum(donor - 1, most - sink)
    passed = jax.random.randint(jax.random.fold_in(key, 1), (couples,), 0, 1 << 20) % (margin + 1)
    lengths = lengths.at[1:1 + 2 * couples:2].set(donor - passed).at[2:2 + 2 * couples:2].set(sink + passed)
    return lengths[jax.random.permutation(jax.random.fold_in(key, 2), count)]


def noise(rng, extent, spread, reach, split=(), held_as=jnp.bfloat16):
    level = level_of(rng, extent, split, -0.22, 0.18) if split else 1.0
    result = jax.random.normal(rng, extent, jnp.float32) * spread * level
    return jnp.minimum(jnp.maximum(result, -reach), reach).astype(held_as)


def setup_inputs(seed: int = 0) -> dict:
    keys = jax.random.split(jax.random.key(seed), 18)
    question_word_vectors = noise(keys[0], (NQROWS, QLEN, D), 1.0, 6.0, ((0, 32),))
    question_numbers = jax.vmap(lambda own: jnp.searchsorted(jnp.cumsum(uneven(own, QSEGS, QLEN, QMOST, 0)), jnp.arange(QLEN), side="right"))(jax.random.split(keys[1], NQROWS)).reshape((NQROWS, QLEN)).astype(jnp.int32)
    document_word_vectors = noise(keys[2], (NPROWS, PLEN, D), 1.0, 6.0, ((0, 32),))
    document_numbers = jax.vmap(lambda own: jnp.searchsorted(jnp.cumsum(uneven(own, PSEGS, PLEN, PMOST, 0)), jnp.arange(PLEN), side="right"))(jax.random.split(keys[3], NPROWS)).reshape((NPROWS, PLEN)).astype(jnp.int32)
    matching_document = plant(jax.random.randint(keys[4], (NQ,), 0, NPASS), jax.random.fold_in(keys[4], 1), 0, NPASS - 1).astype(jnp.int32)
    distance_class_lookup = plant(jax.random.randint(keys[5], (2 * PLEN - 1,), 0, BUCKETS), jax.random.fold_in(keys[5], 1), 0, BUCKETS - 1).astype(jnp.int32)
    softness_scalar = jnp.clip(jnp.exp(jax.random.uniform(keys[6], (1,), jnp.float32, math.log(0.01), math.log(0.04))), 0.01, 0.04)
    distance_shift_grid = noise(keys[7], (BUCKETS, HEADS), 1.0, 4.0, (), jnp.float32)
    rescale_factors = jnp.clip(1.0 + 0.1 * jax.random.normal(keys[8], (3, D), jnp.float32), 0.5, 1.5)
    asking_matrix = noise(keys[9], (D, HEADS * HDIM), (4 * D) ** -0.5, 0.109375)
    addressing_matrix = noise(keys[10], (D, HEADS * HDIM), (4 * D) ** -0.5, 0.109375)
    content_matrix = noise(keys[11], (D, HEADS * HDIM), D ** -0.5, 0.21875)
    attention_merge_matrix = noise(keys[12], (HEADS * HDIM, D), (HEADS * HDIM // 64) ** -0.5, 1.75)
    gating_matrix = noise(keys[13], (D, FF), D ** -0.5, 0.21875)
    expansion_matrix = noise(keys[14], (D, FF), D ** -0.5, 0.21875)
    contraction_matrix = noise(keys[15], (FF, D), (FF // 2) ** -0.5, 0.1875)
    pooling_matrix = noise(keys[16], (D, D), D ** -0.5, 0.21875)
    return dict(question_word_vectors=question_word_vectors, question_numbers=question_numbers, document_word_vectors=document_word_vectors, document_numbers=document_numbers, matching_document=matching_document, distance_class_lookup=distance_class_lookup, softness_scalar=softness_scalar, distance_shift_grid=distance_shift_grid, rescale_factors=rescale_factors, asking_matrix=asking_matrix, addressing_matrix=addressing_matrix, content_matrix=content_matrix, attention_merge_matrix=attention_merge_matrix, gating_matrix=gating_matrix, expansion_matrix=expansion_matrix, contraction_matrix=contraction_matrix, pooling_matrix=pooling_matrix)


@jax.custom_vjp
def low(v):
    return lax.optimization_barrier(v.astype(jnp.bfloat16)).astype(jnp.float32)

@jax.custom_vjp
def low_back(v):
    return v

def low_keep(v):
    return (low(v), None)

def low_pass(kept, grad):
    return (grad,)

def back_keep(v):
    return (v, None)

def back_low(kept, grad):
    return (low(grad),)
low.defvjp(low_keep, low_pass)
low_back.defvjp(back_keep, back_low)
HIGHEST = lax.Precision.HIGHEST
EPSILON = 1e-06
MASKED = -1000000000.0

def round_both(array_in):
    return low_back(low(array_in))

def matmul(operand_a, operand_b):
    return jnp.dot(operand_a, operand_b, precision=HIGHEST)

def rms_norm(x, gain_vec):
    return x * lax.rsqrt(lax.optimization_barrier(jnp.mean(x * x, axis=-1, keepdims=True)) + EPSILON) * gain_vec

def offset_bias(distance_shift_grid, distance_class_lookup, length):
    places = jnp.arange(length, dtype=jnp.int32)
    offsets = places[None, :] - places[:, None] + (PLEN - 1)
    return jnp.transpose(distance_shift_grid[distance_class_lookup[offsets]], (2, 0, 1))

def attend(h, segments, bias_block, asking_matrix, addressing_matrix, content_matrix, attention_merge_matrix):
    row_count, length = segments.shape
    q = round_both(matmul(h, asking_matrix)).reshape(row_count, length, HEADS, HDIM)
    k = round_both(matmul(h, addressing_matrix)).reshape(row_count, length, HEADS, HDIM)
    v = round_both(matmul(h, content_matrix)).reshape(row_count, length, HEADS, HDIM)
    raw_scores = low_back(jnp.einsum('rihd,rjhd->rhij', q, k, precision=HIGHEST))
    scores = raw_scores + bias_block[None]
    same_seg = (segments[:, :, None] == segments[:, None, :])[:, None]
    probs_low = low(jax.nn.softmax(jnp.where(same_seg, scores, MASKED), axis=-1))
    attended = round_both(jnp.einsum('rhij,rjhd->rihd', probs_low, v, precision=HIGHEST))
    return low_back(matmul(attended.reshape(row_count, length, HEADS * HDIM), attention_merge_matrix))

def apply_layer(x, segments, bias_block, rescale_factors, parameter_set):
    asking_matrix, addressing_matrix, content_matrix, attention_merge_matrix, gating_matrix, expansion_matrix, contraction_matrix = parameter_set
    h = low(rms_norm(x, rescale_factors[0]))
    x = x + attend(h, segments, bias_block, asking_matrix, addressing_matrix, content_matrix, attention_merge_matrix)
    normed = low(rms_norm(x, rescale_factors[1]))
    a = low_back(matmul(normed, gating_matrix))
    b = low_back(matmul(normed, expansion_matrix))
    u = low(jax.nn.gelu(a, approximate=True) * b)
    return x + low_back(matmul(u, contraction_matrix))

def run_tower(shared, operands, seg_count):
    bias_block, rescale_factors, parameter_set, pooling_matrix = shared
    x, segments = operands
    for repeat in range(LAYERS):
        x = apply_layer(x, segments, bias_block, rescale_factors, parameter_set)
    z = rms_norm(x, rescale_factors[2])
    seg_table = (segments[:, None, :] == jnp.arange(seg_count, dtype=jnp.int32)[None, :, None]).astype(jnp.float32)
    seg_sizes = lax.optimization_barrier(jnp.sum(seg_table, axis=2))
    pooled = jnp.einsum('rsl,rld->rsd', seg_table, z, precision=HIGHEST) / seg_sizes[:, :, None]
    e = low_back(matmul(low(pooled), pooling_matrix))
    return e * lax.rsqrt(lax.optimization_barrier(jnp.sum(e * e, axis=-1, keepdims=True)) + EPSILON)

def tower_all(shared, embeds, segments, group_rows, seg_count):
    total_rows, length, feature_dim = embeds.shape
    checked = jax.checkpoint(partial(run_tower, seg_count=seg_count))

    def one_group(operands):
        return checked(shared, operands)
    vectors = lax.map(one_group, (embeds.reshape(-1, group_rows, length, feature_dim), segments.reshape(-1, group_rows, length)))
    return vectors.reshape(-1, feature_dim)

def reference(question_word_vectors, question_numbers, document_word_vectors, document_numbers, matching_document, distance_class_lookup, softness_scalar, distance_shift_grid, rescale_factors, asking_matrix, addressing_matrix, content_matrix, attention_merge_matrix, gating_matrix, expansion_matrix, contraction_matrix, pooling_matrix):

    def forward(query_x, passage_x, bias_table, gain_table, wq_f, wk_f, wv_f, wo_f, wg_f, wu_f, wd_f, wp_f):
        parameter_set = (wq_f, wk_f, wv_f, wo_f, wg_f, wu_f, wd_f)
        query_bias = offset_bias(bias_table, distance_class_lookup, QLEN)
        passage_bias = offset_bias(bias_table, distance_class_lookup, PLEN)
        query_vectors = tower_all((query_bias, gain_table, parameter_set, wp_f), query_x, question_numbers, math.gcd(NQROWS, 16), QSEGS)
        passage_vectors = tower_all((passage_bias, gain_table, parameter_set, wp_f), passage_x, document_numbers, math.gcd(NPROWS, 4), PSEGS)
        plain_dot_scores = low_back(matmul(low(query_vectors), low(passage_vectors).T))
        match_scores = plain_dot_scores / softness_scalar[0]
        correct_label = matching_document[:, None] == jnp.arange(NPASS, dtype=jnp.int32)[None, :]
        loss_total = jnp.sum(jax.nn.logsumexp(match_scores, axis=1) - lax.optimization_barrier(jnp.sum(jnp.where(correct_label, match_scores, 0.0), axis=1)))
        return (loss_total, (query_vectors, passage_vectors))
    matrices = tuple((matrix.astype(jnp.float32) for matrix in (asking_matrix, addressing_matrix, content_matrix, attention_merge_matrix, gating_matrix, expansion_matrix, contraction_matrix, pooling_matrix)))
    loss_total, pullback, vectors = jax.vjp(forward, question_word_vectors.astype(jnp.float32), document_word_vectors.astype(jnp.float32), distance_shift_grid, rescale_factors, *matrices, has_aux=True)
    gradients = pullback(jnp.ones_like(loss_total))
    mean_loss = (loss_total / NQ).reshape(1)
    return (mean_loss, vectors[0], vectors[1], gradients[0], gradients[1], gradients[3], gradients[2], gradients[4], gradients[5], gradients[6], gradients[7], gradients[8], gradients[9], gradients[10], gradients[11])
```

```python
import functools

import jax
import jax.numpy as jnp
from jax import lax
from jax.experimental import pallas as pl
from jax.experimental.pallas import tpu as pltpu
from jax.sharding import PartitionSpec as P

LAYERS = 2
QSEGS = 3
PSEGS = 4
HDIM = 64
PACK = 8

HIGHEST = lax.Precision.HIGHEST
EPSILON = 1e-06
MASKED = -1000000000.0
BF = jnp.bfloat16
F32 = jnp.float32
AXES = ("wide", "narrow")


def low(a):
    return a.astype(BF)


def product(a, b):
    return jnp.dot(a, b, preferred_element_type=F32)


def dot_tn(a, b, precision=None):
    return lax.dot_general(
        a, b, (((0,), (0,)), ((), ())), preferred_element_type=F32, precision=precision
    )


def dot_nt(a, b, precision=None):
    return lax.dot_general(
        a, b, (((1,), (1,)), ((), ())), preferred_element_type=F32, precision=precision
    )


def rms_norm(x, gain_vec):
    return x * lax.rsqrt(jnp.mean(x * x, axis=-1, keepdims=True) + EPSILON) * gain_vec


def norm_back(x, gain_vec, grad_in):
    outcome, pullback = jax.vjp(rms_norm, x, gain_vec)
    return pullback(grad_in)


def gated_unit(a, b):
    return jax.nn.gelu(a, approximate=True) * b


def unit_norm(e):
    return e * lax.rsqrt(jnp.sum(e * e, axis=-1, keepdims=True) + EPSILON)


def whole():
    return pl.BlockSpec(memory_space=pltpu.VMEM)


def bias_kernel(qlen, plen, lookup_ref, grid_ref, qseg_ref, pseg_ref, pbias_ref, qbias_ref):
    buckets, heads = grid_ref.shape
    width = lookup_ref.shape[1]
    onehot = (
        lax.broadcasted_iota(jnp.int32, (buckets, width), 0)
        == jnp.broadcast_to(lookup_ref[...], (buckets, width))
    ).astype(F32)
    table = dot_tn(grid_ref[...], onehot, HIGHEST)
    pcol = jnp.transpose(jnp.broadcast_to(pseg_ref[...], (plen, plen)))
    psame = pcol == jnp.broadcast_to(pseg_ref[...], (plen, plen))
    qcol = jnp.transpose(jnp.broadcast_to(qseg_ref[...], (128, 128)))
    qsame = (qcol == jnp.broadcast_to(qseg_ref[...], (128, 128)))[:qlen, :qlen]
    for head in range(heads):
        rows = jnp.broadcast_to(table[head : head + 1, :], (plen, width))
        rolled = pltpu.roll(rows, width - (plen - 1), 1, stride=1, stride_axis=0)
        block = rolled[:, :plen]
        pbias_ref[head] = jnp.where(psame, block, MASKED)
        qbias_ref[head] = jnp.where(qsame, block[:qlen, :qlen], MASKED)


def bias_blocks(lookup, grid, qseg, pseg):
    heads = grid.shape[1]
    qlen, plen = qseg.shape[1], pseg.shape[1]
    width = 2 * plen
    padded = jnp.pad(lookup, (0, width - lookup.shape[0]), constant_values=-1)[None]
    qpad = jnp.pad(qseg, ((0, 0), (0, 128 - qlen)), constant_values=-1)
    return pl.pallas_call(
        functools.partial(bias_kernel, qlen, plen),
        out_shape=(
            jax.ShapeDtypeStruct((heads, plen, plen), F32),
            jax.ShapeDtypeStruct((heads, qlen, qlen), F32),
        ),
        in_specs=[whole()] * 4,
        out_specs=(whole(), whole()),
        name="bias_blocks",
    )(padded, grid, qpad, pseg)


def half_mask(lanes, side):
    return (lax.broadcasted_iota(jnp.int32, (1, lanes), 1) // HDIM) == side


def attend_kernel(qlen, q_ref, k_ref, v_ref, pbias_ref, qbias_ref, o_ref, pp_ref, pq_ref):
    pairs = q_ref.shape[1] // 128
    spans = ((0, qlen, qbias_ref, pq_ref), (qlen, q_ref.shape[0] - qlen, pbias_ref, pp_ref))

    def pair(i, carry):
        lanes = pl.ds(pl.multiple_of(i * 128, 128), 128)
        for start, length, bias_ref, keep_ref in spans:
            rows = pl.ds(start, length)
            q2, k2, v2 = q_ref[rows, lanes], k_ref[rows, lanes], v_ref[rows, lanes]
            total = None
            for side in range(2):
                mine = half_mask(128, side)
                zero = jnp.zeros_like(k2)
                s = dot_nt(q2, jnp.where(mine, k2, zero)) + bias_ref[2 * i + side]
                top = jnp.max(s, axis=-1, keepdims=True)
                e = jnp.exp(s - top)
                p = low(e * (1.0 / jnp.sum(e, axis=-1, keepdims=True)))
                keep_ref[2 * i + side] = p
                part = product(p, jnp.where(mine, v2, zero))
                total = part if total is None else total + part
            o_ref[rows, lanes] = low(total)
        return carry

    lax.fori_loop(0, pairs, pair, 0)


def attend(q, k, v, pbias, qbias):
    heads, plen, _ = pbias.shape
    qlen = qbias.shape[1]
    return pl.pallas_call(
        functools.partial(attend_kernel, qlen),
        out_shape=(
            jax.ShapeDtypeStruct(q.shape, BF),
            jax.ShapeDtypeStruct((heads, plen, plen), BF),
            jax.ShapeDtypeStruct((heads, qlen, qlen), BF),
        ),
        in_specs=[whole()] * 5,
        out_specs=(whole(),) * 3,
        name="attend",
    )(q, k, v, pbias, qbias)


def attend_back_kernel(
    qlen, q_ref, k_ref, v_ref, o_ref, go_ref, pp_ref, pq_ref, acc_ref, gq_ref, gk_ref, gv_ref, ds_ref
):
    pairs = q_ref.shape[1] // 128
    plen = q_ref.shape[0] - qlen

    def pair(i, carry):
        lanes = pl.ds(pl.multiple_of(i * 128, 128), 128)
        for start, length, keep_ref in ((qlen, plen, pp_ref), (0, qlen, pq_ref)):
            rows = pl.ds(start, length)
            q2, k2, v2 = q_ref[rows, lanes], k_ref[rows, lanes], v_ref[rows, lanes]
            o2, go2 = o_ref[rows, lanes], go_ref[rows, lanes]
            prod = o2.astype(F32) * go2.astype(F32)
            gq, gk, gv = None, None, None
            for side in range(2):
                mine = half_mask(128, side)
                zero = jnp.zeros_like(k2)
                p = keep_ref[2 * i + side]
                gp = dot_nt(go2, jnp.where(mine, v2, zero))
                delta = jnp.sum(jnp.where(mine, prod, 0.0), axis=-1, keepdims=True)
                ds = p.astype(F32) * (gp - delta)
                if start == qlen:
                    if acc_ref is None:
                        ds_ref[2 * i + side] = ds
                    else:
                        ds_ref[2 * i + side] = ds + acc_ref[2 * i + side]
                else:
                    ds_ref[2 * i + side, :length, :length] += ds
                dsl = low(ds)
                a = product(dsl, jnp.where(mine, k2, zero))
                b = dot_tn(dsl, jnp.where(mine, q2, zero))
                c = dot_tn(p, jnp.where(mine, go2, zero))
                gq = a if gq is None else gq + a
                gk = b if gk is None else gk + b
                gv = c if gv is None else gv + c
            gq_ref[rows, lanes] = low(gq)
            gk_ref[rows, lanes] = low(gk)
            gv_ref[rows, lanes] = low(gv)
        return carry

    lax.fori_loop(0, pairs, pair, 0)


def attend_back(q, k, v, o, go, pp, pq, acc):
    heads, plen, _ = pp.shape
    qlen = pq.shape[1]
    operands = [q, k, v, o, go, pp, pq] + ([] if acc is None else [acc])

    def body(*refs):
        ins = list(refs[: len(operands)])
        if acc is None:
            ins.append(None)
        attend_back_kernel(qlen, *ins, *refs[len(operands) :])

    return pl.pallas_call(
        body,
        out_shape=(jax.ShapeDtypeStruct(q.shape, BF),) * 3
        + (jax.ShapeDtypeStruct((heads, plen, plen), F32),),
        in_specs=[whole()] * len(operands),
        out_specs=(whole(),) * 4,
        name="attend_back",
    )(*operands)


def bias_back_kernel(ds_ref, lookup_ref, out_ref, diag_ref):
    heads, plen, _ = ds_ref.shape
    width = lookup_ref.shape[1]
    buckets = out_ref.shape[0]
    for head in range(heads):
        block = ds_ref[head]
        wide_block = jnp.concatenate([block, jnp.zeros_like(block)], axis=1)
        rows = plen
        while rows > 8:
            rows //= 2
            wide_block = wide_block[:rows] + pltpu.roll(wide_block[rows:], width - rows, 1)
        at = lax.broadcasted_iota(jnp.int32, (8, width), 0)
        for bit in (4, 2, 1):
            moved = pltpu.roll(wide_block, width - bit, 1)
            wide_block = jnp.where((at & bit) != 0, moved, wide_block)
        rolled = pltpu.roll(wide_block, plen - 1, 1)
        diag_ref[head : head + 1, :] = jnp.sum(rolled, axis=0, keepdims=True)
    onehot = (
        lax.broadcasted_iota(jnp.int32, (buckets, width), 0)
        == jnp.broadcast_to(lookup_ref[...], (buckets, width))
    ).astype(F32)
    out_ref[...] = dot_nt(onehot, diag_ref[...], HIGHEST)


def bias_back(ds, lookup, buckets):
    heads, plen, _ = ds.shape
    width = 2 * plen
    padded = jnp.pad(lookup, (0, width - lookup.shape[0]), constant_values=-1)[None]
    return pl.pallas_call(
        bias_back_kernel,
        out_shape=jax.ShapeDtypeStruct((buckets, heads), F32),
        in_specs=[whole()] * 2,
        out_specs=whole(),
        scratch_shapes=[pltpu.VMEM((heads, width), F32)],
        name="bias_back",
    )(ds, padded)


def stage_orders(wide, narrow):
    wbits = [1 << i for i in range(wide.bit_length() - 1)]
    nbits = [1 << i for i in range(narrow.bit_length() - 1)]
    w = lambda bits: [("wide", b) for b in bits]
    n = [("narrow", b) for b in nbits]
    tail = w(reversed(wbits[2:]))
    return (w(wbits[:1]) + w(wbits[1:2]) + n + tail, w(wbits[:1]) + n + w(wbits[1:2]) + tail)


def place_of(order, dw, dn):
    place = 0
    for axis, bit in order:
        own = dw if axis == "wide" else dn
        place = place * 2 + (own // bit) % 2
    return place


def traced_place(order, dw, dn):
    place = 0
    for axis, bit in order:
        own = dw if axis == "wide" else dn
        shift = bit.bit_length() - 1
        place = place * 2 + (lax.shift_right_logical(own, shift) & 1)
    return place


def wgrad_kernel(plan, me_ref, *refs):
    wide, narrow, row_axis, depth, pieces, tile_rows, tile_lanes, n_in = plan
    ins = refs[:n_in]
    outs = refs[n_in : n_in + 2 * len(pieces)]
    row_s, lane_s = refs[n_in + 2 * len(pieces) :]
    me_w, me_n = me_ref[0], me_ref[1]
    row_refs, lane_refs = ins[: n_in // 2], ins[n_in // 2 :]
    start = 0
    for r in row_refs:
        row_s[start : start + r.shape[0], :] = r[...]
        start += r.shape[0]
    start = 0
    for r in lane_refs:
        lane_s[start : start + r.shape[0], :] = r[...]
        start += r.shape[0]
    rows, lanes = row_s.shape[1], lane_s.shape[1]
    if row_axis == "wide":
        block_rows, block_lanes = rows // wide, lanes // narrow
    else:
        block_rows, block_lanes = rows // narrow, lanes // wide

    def tile(rt, lt):
        acc = low(
            dot_tn(
                row_s[:, pl.ds(pl.multiple_of(rt * tile_rows, 128), tile_rows)],
                lane_s[:, pl.ds(pl.multiple_of(lt * tile_lanes, 128), tile_lanes)],
            )
        )
        for bi in range(tile_rows // block_rows):
            for bj in range(tile_lanes // block_lanes):
                r_at = rt * (tile_rows // block_rows) + bi
                l_at = lt * (tile_lanes // block_lanes) + bj
                w_at, n_at = (r_at, l_at) if row_axis == "wide" else (l_at, r_at)
                dw, dn = w_at ^ me_w, n_at ^ me_n
                block = acc[
                    bi * block_rows : (bi + 1) * block_rows,
                    bj * block_lanes : (bj + 1) * block_lanes,
                ]
                for k, (order, first, count) in enumerate(pieces):
                    keep_ref, send_ref = outs[2 * k], outs[2 * k + 1]
                    half = keep_ref.shape[0]
                    place = traced_place(order, dw, dn)
                    at = place & (half - 1)
                    part = block[first : first + count, :]

                    @pl.when(place < half)
                    def _():
                        keep_ref[at] = part

                    @pl.when(place >= half)
                    def _():
                        send_ref[at] = part

    rts, lts = rows // tile_rows, lanes // tile_lanes
    if rts * lts == 1:
        tile(0, 0)
    else:

        def step(t, carry):
            tile(t // lts, t % lts)
            return carry

        lax.fori_loop(0, rts * lts, step, 0)


def wgrad(me, row_ops, lane_ops, row_axis, pieces, wide, narrow):
    rows, lanes = row_ops[0].shape[1], lane_ops[0].shape[1]
    if row_axis == "wide":
        block_rows, block_lanes = rows // wide, lanes // narrow
    else:
        block_rows, block_lanes = rows // narrow, lanes // wide
    half = wide * narrow // 2
    if block_lanes % 128 or block_rows % 8:
        total = sum(dot_tn(a, b) for a, b in zip(row_ops, lane_ops))
        blocks = low(total).reshape(rows // block_rows, block_rows, lanes // block_lanes, block_lanes)
        blocks = blocks.transpose((0, 2, 1, 3) if row_axis == "wide" else (2, 0, 1, 3))
        blocks = blocks.reshape(wide * narrow, block_rows, block_lanes)
        outs = []
        for order, first, count in pieces:
            table = [0] * (wide * narrow)
            for dw in range(wide):
                for dn in range(narrow):
                    table[place_of(order, dw, dn)] = (dw, dn)
            dws = jnp.array([t[0] for t in table], jnp.int32)
            dns = jnp.array([t[1] for t in table], jnp.int32)
            at = (dws ^ me[0]) * narrow + (dns ^ me[1])
            moved = jnp.take(blocks[:, first : first + count], at, axis=0)
            outs += [moved[:half], moved[half:]]
        return outs
    depth = sum(a.shape[0] for a in row_ops)
    tile_rows = rows if rows <= 384 else 384
    while rows % tile_rows or tile_rows % block_rows:
        tile_rows += 128
    tile_lanes = block_lanes
    while tile_lanes < 512 and lanes % (2 * tile_lanes) == 0:
        tile_lanes *= 2
    if row_axis == "wide" and rows // wide >= 128:
        tile_rows = 2 * (rows // wide)
    n_in = len(row_ops) + len(lane_ops)
    plan = (wide, narrow, row_axis, depth, pieces, tile_rows, tile_lanes, n_in)
    return pl.pallas_call(
        functools.partial(wgrad_kernel, plan),
        out_shape=tuple(
            jax.ShapeDtypeStruct((half, count, block_lanes), BF) for _, _, count in pieces for _ in range(2)
        ),
        in_specs=[pl.BlockSpec(memory_space=pltpu.SMEM)] + [whole()] * n_in,
        out_specs=(whole(),) * (2 * len(pieces)),
        scratch_shapes=[pltpu.VMEM((depth, rows), BF), pltpu.VMEM((depth, lanes), BF)],
        name="wgrad",
        cost_estimate=pl.CostEstimate(
            flops=2 * depth * rows * lanes, bytes_accessed=4 * rows * lanes, transcendentals=0
        ),
    )(me, *row_ops, *lane_ops)


def swap(a, axis, bit):
    size = lax.axis_size(axis)
    return lax.ppermute(a, axis, [(i, i ^ bit) for i in range(size)])


def reduce_blocks(keep, send, order):
    for k, (axis, bit) in enumerate(order):
        got = swap(send, axis, bit)
        if k == len(order) - 1:
            return keep[0].astype(F32) + got[0].astype(F32)
        half = keep.shape[0] // 2
        send = low(keep[half:].astype(F32) + got[half:].astype(F32))
        keep = low(keep[:half].astype(F32) + got[:half].astype(F32))


def gather_all(rows, order):
    out = rows[None]
    for axis, bit in reversed(order):
        out = jnp.concatenate([out, swap(out, axis, bit)], axis=0)
    return out


def sum_all(a, order):
    for axis, bit in order:
        a = a + swap(a, axis, bit)
    return a


def layer_forward(x, blocks, gains, matrices):
    wq, wk, wv, wo, wg, wu, wd = matrices
    h = low(rms_norm(x, gains[0]))
    q, k, v = low(product(h, wq)), low(product(h, wk)), low(product(h, wv))
    o, pp, pq = attend(q, k, v, *blocks)
    x_mid = x + product(o, wo)
    normed = low(rms_norm(x_mid, gains[1]))
    a = product(normed, wg)
    b = product(normed, wu)
    u = low(gated_unit(a, b))
    return x_mid + product(u, wd), (x, h, q, k, v, pp, pq, o, x_mid, normed, a, b, u)


def layer_backward_ffn(grad_x, stored, gains, matrices):
    wq, wk, wv, wo, wg, wu, wd = matrices
    x, h, q, k, v, pp, pq, o, x_mid, normed, a, b, u = stored
    grad_f = low(grad_x)
    grad_a, grad_b = jax.vjp(gated_unit, a, b)[1](dot_nt(grad_f, wd))
    grad_a, grad_b = low(grad_a), low(grad_b)
    grad_normed = dot_nt(grad_a, wg) + dot_nt(grad_b, wu)
    back_mid, gain_mid = norm_back(x_mid, gains[1], grad_normed)
    return grad_x + back_mid, gain_mid, (grad_f, grad_a, grad_b)


def layer_backward_attention(grad_mid, stored, gains, matrices, acc):
    wq, wk, wv, wo, wg, wu, wd = matrices
    x, h, q, k, v, pp, pq, o, x_mid, normed, a, b, u = stored
    grad_y = low(grad_mid)
    grad_o = low(dot_nt(grad_y, wo))
    grad_q, grad_k, grad_v, acc = attend_back(q, k, v, o, grad_o, pp, pq, acc)
    grad_h = dot_nt(grad_q, wq) + dot_nt(grad_k, wk) + dot_nt(grad_v, wv)
    back_in, gain_in = norm_back(x, gains[0], grad_h)
    return grad_mid + back_in, gain_in, acc, (grad_y, grad_q, grad_k, grad_v)


def local(
    wide,
    narrow,
    query_x,
    query_seg,
    passage_x,
    passage_seg,
    labels,
    lookup,
    softness,
    bias_grid,
    gains,
    wq,
    wk,
    wv,
    wo,
    wg,
    wu,
    wd,
    wp,
):
    qrows, qlen, feat = query_x.shape
    prows, plen, _ = passage_x.shape
    buckets, heads = bias_grid.shape
    matrices = (wq, wk, wv, wo, wg, wu, wd)
    devices = wide * narrow
    order_a, order_b = stage_orders(wide, narrow)
    me_w, me_n = lax.axis_index("wide"), lax.axis_index("narrow")
    me = jnp.stack([me_w, me_n]).astype(jnp.int32)
    tokens = qlen + plen

    blocks = bias_blocks(lookup, bias_grid, query_seg, passage_seg)
    x = jnp.concatenate([query_x.reshape(-1, feat), passage_x.reshape(-1, feat)], axis=0).astype(F32)
    saved = []
    for _ in range(LAYERS):
        x, stored = layer_forward(x, blocks, gains, matrices)
        saved.append(stored)
    z = rms_norm(x, gains[2])
    token = lax.broadcasted_iota(jnp.int32, (PACK, tokens), 1)
    slot = lax.broadcasted_iota(jnp.int32, (PACK, tokens), 0)
    segment = jnp.concatenate([query_seg[0], passage_seg[0] + QSEGS])[None]
    table = (slot == segment).astype(F32)
    sizes = jnp.maximum(jnp.sum(table, axis=1, keepdims=True), 1.0)
    pooled = low(jnp.dot(table, z, precision=HIGHEST) / sizes)
    e = product(pooled, wp)
    vectors = unit_norm(e)
    kinds = lax.broadcasted_iota(jnp.int32, (PACK, 1), 0)
    label_row = jnp.concatenate([labels // 32, labels % 32]).astype(F32)
    label_row = jnp.pad(label_row, (0, feat - 2 * QSEGS))[None]
    packed = low(jnp.where(kinds == PACK - 1, label_row, vectors))
    every = gather_all(packed, order_a)
    every_label = every[:, PACK - 1, : 2 * QSEGS].astype(F32)
    label_of = (every_label[:, :QSEGS] * 32.0 + every_label[:, QSEGS:]).astype(jnp.int32)
    label_of = jnp.pad(label_of, ((0, 0), (0, PACK - QSEGS)), constant_values=-1).reshape(-1, 1)
    flat = every.reshape(devices * PACK, feat)
    size = devices * PACK
    r = jnp.arange(devices, dtype=jnp.int32)
    dw, dn = jnp.zeros_like(r), jnp.zeros_like(r)
    for k, (axis, bit) in enumerate(reversed(order_a)):
        on = ((r >> k) & 1) * bit
        if axis == "wide":
            dw = dw + on
        else:
            dn = dn + on
    device_of = (dw ^ me_w) * narrow + (dn ^ me_n)
    lane_slot = jnp.arange(size, dtype=jnp.int32) % PACK
    is_query = (lane_slot < QSEGS)[:, None]
    is_passage = ((lane_slot >= QSEGS) & (lane_slot < QSEGS + PSEGS))[None, :]
    document = (jnp.repeat(device_of, PACK) * PSEGS + lane_slot - QSEGS)[None, :]
    sharp = softness[0]
    match = dot_nt(flat, flat) / sharp
    match = jnp.where(is_passage, match, MASKED)
    top = jnp.max(match, axis=1, keepdims=True)
    ex = jnp.exp(match - top)
    line = jnp.sum(ex, axis=1, keepdims=True)
    hit = (label_of == document) & is_passage & is_query
    loss_rows = top[:PACK] + jnp.log(line[:PACK]) - jnp.sum(
        jnp.where(hit[:PACK], match[:PACK], 0.0), axis=1, keepdims=True
    )
    loss_part = jnp.sum(jnp.where(is_query[:PACK], loss_rows, 0.0))
    g_sim = low(jnp.where(is_query & is_passage, (ex / line - hit.astype(F32)) / sharp, 0.0))
    g_vectors = product(g_sim[:PACK], flat) + dot_tn(g_sim[:, :PACK], flat)
    grad_e = low(jax.vjp(unit_norm, e)[1](g_vectors)[0])
    grad_pooled = dot_nt(grad_e, wp) / sizes
    grad_z = dot_tn(table, grad_pooled, HIGHEST)
    grad_x, gain_final = norm_back(x, gains[2], grad_z)

    args = (wide, narrow)
    block = feat // wide
    ff_rows = feat // narrow
    proj = wgrad(me, [grad_e], [pooled], "wide", [(order_a, 0, block)], *args)

    first, second = saved
    grad_mid, gain_mid, ffn_2 = layer_backward_ffn(grad_x, second, gains, matrices)
    grad_x, gain_in, acc, att_2 = layer_backward_attention(grad_mid, second, gains, matrices, None)
    grad_mid, more, ffn_1 = layer_backward_ffn(grad_x, first, gains, matrices)
    gain_mid = gain_mid + more
    u_1, u_2 = first[-1], second[-1]
    normed_1, normed_2 = first[9], second[9]
    half = ff_rows // 2
    down = wgrad(me, [ffn_1[0], ffn_2[0]], [u_1, u_2], "wide", [(order_a, 0, block)], *args)
    gate = wgrad(
        me, [normed_1, normed_2], [ffn_1[1], ffn_2[1]], "narrow", [(order_b, 0, ff_rows)], *args
    )
    up = wgrad(
        me,
        [normed_1, normed_2],
        [ffn_1[2], ffn_2[2]],
        "narrow",
        [(order_a, 0, half), (order_b, half, ff_rows - half)],
        *args,
    )
    grad_x, more, acc, att_1 = layer_backward_attention(grad_mid, first, gains, matrices, acc)
    gain_in = gain_in + more
    out = wgrad(
        me, [att_1[0], att_2[0]], [first[7], second[7]], "wide", [(order_a, 0, block)], *args
    )
    hs = [first[1], second[1]]
    query = wgrad(me, [att_1[1], att_2[1]], hs, "wide", [(order_a, 0, block)], *args)
    key = wgrad(me, [att_1[2], att_2[2]], hs, "wide", [(order_b, 0, block)], *args)
    value = wgrad(me, [att_1[3], att_2[3]], hs, "wide", [(order_b, 0, block)], *args)

    grad_proj = reduce_blocks(*proj, order_a).T
    grad_down = reduce_blocks(*down, order_a).T
    grad_gate = reduce_blocks(*gate, order_b)
    grad_up = jnp.concatenate(
        [reduce_blocks(*up[:2], order_a), reduce_blocks(*up[2:], order_b)], axis=0
    )
    grad_out = reduce_blocks(*out, order_a).T
    grad_query = reduce_blocks(*query, order_a).T
    grad_key = reduce_blocks(*key, order_b).T
    grad_value = reduce_blocks(*value, order_b).T

    bucket_grad = bias_back(acc, lookup, buckets)
    small = jnp.concatenate(
        [
            gain_in.reshape(-1),
            gain_mid.reshape(-1),
            gain_final.reshape(-1),
            bucket_grad.reshape(-1),
            loss_part.reshape(1),
        ]
    )
    count = small.shape[0]
    small = jnp.pad(small, (0, -count % 1024)).reshape(-1, 128)
    small = sum_all(small, order_a).reshape(-1)
    gain_total = small[: 3 * feat].reshape(3, feat)
    bucket_total = small[3 * feat : count - 1].reshape(buckets, heads)
    mean_loss = small[count - 1 : count] / (qrows * QSEGS * devices)
    return (
        mean_loss,
        vectors[:QSEGS],
        vectors[QSEGS : QSEGS + PSEGS],
        grad_x[:qlen].reshape(1, qlen, feat),
        grad_x[qlen:].reshape(1, plen, feat),
        gain_total,
        bucket_total,
        grad_query,
        grad_key,
        grad_value,
        grad_out,
        grad_gate,
        grad_up,
        grad_down,
        grad_proj,
    )


def solution(mesh):
    rows3, rows2, rows1 = P(AXES, None, None), P(AXES, None), P(AXES)
    return jax.shard_map(
        functools.partial(local, mesh.shape["wide"], mesh.shape["narrow"]),
        mesh=mesh,
        in_specs=(rows3, rows2, rows3, rows2, rows1) + (P(),) * 12,
        out_specs=(P(), rows2, rows2, rows3, rows3, P(), P()) + (P("narrow", "wide"),) * 8,
        check_vma=False,
    )
```

```python
import functools

import jax
import jax.numpy as jnp
from jax import lax
from jax.experimental import pallas as pl
from jax.experimental.pallas import tpu as pltpu
from jax.sharding import PartitionSpec as P

LAYERS = 2
QSEGS = 3
PSEGS = 4
HDIM = 64
PACK = 8

HIGHEST = lax.Precision.HIGHEST
EPSILON = 1e-06
MASKED = -1000000000.0
BF = jnp.bfloat16
F32 = jnp.float32
AXES = ("wide", "narrow")


def low(a):
    return a.astype(BF)


def product(a, b):
    return jnp.dot(a, b, preferred_element_type=F32)


def dot_tn(a, b, precision=None):
    return lax.dot_general(
        a, b, (((0,), (0,)), ((), ())), preferred_element_type=F32, precision=precision
    )


def dot_nt(a, b, precision=None):
    return lax.dot_general(
        a, b, (((1,), (1,)), ((), ())), preferred_element_type=F32, precision=precision
    )


def rms_norm(x, gain_vec):
    return x * lax.rsqrt(jnp.mean(x * x, axis=-1, keepdims=True) + EPSILON) * gain_vec


def norm_back(x, gain_vec, grad_in):
    outcome, pullback = jax.vjp(rms_norm, x, gain_vec)
    return pullback(grad_in)


def gated_unit(a, b):
    return jax.nn.gelu(a, approximate=True) * b


def whole():
    return pl.BlockSpec(memory_space=pltpu.VMEM)


def bias_kernel(qlen, plen, lookup_ref, grid_ref, qseg_ref, pseg_ref, pbias_ref, qbias_ref, wide_s, short_s):
    buckets, heads = grid_ref.shape
    width = 2 * plen
    wide_s[...] = jnp.full((1, width), -1, jnp.int32)
    wide_s[:, : lookup_ref.shape[1]] = lookup_ref[...]
    onehot = (
        lax.broadcasted_iota(jnp.int32, (buckets, width), 0)
        == jnp.broadcast_to(wide_s[...], (buckets, width))
    ).astype(F32)
    table = dot_tn(grid_ref[...], onehot, HIGHEST)
    pcol = jnp.transpose(jnp.broadcast_to(pseg_ref[...], (plen, plen)))
    psame = pcol == jnp.broadcast_to(pseg_ref[...], (plen, plen))
    short_s[...] = jnp.full((1, 128), -1, jnp.int32)
    short_s[:, :qlen] = qseg_ref[...]
    qcol = jnp.transpose(jnp.broadcast_to(short_s[...], (128, 128)))
    qsame = (qcol == jnp.broadcast_to(short_s[...], (128, 128)))[:qlen, :qlen]
    for head in range(heads):
        rows = jnp.broadcast_to(table[head : head + 1, :], (plen, width))
        rolled = pltpu.roll(rows, width - (plen - 1), 1, stride=1, stride_axis=0)
        block = rolled[:, :plen]
        pbias_ref[head] = jnp.where(psame, block, MASKED)
        qbias_ref[head] = jnp.where(qsame, block[:qlen, :qlen], MASKED)


def bias_blocks(lookup, grid, qseg, pseg):
    heads = grid.shape[1]
    qlen, plen = qseg.shape[1], pseg.shape[1]
    return pl.pallas_call(
        functools.partial(bias_kernel, qlen, plen),
        out_shape=(
            jax.ShapeDtypeStruct((heads, plen, plen), F32),
            jax.ShapeDtypeStruct((heads, qlen, qlen), F32),
        ),
        in_specs=[whole()] * 4,
        out_specs=(whole(), whole()),
        scratch_shapes=[pltpu.VMEM((1, 2 * plen), jnp.int32), pltpu.VMEM((1, 128), jnp.int32)],
        name="bias_blocks",
        compiler_params=pltpu.CompilerParams(vmem_limit_bytes=8 << 20),
        cost_estimate=pl.CostEstimate(
            flops=2 * heads * plen * plen, bytes_accessed=8 * heads * plen * plen, transcendentals=0
        ),
    )(lookup[None], grid, qseg, pseg)


def half_mask(lanes, side):
    return (lax.broadcasted_iota(jnp.int32, (1, lanes), 1) // HDIM) == side


def attend_kernel(qlen, q_ref, k_ref, v_ref, pbias_ref, qbias_ref, o_ref, pp_ref, pq_ref):
    pairs = q_ref.shape[1] // 128
    spans = ((0, qlen, qbias_ref, pq_ref), (qlen, q_ref.shape[0] - qlen, pbias_ref, pp_ref))

    def pair(i, carry):
        lanes = pl.ds(pl.multiple_of(i * 128, 128), 128)
        for start, length, bias_ref, keep_ref in spans:
            rows = pl.ds(start, length)
            q2, k2, v2 = q_ref[rows, lanes], k_ref[rows, lanes], v_ref[rows, lanes]
            total = None
            for side in range(2):
                mine = half_mask(128, side)
                zero = jnp.zeros_like(k2)
                s = dot_nt(q2, jnp.where(mine, k2, zero)) + bias_ref[2 * i + side]
                top = jnp.max(s, axis=-1, keepdims=True)
                e = jnp.exp(s - top)
                p = low(e * (1.0 / jnp.sum(e, axis=-1, keepdims=True)))
                keep_ref[2 * i + side] = p
                part = product(p, jnp.where(mine, v2, zero))
                total = part if total is None else total + part
            o_ref[rows, lanes] = low(total)
        return carry

    lax.fori_loop(0, pairs, pair, 0)


def attend(q, k, v, pbias, qbias):
    heads, plen, _ = pbias.shape
    qlen = qbias.shape[1]
    return pl.pallas_call(
        functools.partial(attend_kernel, qlen),
        out_shape=(
            jax.ShapeDtypeStruct(q.shape, BF),
            jax.ShapeDtypeStruct((heads, plen, plen), BF),
            jax.ShapeDtypeStruct((heads, qlen, qlen), BF),
        ),
        in_specs=[whole()] * 5,
        out_specs=(whole(),) * 3,
        name="attend",
        compiler_params=pltpu.CompilerParams(vmem_limit_bytes=16 << 20),
        cost_estimate=pl.CostEstimate(
            flops=4 * heads * HDIM * plen * plen, bytes_accessed=12 * heads * plen * plen, transcendentals=heads * plen * plen
        ),
    )(q, k, v, pbias, qbias)


def attend_back_kernel(
    qlen, q_ref, k_ref, v_ref, o_ref, go_ref, pp_ref, pq_ref, acc_ref, gq_ref, gk_ref, gv_ref, ds_ref
):
    pairs = q_ref.shape[1] // 128
    plen = q_ref.shape[0] - qlen

    def pair(i, carry):
        lanes = pl.ds(pl.multiple_of(i * 128, 128), 128)
        for start, length, keep_ref in ((qlen, plen, pp_ref), (0, qlen, pq_ref)):
            rows = pl.ds(start, length)
            q2, k2, v2 = q_ref[rows, lanes], k_ref[rows, lanes], v_ref[rows, lanes]
            o2, go2 = o_ref[rows, lanes], go_ref[rows, lanes]
            prod = o2.astype(F32) * go2.astype(F32)
            gq, gk, gv = None, None, None
            for side in range(2):
                mine = half_mask(128, side)
                zero = jnp.zeros_like(k2)
                p = keep_ref[2 * i + side]
                gp = dot_nt(go2, jnp.where(mine, v2, zero))
                delta = jnp.sum(jnp.where(mine, prod, 0.0), axis=-1, keepdims=True)
                ds = p.astype(F32) * (gp - delta)
                if start == qlen:
                    if acc_ref is None:
                        ds_ref[2 * i + side] = ds
                    else:
                        ds_ref[2 * i + side] = ds + acc_ref[2 * i + side]
                else:
                    ds_ref[2 * i + side, :length, :length] += ds
                dsl = low(ds)
                a = product(dsl, jnp.where(mine, k2, zero))
                b = dot_tn(dsl, jnp.where(mine, q2, zero))
                c = dot_tn(p, jnp.where(mine, go2, zero))
                gq = a if gq is None else gq + a
                gk = b if gk is None else gk + b
                gv = c if gv is None else gv + c
            gq_ref[rows, lanes] = low(gq)
            gk_ref[rows, lanes] = low(gk)
            gv_ref[rows, lanes] = low(gv)
        return carry

    lax.fori_loop(0, pairs, pair, 0)


def attend_back(q, k, v, o, go, pp, pq, acc):
    heads, plen, _ = pp.shape
    qlen = pq.shape[1]
    operands = [q, k, v, o, go, pp, pq] + ([] if acc is None else [acc])

    def body(*refs):
        ins = list(refs[: len(operands)])
        if acc is None:
            ins.append(None)
        attend_back_kernel(qlen, *ins, *refs[len(operands) :])

    return pl.pallas_call(
        body,
        out_shape=(jax.ShapeDtypeStruct(q.shape, BF),) * 3
        + (jax.ShapeDtypeStruct((heads, plen, plen), F32),),
        in_specs=[whole()] * len(operands),
        out_specs=(whole(),) * 4,
        name="attend_back",
        compiler_params=pltpu.CompilerParams(vmem_limit_bytes=20 << 20),
        cost_estimate=pl.CostEstimate(
            flops=8 * heads * HDIM * plen * plen, bytes_accessed=12 * heads * plen * plen, transcendentals=0
        ),
    )(*operands)


def small_kernel(
    buckets, ds_ref, lookup_ref, in_ref, mid_ref, final_ref, loss_ref, out_ref, diag_ref, wide_s
):
    heads, plen, _ = ds_ref.shape
    out_ref[...] = jnp.zeros_like(out_ref)
    out_ref[0:1, :] = in_ref[...]
    out_ref[1:2, :] = mid_ref[...]
    out_ref[2:3, :] = final_ref[...]
    out_ref[3:4, :128] = loss_ref[...]
    width = 2 * plen
    wide_s[...] = jnp.full((1, width), -1, jnp.int32)
    wide_s[:, : lookup_ref.shape[1]] = lookup_ref[...]
    for head in range(heads):
        block = ds_ref[head]
        wide_block = jnp.concatenate([block, jnp.zeros_like(block)], axis=1)
        rows = plen
        while rows > 8:
            rows //= 2
            wide_block = wide_block[:rows] + pltpu.roll(wide_block[rows:], width - rows, 1)
        at = lax.broadcasted_iota(jnp.int32, (8, width), 0)
        for bit in (4, 2, 1):
            moved = pltpu.roll(wide_block, width - bit, 1)
            wide_block = jnp.where((at & bit) != 0, moved, wide_block)
        rolled = pltpu.roll(wide_block, plen - 1, 1)
        diag_ref[head : head + 1, :] = jnp.sum(rolled, axis=0, keepdims=True)
    onehot = (
        lax.broadcasted_iota(jnp.int32, (buckets, width), 0)
        == jnp.broadcast_to(wide_s[...], (buckets, width))
    ).astype(F32)
    out_ref[4 : 4 + heads, :buckets] = dot_nt(diag_ref[...], onehot, HIGHEST)


def small_sums(ds, lookup, buckets, gain_in, gain_mid, gain_final, loss):
    heads, plen, _ = ds.shape
    width = 2 * plen
    return pl.pallas_call(
        functools.partial(small_kernel, buckets),
        out_shape=jax.ShapeDtypeStruct((4 + heads, gain_in.shape[1]), F32),
        in_specs=[whole()] * 6,
        out_specs=whole(),
        scratch_shapes=[pltpu.VMEM((heads, width), F32), pltpu.VMEM((1, width), jnp.int32)],
        name="small_sums",
        compiler_params=pltpu.CompilerParams(vmem_limit_bytes=8 << 20),
    )(ds, lookup[None], gain_in, gain_mid, gain_final, loss)


def segment_table(seg_ref, first):
    rows, length = PACK, seg_ref.shape[1]
    slot = lax.broadcasted_iota(jnp.int32, (rows, length), 0)
    return (slot == jnp.broadcast_to(seg_ref[...], (rows, length)) + first).astype(F32)


def pool_kernel(
    x_ref, gain_ref, qseg_ref, pseg_ref, label_ref, wp_ref, packed_ref, vec_ref, e_ref, pooled_ref
):
    qlen = qseg_ref.shape[1]
    x = x_ref[...]
    z = x * lax.rsqrt(jnp.mean(x * x, axis=-1, keepdims=True) + EPSILON) * gain_ref[...]
    qt, pt = segment_table(qseg_ref, 0), segment_table(pseg_ref, QSEGS)
    sizes = jnp.sum(qt, axis=1, keepdims=True) + jnp.sum(pt, axis=1, keepdims=True)
    sums = jnp.dot(qt, z[:qlen], precision=HIGHEST, preferred_element_type=F32) + jnp.dot(
        pt, z[qlen:], precision=HIGHEST, preferred_element_type=F32
    )
    pooled = low(sums / jnp.maximum(sizes, 1.0))
    pooled_ref[...] = pooled
    e = product(pooled, wp_ref[...])
    e_ref[...] = e
    vec = e * lax.rsqrt(jnp.sum(e * e, axis=-1, keepdims=True) + EPSILON)
    vec_ref[...] = vec
    at = lax.broadcasted_iota(jnp.int32, vec.shape, 1)
    row = lax.broadcasted_iota(jnp.int32, vec.shape, 0)
    code = jnp.zeros(vec.shape, F32)
    for i in range(QSEGS):
        label = label_ref[i]
        high = lax.shift_right_logical(label, 5).astype(F32)
        rest = (label & 31).astype(F32)
        code = jnp.where(at == i, high, jnp.where(at == QSEGS + i, rest, code))
    packed_ref[...] = low(jnp.where(row == PACK - 1, code, vec))


def pool(x, gain, qseg, pseg, labels, wp):
    feat = x.shape[1]
    shape = (PACK, feat)
    return pl.pallas_call(
        pool_kernel,
        out_shape=(
            jax.ShapeDtypeStruct(shape, BF),
            jax.ShapeDtypeStruct(shape, F32),
            jax.ShapeDtypeStruct(shape, F32),
            jax.ShapeDtypeStruct(shape, BF),
        ),
        in_specs=[whole()] * 4 + [pl.BlockSpec(memory_space=pltpu.SMEM), whole()],
        out_specs=(whole(),) * 4,
        name="pool",
        compiler_params=pltpu.CompilerParams(vmem_limit_bytes=12 << 20),
    )(x, gain, qseg, pseg, labels, wp)


def loss_kernel(
    narrow, stages, me_ref, sharp_ref, here_ref, there_ref, vec_ref, e_ref, x_ref, gain_ref,
    qseg_ref, pseg_ref, wp_ref, gx_ref, ggain_ref, loss_ref, ge_ref, flat_s,
):
    half = here_ref.shape[0]
    flat_s[:half, :] = here_ref[...]
    flat_s[half:, :] = there_ref[...]
    size = 2 * half
    tile = min(size, 256)
    sharp = sharp_ref[0]
    lane = lax.broadcasted_iota(jnp.int32, (1, size), 1)
    block, slot = lax.shift_right_logical(lane, 3), lane & (PACK - 1)
    dw, dn = jnp.zeros_like(block), jnp.zeros_like(block)
    for k, (axis, bit) in enumerate(stages):
        on = (lax.shift_right_logical(block, k) & 1) * bit
        dw, dn = (dw + on, dn) if axis == "wide" else (dw, dn + on)
    device = (dw ^ me_ref[0]) * narrow + (dn ^ me_ref[1])
    is_passage = (slot >= QSEGS) & (slot < QSEGS + PSEGS)
    document = jnp.where(is_passage, device * PSEGS + slot - QSEGS, -2)
    row = lax.broadcasted_iota(jnp.int32, (tile, 1), 0)
    row_slot = row & (PACK - 1)
    is_query = row_slot < QSEGS
    across = lax.broadcasted_iota(jnp.int32, (tile, tile), 1)
    source = low((across == row - row_slot + PACK - 1).astype(F32))
    place = lax.broadcasted_iota(jnp.int32, (tile, 128), 1)
    weigh = jnp.where(place == row_slot, 32.0, 0.0) + jnp.where(place == row_slot + QSEGS, 1.0, 0.0)
    mine = lax.broadcasted_iota(jnp.int32, (1, 128), 1) < PACK
    grad = None
    for t in range(size // tile):
        rows = flat_s[t * tile : (t + 1) * tile, :]
        match = dot_nt(rows, flat_s[...]) / sharp
        match = jnp.where(is_passage, match, MASKED)
        label = jnp.sum(product(source, rows[:, :128]) * weigh, axis=1, keepdims=True)
        hit = (label.astype(jnp.int32) == document) & is_query
        top = jnp.max(match, axis=1, keepdims=True)
        ex = jnp.exp(match - top)
        line = jnp.sum(ex, axis=1, keepdims=True)
        g = (ex / line - hit.astype(F32)) / sharp
        g = low(jnp.where(is_query & is_passage, g, 0.0))
        back = dot_tn(jnp.where(mine, g[:, :128], jnp.zeros_like(g[:, :128])), rows)[:PACK]
        if t == 0:
            part = jnp.sum(jnp.where(hit, match, 0.0), axis=1, keepdims=True)
            part = jnp.where(is_query & (row < PACK), top + jnp.log(line) - part, 0.0)
            loss_ref[...] = jnp.broadcast_to(jnp.sum(part, axis=0, keepdims=True), loss_ref.shape)
            grad = product(g[:16], flat_s[...])[:PACK]
        grad = grad + back
    e, vec = e_ref[...], vec_ref[...]
    scale = lax.rsqrt(jnp.sum(e * e, axis=-1, keepdims=True) + EPSILON)
    ge = low((grad - vec * jnp.sum(vec * grad, axis=-1, keepdims=True)) * scale)
    ge_ref[...] = ge
    qt, pt = segment_table(qseg_ref, 0), segment_table(pseg_ref, QSEGS)
    sizes = jnp.sum(qt, axis=1, keepdims=True) + jnp.sum(pt, axis=1, keepdims=True)
    pooled = dot_nt(ge, wp_ref[...]) / jnp.maximum(sizes, 1.0)
    qlen = qseg_ref.shape[1]
    gain = gain_ref[...]
    total = None
    for table, start, count in ((qt, 0, qlen), (pt, qlen, pseg_ref.shape[1])):
        gz = dot_tn(table, pooled, HIGHEST)
        x = x_ref[start : start + count, :]
        r = lax.rsqrt(jnp.mean(x * x, axis=-1, keepdims=True) + EPSILON)
        unit = x * r
        scaled = gz * gain
        gx_ref[start : start + count, :] = r * (
            scaled - unit * jnp.mean(unit * scaled, axis=-1, keepdims=True)
        )
        part = jnp.sum(gz * unit, axis=0, keepdims=True)
        total = part if total is None else total + part
    ggain_ref[...] = total


def loss_back(me, narrow, stages, sharp, here, there, vec, e, x, gain, qseg, pseg, wp):
    feat = x.shape[1]
    size = 2 * here.shape[0]
    smem = pl.BlockSpec(memory_space=pltpu.SMEM)
    return pl.pallas_call(
        functools.partial(loss_kernel, narrow, stages),
        out_shape=(
            jax.ShapeDtypeStruct(x.shape, F32),
            jax.ShapeDtypeStruct((1, feat), F32),
            jax.ShapeDtypeStruct((1, 128), F32),
            jax.ShapeDtypeStruct((PACK, feat), BF),
        ),
        in_specs=[smem, smem] + [whole()] * 9,
        out_specs=(whole(),) * 4,
        scratch_shapes=[pltpu.VMEM((size, feat), BF)],
        name="loss_back",
        compiler_params=pltpu.CompilerParams(vmem_limit_bytes=(12 if size <= 512 else 40) << 20),
    )(me, sharp, here, there, vec, e, x, gain, qseg, pseg, wp)


def join_kernel(a_ref, b_ref, out_ref):
    rows = a_ref.shape[0]
    out_ref[:rows, :] = a_ref[...]
    out_ref[rows:, :] = b_ref[...]


def join(a, b):
    return pl.pallas_call(
        join_kernel,
        out_shape=jax.ShapeDtypeStruct((2 * a.shape[0], a.shape[1]), a.dtype),
        in_specs=[whole()] * 2,
        out_specs=whole(),
        name="join",
        compiler_params=pltpu.CompilerParams(vmem_limit_bytes=4 << 20),
    )(a, b)


def stage_orders(wide, narrow):
    wbits = [1 << i for i in range(wide.bit_length() - 1)]
    nbits = [1 << i for i in range(narrow.bit_length() - 1)]
    w = lambda bits: [("wide", b) for b in bits]
    n = [("narrow", b) for b in nbits]
    tail = w(wbits[2:])
    return (w(wbits[:1]) + w(wbits[1:2]) + n + tail, w(wbits[:1]) + n + w(wbits[1:2]) + tail)


def place_of(order, dw, dn):
    place = 0
    for axis, bit in order:
        own = dw if axis == "wide" else dn
        place = place * 2 + (own // bit) % 2
    return place


def traced_place(order, dw, dn):
    place = 0
    for axis, bit in order:
        own = dw if axis == "wide" else dn
        place = place * 2 + (lax.shift_right_logical(own, bit.bit_length() - 1) & 1)
    return place


def wgrad_kernel(jobs, groups, n_ops, me_ref, *refs):
    ops, (keep_ref, send_ref) = refs[:n_ops], refs[n_ops : n_ops + 2]
    held = refs[n_ops + 2 : n_ops + 2 + len(groups)]
    turned_s, sems = refs[-2:]
    me_w, me_n = me_ref[0], me_ref[1]
    half = keep_ref.shape[0]
    copies = []
    for ids, buf in zip(groups, held):
        first, own = 0, []
        for i in ids:
            count = ops[i].shape[0]
            sem = sems.at[sum(len(c) for c in copies) + len(own)]
            own.append(pltpu.make_async_copy(ops[i], buf.at[first : first + count], sem))
            first += count
        copies.append(own)
    for own in copies:
        for c in own:
            c.start()
    ready = set()

    def arrive(g):
        if g not in ready:
            for c in copies[g]:
                c.wait()
            ready.add(g)

    def store(acc, job, w_first, n_first):
        row_axis, block_rows, block_lanes, targets = job[2:]
        blocks = [
            (bi, bj)
            for bi in range(acc.shape[0] // block_rows)
            for bj in range(acc.shape[1] // block_lanes)
        ]
        bases = [traced_place(t[0], w_first ^ me_w, n_first ^ me_n) for t in targets]
        for core in range(2):

            @pl.when((me_w & 1) == core)
            def _():
                for bi, bj in blocks:
                    w, n = (bi, bj) if row_axis == "wide" else (bj, bi)
                    out_ref = keep_ref if (w & 1) == core else send_ref
                    for (order, first, count, offset), base in zip(targets, bases):
                        at = (base ^ place_of(order, w, n)) & (half - 1)
                        for k in range(block_lanes // 128):
                            lane = bj * block_lanes + k * 128
                            row = bi * block_rows + first
                            out_ref[at, offset + k * count : offset + (k + 1) * count, :] = acc[
                                row : row + count, lane : lane + 128
                            ]

    for job in jobs:
        rg, lg, row_axis, block_rows, block_lanes, targets = job
        arrive(rg)
        arrive(lg)
        row_s, lane_s = held[rg], held[lg]
        depth, rows, lanes = row_s.shape[0], row_s.shape[1], lane_s.shape[1]
        tile_rows = 384
        tile_lanes = block_lanes
        while tile_lanes < 512 and lanes % (2 * tile_lanes) == 0:
            tile_lanes *= 2
        per_row, per_lane = tile_rows // block_rows, tile_lanes // block_lanes

        def row_step(rt, carry):
            mine = row_s[:, pl.ds(pl.multiple_of(rt * tile_rows, 128), tile_rows)]
            if depth > 16:
                turned_s[...] = mine.T

            def lane_step(lt, inner):
                part = lane_s[:, pl.ds(pl.multiple_of(lt * tile_lanes, 128), tile_lanes)]
                acc = product(turned_s[...], part) if depth > 16 else dot_tn(mine, part)
                if row_axis == "wide":
                    store(low(acc), job, rt * per_row, lt * per_lane)
                else:
                    store(low(acc), job, lt * per_lane, rt * per_row)
                return inner

            if lanes == tile_lanes:
                return lane_step(0, carry)
            return lax.fori_loop(0, lanes // tile_lanes, lane_step, carry)

        lax.fori_loop(0, rows // tile_rows, row_step, 0)


def wgrad(me, ops, groups, jobs, total_rows, wide, narrow, vmem):
    half = wide * narrow // 2
    width = lambda g: ops[groups[g][0]].shape[1]
    depth = [sum(ops[i].shape[0] for i in g) for g in groups]
    full = []
    for rg, lg, row_axis, targets in jobs:
        split = (wide, narrow) if row_axis == "wide" else (narrow, wide)
        full.append((rg, lg, row_axis, width(rg) // split[0], width(lg) // split[1], targets))
    flops = sum(2 * depth[j[0]] * width(j[0]) * width(j[1]) for j in full)
    return pl.pallas_call(
        functools.partial(wgrad_kernel, full, groups, len(ops)),
        out_shape=(jax.ShapeDtypeStruct((half, total_rows, 128), BF),) * 2,
        in_specs=[pl.BlockSpec(memory_space=pltpu.SMEM)]
        + [pl.BlockSpec(memory_space=pl.ANY)] * len(ops),
        out_specs=(whole(),) * 2,
        scratch_shapes=[pltpu.VMEM((d, width(g)), BF) for g, d in enumerate(depth)]
        + [pltpu.VMEM((384, max(depth)), BF), pltpu.SemaphoreType.DMA((sum(map(len, groups)),))],
        name="wgrad",
        compiler_params=pltpu.CompilerParams(vmem_limit_bytes=vmem << 20),
        cost_estimate=pl.CostEstimate(flops=flops, bytes_accessed=flops // 256, transcendentals=0),
    )(me, *ops)


def swap(a, axis, bit):
    size = lax.axis_size(axis)
    return lax.ppermute(a, axis, [(i, i ^ bit) for i in range(size)])


class Chunk:
    def __init__(self, keep, send, split, orders, finals):
        self.rows, self.split, self.orders, self.finals = keep.shape[1], split, orders, finals
        self.stage, self.parts = 0, [(keep, send)]
        self.done = False

    def spans(self, stage):
        if self.orders[0][stage] == self.orders[1][stage] and (
            stage == 0 or self.orders[0][stage:] == self.orders[1][stage:]
        ):
            return [(0, self.rows, self.orders[0])]
        return [(0, self.split, self.orders[0]), (self.split, self.rows, self.orders[1])]

    def start(self):
        return [
            swap(send, *order[self.stage])
            for (keep, send), (_, _, order) in zip(self.parts, self.spans(self.stage))
        ]


class Total:
    def __init__(self, value, order):
        self.value, self.order, self.stage = value, order, 0
        self.done = False

    def start(self):
        return [swap(self.value, *self.order[self.stage])]


def advance(flows, gots):
    operands, shapes, steps = [], [], []
    for f, got in zip(flows, gots):
        if isinstance(f, Total):
            steps.append(("sum", len(operands), len(shapes)))
            operands += [f.value, got[0]]
            shapes.append(jax.ShapeDtypeStruct(f.value.shape, F32))
            continue
        now = f.spans(f.stage)
        last = f.stage == len(f.orders[0]) - 1
        first_in, first_out = len(operands), len(shapes)
        for (keep, _), g in zip(f.parts, got):
            operands += [keep, g]
        half = f.parts[0][0].shape[0] // 2
        if last:
            for kind, offset, rows, lanes in f.finals:
                shapes.append(jax.ShapeDtypeStruct((rows, lanes), F32))
            steps.append(("final", first_in, first_out, f.finals))
        else:
            later = f.spans(f.stage + 1)
            for lo, hi, _ in later:
                shapes += [jax.ShapeDtypeStruct((half, hi - lo, 128), BF)] * 2
            steps.append(("halve", first_in, first_out, [n[:2] for n in now], [n[:2] for n in later]))

    def body(*refs):
        ins, outs = refs[: len(operands)], refs[len(operands) :]
        for step in steps:
            kind, i, o = step[:3]
            if kind == "sum":
                outs[o][...] = ins[i][...] + ins[i + 1][...]
            elif kind == "final":
                for n, (_, offset, rows, lanes) in enumerate(step[3]):
                    for k in range(lanes // 128):
                        span = pl.ds(offset + k * rows, rows)
                        value = ins[i][0, span, :].astype(F32) + ins[i + 1][0, span, :].astype(F32)
                        outs[o + n][:, k * 128 : (k + 1) * 128] = value
            else:
                for p, (lo, hi) in enumerate(step[3]):
                    for q, (lo2, hi2) in enumerate(step[4]):
                        a, b = max(lo, lo2), min(hi, hi2)
                        if a >= b:
                            continue
                        keep_ref, got_ref = ins[i + 2 * p], ins[i + 2 * p + 1]
                        half = keep_ref.shape[0] // 2
                        for side in range(2):
                            out_ref = outs[o + 2 * q + side]

                            def block(n, carry):
                                src = pl.ds(a - lo, b - a)
                                value = keep_ref[side * half + n, src, :].astype(F32)
                                value = value + got_ref[side * half + n, src, :].astype(F32)
                                out_ref[n, a - lo2 : b - lo2, :] = low(value)
                                return carry

                            if half == 1:
                                block(0, 0)
                            else:
                                lax.fori_loop(0, half, block, 0)

    outs = pl.pallas_call(
        body,
        out_shape=tuple(shapes),
        in_specs=[whole()] * len(operands),
        out_specs=(whole(),) * len(shapes),
        name="advance",
        compiler_params=pltpu.CompilerParams(vmem_limit_bytes=16 << 20),
    )(*operands)
    at = 0
    for f, step in zip(flows, steps):
        f.stage += 1
        if step[0] == "sum":
            f.value = outs[at]
            at += 1
            f.done = f.stage == len(f.order)
        elif step[0] == "final":
            f.result = [
                out.T if final[0] == "turn" else out
                for out, final in zip(outs[at : at + len(step[3])], step[3])
            ]
            at += len(step[3])
            f.done = True
        else:
            f.parts = [(outs[at + 2 * q], outs[at + 2 * q + 1]) for q in range(len(step[4]))]
            at += 2 * len(step[4])


def exchange(flows, compute, inputs):
    live = [f for f in flows if not f.done]
    sent = [f.value if isinstance(f, Total) else f.parts for f in live]
    sent, inputs = lax.optimization_barrier((sent, inputs))
    for f, value in zip(live, sent):
        if isinstance(f, Total):
            f.value = value
        else:
            f.parts = value
    got = [f.start() for f in live]
    got, made = lax.optimization_barrier((got, compute(*inputs)))
    advance(live, got)
    return made


def gather_all(rows, stages):
    for k, (axis, bit) in enumerate(stages):
        got = swap(rows, axis, bit)
        if k == len(stages) - 1:
            return rows, got
        rows = join(rows, got)


def layer_forward(x, blocks, gains, matrices):
    wq, wk, wv, wo, wg, wu, wd = matrices
    h = low(rms_norm(x, gains[0]))
    q, k, v = low(product(h, wq)), low(product(h, wk)), low(product(h, wv))
    o, pp, pq = attend(q, k, v, *blocks)
    x_mid = x + product(o, wo)
    normed = low(rms_norm(x_mid, gains[1]))
    a = product(normed, wg)
    b = product(normed, wu)
    u = low(gated_unit(a, b))
    return x_mid + product(u, wd), (x, h, q, k, v, pp, pq, o, x_mid, normed, a, b, u)


def layer_backward_ffn(grad_x, stored, gains, matrices):
    wq, wk, wv, wo, wg, wu, wd = matrices
    x, h, q, k, v, pp, pq, o, x_mid, normed, a, b, u = stored
    grad_f = low(grad_x)
    grad_a, grad_b = jax.vjp(gated_unit, a, b)[1](dot_nt(grad_f, wd))
    grad_a, grad_b = low(grad_a), low(grad_b)
    grad_normed = dot_nt(grad_a, wg) + dot_nt(grad_b, wu)
    back_mid, gain_mid = norm_back(x_mid, gains[1], grad_normed)
    return grad_x + back_mid, gain_mid, (grad_f, grad_a, grad_b)


def layer_backward_attention(grad_mid, stored, gains, matrices, acc):
    wq, wk, wv, wo, wg, wu, wd = matrices
    x, h, q, k, v, pp, pq, o, x_mid, normed, a, b, u = stored
    grad_y = low(grad_mid)
    grad_o = low(dot_nt(grad_y, wo))
    grad_q, grad_k, grad_v, acc = attend_back(q, k, v, o, grad_o, pp, pq, acc)
    grad_h = dot_nt(grad_q, wq) + dot_nt(grad_k, wk) + dot_nt(grad_v, wv)
    back_in, gain_in = norm_back(x, gains[0], grad_h)
    return grad_mid + back_in, gain_in, acc, (grad_y, grad_q, grad_k, grad_v)


def local(
    wide,
    narrow,
    query_x,
    query_seg,
    passage_x,
    passage_seg,
    labels,
    lookup,
    softness,
    bias_grid,
    gains,
    wq,
    wk,
    wv,
    wo,
    wg,
    wu,
    wd,
    wp,
):
    qrows, qlen, feat = query_x.shape
    prows, plen, _ = passage_x.shape
    buckets, heads = bias_grid.shape
    matrices = (wq, wk, wv, wo, wg, wu, wd)
    order_a, order_b = stage_orders(wide, narrow)
    me_w, me_n = lax.axis_index("wide"), lax.axis_index("narrow")
    me = jnp.stack([me_w, me_n]).astype(jnp.int32)

    blocks = bias_blocks(lookup, bias_grid, query_seg, passage_seg)
    x = jnp.concatenate([query_x.reshape(-1, feat), passage_x.reshape(-1, feat)], axis=0).astype(F32)
    saved = []
    for _ in range(LAYERS):
        x, stored = layer_forward(x, blocks, gains, matrices)
        saved.append(stored)
    packed, vectors, e, pooled = pool(x, gains[2:3], query_seg, passage_seg, labels, wp)
    stages = order_b[1:] + order_b[:1]
    here, there = gather_all(packed, stages)
    grad_x, gain_final, loss_part, grad_e = loss_back(
        me, narrow, stages, softness, here, there, vectors, e, x, gains[2:3], query_seg, passage_seg, wp
    )
    hidden = wd.shape[0]
    block, cols, ff_block, ff_cols = feat // wide, feat // narrow, hidden // wide, hidden // narrow
    first, second = saved
    grad_mid, gain_mid, ffn_2 = layer_backward_ffn(grad_x, second, gains, matrices)
    grad_x, gain_in, acc, att_2 = layer_backward_attention(grad_mid, second, gains, matrices, None)

    x, h, q, k, v, pp, pq, o, x_mid, normed, a, b, u = first
    h_2, o_2, normed_2, u_2 = second[1], second[7], second[9], second[12]
    grad_f = low(grad_x)
    grad_a, grad_b = jax.vjp(gated_unit, a, b)[1](dot_nt(grad_f, wd))
    grad_a, grad_b = low(grad_a), low(grad_b)

    def attention_back(grad_a, grad_b):
        grad_normed = dot_nt(grad_a, wg) + dot_nt(grad_b, wu)
        back_mid, more = norm_back(x_mid, gains[1], grad_normed)
        grad_mid = grad_x + back_mid
        grad_y = low(grad_mid)
        grad_o = low(dot_nt(grad_y, wo))
        grad_q, grad_k, grad_v, total = attend_back(q, k, v, o, grad_o, pp, pq, acc)
        return grad_mid, gain_mid + more, grad_y, grad_q, grad_k, grad_v, total

    def input_back(grad_q, grad_k, grad_v, grad_mid, gain_mid, acc):
        grad_h = dot_nt(grad_q, wq) + dot_nt(grad_k, wk) + dot_nt(grad_v, wv)
        back_in, more = norm_back(x, gains[0], grad_h)
        sums = small_sums(
            acc, lookup, buckets, (gain_in + more)[None], gain_mid[None], gain_final, loss_part
        )
        return grad_mid + back_in, sums

    if cols % 128 or ff_block % 128 or block % 16:
        grad_mid, gain_mid, grad_y, grad_q, grad_k, grad_v, acc = attention_back(grad_a, grad_b)
        grad_x, sums = input_back(grad_q, grad_k, grad_v, grad_mid, gain_mid, acc)
        for axis, bit in order_a:
            sums = sums + swap(sums, axis, bit)

        def scatter(*pairs):
            full = low(sum(dot_tn(left, right) for left, right in pairs))
            full = lax.psum_scatter(full, "wide", scatter_dimension=1, tiled=True)
            return lax.psum_scatter(full, "narrow", scatter_dimension=0, tiled=True).astype(F32)

        grad_query = scatter((h, grad_q), (h_2, att_2[1]))
        grad_key = scatter((h, grad_k), (h_2, att_2[2]))
        grad_value = scatter((h, grad_v), (h_2, att_2[3]))
        grad_out = scatter((o, grad_y), (o_2, att_2[0]))
        grad_gate = scatter((normed, grad_a), (normed_2, ffn_2[1]))
        grad_up = scatter((normed, grad_b), (normed_2, ffn_2[2]))
        grad_down = scatter((u, grad_f), (u_2, ffn_2[0]))
        grad_proj = scatter((pooled, grad_e))
    else:
        orders = (order_a, order_b)
        down_rows, att_rows = block * ff_cols // 128, block * cols // 128
        parts = wgrad(
            me,
            [grad_f, ffn_2[0], u, u_2, normed, normed_2, grad_a, ffn_2[1]],
            [(0, 1), (2, 3), (4, 5), (6, 7)],
            [
                (0, 1, "wide", [(order_a, 0, block, 0)]),
                (2, 3, "narrow", [(order_b, 0, cols, down_rows)]),
            ],
            down_rows + cols,
            wide,
            narrow,
            16,
        )
        finals = [("turn", 0, block, ff_cols), ("keep", down_rows, cols, ff_block)]
        ffn = Chunk(*parts, down_rows, orders, finals)

        cut = (cols + att_rows) // 2 // 16 * 16

        def make_up(grad_b, *rest):
            return wgrad(
                me,
                [normed, normed_2, grad_b, ffn_2[2], grad_e, pooled],
                [(0, 1), (2, 3), (4,), (5,)],
                [
                    (0, 1, "narrow", [(order_a, 0, cut, 0), (order_b, cut, cols - cut, cut)]),
                    (2, 3, "wide", [(order_b, 0, block, cols)]),
                ],
                cols + att_rows,
                wide,
                narrow,
                12,
            )

        parts = exchange([ffn], make_up, (grad_b, normed, normed_2, grad_a))
        finals = [("keep", 0, cols, ff_block), ("turn", cols, block, cols)]
        up = Chunk(*parts, cut, orders, finals)
        grad_mid, gain_mid, grad_y, grad_q, grad_k, grad_v, acc = exchange(
            [ffn, up], attention_back, (grad_a, grad_b)
        )

        def make_rest(grad_y, grad_q, grad_k, grad_v, grad_mid, gain_mid, acc):
            parts = wgrad(
                me,
                [grad_y, att_2[0], o, o_2, grad_q, att_2[1], h, h_2, grad_k, att_2[2], grad_v, att_2[3]],
                [(0, 1), (2, 3), (4, 5), (6, 7), (8, 9), (10, 11)],
                [
                    (0, 1, "wide", [(order_a, 0, block, 0)]),
                    (2, 3, "wide", [(order_a, 0, block, att_rows)]),
                    (4, 3, "wide", [(order_b, 0, block, 2 * att_rows)]),
                    (5, 3, "wide", [(order_b, 0, block, 3 * att_rows)]),
                ],
                4 * att_rows,
                wide,
                narrow,
                12,
            )
            return parts, input_back(grad_q, grad_k, grad_v, grad_mid, gain_mid, acc)

        parts, (grad_x, sums) = exchange(
            [ffn, up], make_rest, (grad_y, grad_q, grad_k, grad_v, grad_mid, gain_mid, acc)
        )
        att = Chunk(*parts, 2 * att_rows, orders, [("turn", i * att_rows, block, cols) for i in range(4)])
        total = Total(sums, order_a)
        flows = [ffn, up, att, total]
        while not all(f.done for f in flows):
            exchange(flows, lambda: (), ())
        sums = total.value
        grad_down, grad_gate = ffn.result
        grad_up, grad_proj = up.result
        grad_out, grad_query, grad_key, grad_value = att.result
    gain_total, bucket_total = sums[:3], sums[4 : 4 + heads, :buckets].T
    mean_loss = sums[3, :1] / (qrows * QSEGS * wide * narrow)
    return (
        mean_loss,
        vectors[:QSEGS],
        vectors[QSEGS : QSEGS + PSEGS],
        grad_x[:qlen].reshape(1, qlen, feat),
        grad_x[qlen:].reshape(1, plen, feat),
        gain_total,
        bucket_total,
        grad_query,
        grad_key,
        grad_value,
        grad_out,
        grad_gate,
        grad_up,
        grad_down,
        grad_proj,
    )


def solution(mesh):
    rows3, rows2, rows1 = P(AXES, None, None), P(AXES, None), P(AXES)
    return jax.shard_map(
        functools.partial(local, mesh.shape["wide"], mesh.shape["narrow"]),
        mesh=mesh,
        in_specs=(rows3, rows2, rows3, rows2, rows1) + (P(),) * 12,
        out_specs=(P(), rows2, rows2, rows3, rows3, P(), P()) + (P("narrow", "wide"),) * 8,
        check_vma=False,
    )
```

```python
import functools

import jax
import jax.numpy as jnp
from jax import lax
from jax.experimental import pallas as pl
from jax.experimental.pallas import tpu as pltpu
from jax.sharding import PartitionSpec as P

LAYERS = 2
QSEGS = 3
PSEGS = 4
HDIM = 64
PACK = 8

HIGHEST = lax.Precision.HIGHEST
EPSILON = 1e-06
MASKED = -1000000000.0
BF = jnp.bfloat16
F32 = jnp.float32
AXES = ("wide", "narrow")


def low(a):
    return a.astype(BF)


def product(a, b):
    return jnp.dot(a, b, preferred_element_type=F32)


def dot_tn(a, b, precision=None):
    return lax.dot_general(
        a, b, (((0,), (0,)), ((), ())), preferred_element_type=F32, precision=precision
    )


def dot_nt(a, b, precision=None):
    return lax.dot_general(
        a, b, (((1,), (1,)), ((), ())), preferred_element_type=F32, precision=precision
    )


def rms_norm(x, gain_vec):
    return x * lax.rsqrt(jnp.mean(x * x, axis=-1, keepdims=True) + EPSILON) * gain_vec


def norm_back(x, gain_vec, grad_in):
    outcome, pullback = jax.vjp(rms_norm, x, gain_vec)
    return pullback(grad_in)


def whole():
    return pl.BlockSpec(memory_space=pltpu.VMEM)


def bias_kernel(qlen, plen, lookup_ref, grid_ref, qseg_ref, pseg_ref, pbias_ref, qbias_ref, wide_s, short_s):
    heads, buckets = grid_ref.shape
    width = 2 * plen
    wide_s[...] = jnp.full((1, width), -1, jnp.int32)
    wide_s[:, : lookup_ref.shape[1]] = lookup_ref[...]
    onehot = (
        lax.broadcasted_iota(jnp.int32, (buckets, width), 0)
        == jnp.broadcast_to(wide_s[...], (buckets, width))
    ).astype(F32)
    table = jnp.dot(grid_ref[...], onehot, precision=HIGHEST, preferred_element_type=F32)
    pcol = jnp.transpose(jnp.broadcast_to(pseg_ref[...], (plen, plen)))
    psame = pcol == jnp.broadcast_to(pseg_ref[...], (plen, plen))
    short_s[...] = jnp.full((1, 128), -1, jnp.int32)
    short_s[:, :qlen] = qseg_ref[...]
    qcol = jnp.transpose(jnp.broadcast_to(short_s[...], (128, 128)))
    qsame = (qcol == jnp.broadcast_to(short_s[...], (128, 128)))[:qlen, :qlen]
    for head in range(heads):
        rows = jnp.broadcast_to(table[head : head + 1, :], (plen, width))
        rolled = pltpu.roll(rows, width - (plen - 1), 1, stride=1, stride_axis=0)
        block = rolled[:, :plen]
        pbias_ref[head] = jnp.where(psame, block, MASKED)
        qbias_ref[head] = jnp.where(qsame, block[:qlen, :qlen], MASKED)


def half_mask(lanes, side):
    return (lax.broadcasted_iota(jnp.int32, (1, lanes), 1) // HDIM) == side


def attend_kernel(qlen, q_ref, k_ref, v_ref, pbias_ref, qbias_ref, o_ref, pp_ref, pq_ref):
    pairs = q_ref.shape[1] // 128
    spans = ((0, qlen, qbias_ref, pq_ref), (qlen, q_ref.shape[0] - qlen, pbias_ref, pp_ref))

    def pair(i, carry):
        lanes = pl.ds(pl.multiple_of(i * 128, 128), 128)
        for start, length, bias_ref, keep_ref in spans:
            rows = pl.ds(start, length)
            q2, k2, v2 = q_ref[rows, lanes], k_ref[rows, lanes], v_ref[rows, lanes]
            total = None
            for side in range(2):
                mine = half_mask(128, side)
                zero = jnp.zeros_like(k2)
                s = dot_nt(q2, jnp.where(mine, k2, zero)) + bias_ref[2 * i + side]
                top = jnp.max(s, axis=-1, keepdims=True)
                e = jnp.exp(s - top)
                p = low(e * (1.0 / jnp.sum(e, axis=-1, keepdims=True)))
                keep_ref[2 * i + side] = p
                part = product(p, jnp.where(mine, v2, zero))
                total = part if total is None else total + part
            o_ref[rows, lanes] = low(total)
        return carry

    lax.fori_loop(0, pairs, pair, 0)


def attend_back_kernel(
    qlen, q_ref, k_ref, v_ref, o_ref, go_ref, pp_ref, pq_ref, acc_ref, gq_ref, gk_ref, gv_ref, ds_ref
):
    pairs = q_ref.shape[1] // 128
    plen = q_ref.shape[0] - qlen

    def pair(i, carry):
        lanes = pl.ds(pl.multiple_of(i * 128, 128), 128)
        for start, length, keep_ref in ((qlen, plen, pp_ref), (0, qlen, pq_ref)):
            rows = pl.ds(start, length)
            q2, k2, v2 = q_ref[rows, lanes], k_ref[rows, lanes], v_ref[rows, lanes]
            o2, go2 = o_ref[rows, lanes], go_ref[rows, lanes]
            prod = o2.astype(F32) * go2.astype(F32)
            gq, gk, gv = None, None, None
            for side in range(2):
                mine = half_mask(128, side)
                zero = jnp.zeros_like(k2)
                p = keep_ref[2 * i + side]
                gp = dot_nt(go2, jnp.where(mine, v2, zero))
                delta = jnp.sum(jnp.where(mine, prod, 0.0), axis=-1, keepdims=True)
                ds = p.astype(F32) * (gp - delta)
                if start == qlen:
                    if acc_ref is None:
                        ds_ref[2 * i + side] = ds
                    else:
                        ds_ref[2 * i + side] = ds + acc_ref[2 * i + side]
                else:
                    ds_ref[2 * i + side, :length, :length] += ds
                dsl = low(ds)
                a = product(dsl, jnp.where(mine, k2, zero))
                b = dot_tn(dsl, jnp.where(mine, q2, zero))
                c = dot_tn(p, jnp.where(mine, go2, zero))
                gq = a if gq is None else gq + a
                gk = b if gk is None else gk + b
                gv = c if gv is None else gv + c
            gq_ref[rows, lanes] = low(gq)
            gk_ref[rows, lanes] = low(gk)
            gv_ref[rows, lanes] = low(gv)
        return carry

    lax.fori_loop(0, pairs, pair, 0)


def attend_back(q, k, v, o, go, pp, pq, acc):
    heads, plen, _ = pp.shape
    qlen = pq.shape[1]
    operands = [q, k, v, o, go, pp, pq] + ([] if acc is None else [acc])

    def body(*refs):
        ins = list(refs[: len(operands)])
        if acc is None:
            ins.append(None)
        attend_back_kernel(qlen, *ins, *refs[len(operands) :])

    return pl.pallas_call(
        body,
        out_shape=(jax.ShapeDtypeStruct(q.shape, BF),) * 3
        + (jax.ShapeDtypeStruct((heads, plen, plen), F32),),
        in_specs=[whole()] * len(operands),
        out_specs=(whole(),) * 4,
        name="attend_back",
        compiler_params=pltpu.CompilerParams(vmem_limit_bytes=14 << 20),
        cost_estimate=pl.CostEstimate(
            flops=8 * heads * HDIM * plen * plen, bytes_accessed=12 * heads * plen * plen, transcendentals=0
        ),
    )(*operands)


def small_kernel(
    buckets, ds_ref, lookup_ref, in_ref, mid_ref, final_ref, loss_ref, out_ref, diag_ref, wide_s
):
    heads, plen, _ = ds_ref.shape
    out_ref[...] = jnp.zeros_like(out_ref)
    out_ref[0:1, :] = in_ref[...]
    out_ref[1:2, :] = mid_ref[...]
    out_ref[2:3, :] = final_ref[...]
    out_ref[3:4, :128] = loss_ref[...]
    width = 2 * plen
    wide_s[...] = jnp.full((1, width), -1, jnp.int32)
    wide_s[:, : lookup_ref.shape[1]] = lookup_ref[...]
    for head in range(heads):
        block = ds_ref[head]
        wide_block = jnp.concatenate([block, jnp.zeros_like(block)], axis=1)
        rows = plen
        while rows > 8:
            rows //= 2
            wide_block = wide_block[:rows] + pltpu.roll(wide_block[rows:], width - rows, 1)
        at = lax.broadcasted_iota(jnp.int32, (8, width), 0)
        for bit in (4, 2, 1):
            moved = pltpu.roll(wide_block, width - bit, 1)
            wide_block = jnp.where((at & bit) != 0, moved, wide_block)
        rolled = pltpu.roll(wide_block, plen - 1, 1)
        diag_ref[head : head + 1, :] = jnp.sum(rolled, axis=0, keepdims=True)
    onehot = (
        lax.broadcasted_iota(jnp.int32, (buckets, width), 0)
        == jnp.broadcast_to(wide_s[...], (buckets, width))
    ).astype(F32)
    out_ref[4 : 4 + heads, :buckets] = dot_nt(diag_ref[...], onehot, HIGHEST)


def small_sums(ds, lookup, buckets, gain_in, gain_mid, gain_final, loss):
    heads, plen, _ = ds.shape
    width = 2 * plen
    return pl.pallas_call(
        functools.partial(small_kernel, buckets),
        out_shape=jax.ShapeDtypeStruct((4 + heads, gain_in.shape[1]), F32),
        in_specs=[whole()] * 6,
        out_specs=whole(),
        scratch_shapes=[pltpu.VMEM((heads, width), F32), pltpu.VMEM((1, width), jnp.int32)],
        name="small_sums",
        compiler_params=pltpu.CompilerParams(vmem_limit_bytes=8 << 20),
    )(ds, lookup[None], gain_in, gain_mid, gain_final, loss)


def segment_table(seg_ref, first):
    rows, length = PACK, seg_ref.shape[1]
    slot = lax.broadcasted_iota(jnp.int32, (rows, length), 0)
    return (slot == jnp.broadcast_to(seg_ref[...], (rows, length)) + first).astype(F32)


def pool_kernel(
    x_ref, gain_ref, qseg_ref, pseg_ref, label_ref, wp_ref, packed_ref, vec_ref, e_ref, pooled_ref
):
    qlen = qseg_ref.shape[1]
    x = x_ref[...]
    z = x * lax.rsqrt(jnp.mean(x * x, axis=-1, keepdims=True) + EPSILON) * gain_ref[...]
    qt, pt = segment_table(qseg_ref, 0), segment_table(pseg_ref, QSEGS)
    sizes = jnp.sum(qt, axis=1, keepdims=True) + jnp.sum(pt, axis=1, keepdims=True)
    sums = jnp.dot(qt, z[:qlen], precision=HIGHEST, preferred_element_type=F32) + jnp.dot(
        pt, z[qlen:], precision=HIGHEST, preferred_element_type=F32
    )
    pooled = low(sums / jnp.maximum(sizes, 1.0))
    pooled_ref[...] = pooled
    e = product(pooled, wp_ref[...])
    e_ref[...] = e
    vec = e * lax.rsqrt(jnp.sum(e * e, axis=-1, keepdims=True) + EPSILON)
    vec_ref[...] = vec
    at = lax.broadcasted_iota(jnp.int32, vec.shape, 1)
    row = lax.broadcasted_iota(jnp.int32, vec.shape, 0)
    code = jnp.zeros(vec.shape, F32)
    for i in range(QSEGS):
        label = label_ref[i]
        high = lax.shift_right_logical(label, 5).astype(F32)
        rest = (label & 31).astype(F32)
        code = jnp.where(at == i, high, jnp.where(at == QSEGS + i, rest, code))
    packed_ref[...] = low(jnp.where(row == PACK - 1, code, vec))


SLOPE = 0.7978845608028654
CUBE = 0.044715
SAVED = ("h", "q", "k", "v", "pp", "pq", "o", "x_mid", "normed", "da", "db", "u")


def unit_scale(x):
    return lax.rsqrt(jnp.mean(x * x, axis=-1, keepdims=True) + EPSILON)


def gated_parts(a, b):
    square = a * a
    th = jnp.tanh(a * (SLOPE + (SLOPE * CUBE) * square))
    half = 0.5 + 0.5 * th
    value = a * half
    slope = half + (0.5 * a) * (1.0 - th * th) * (SLOPE + (3.0 * SLOPE * CUBE) * square)
    return low(value * b), low(b * slope), low(value)


def forward_kernel(qlen, plen, n_tiles, *refs):
    (qx_ref, px_ref, lookup_ref, grid_ref, qseg_ref, pseg_ref, gains_ref, label_ref), refs = refs[:8], refs[8:]
    hbm, refs = refs[:8], refs[8:]
    packed_ref, vec_ref, e_ref, pooled_ref, x_mid_out, x_out = refs[:6]
    refs = refs[6:]
    outs = [dict(zip(SAVED, refs[n * len(SAVED) : (n + 1) * len(SAVED)])) for n in range(LAYERS)]
    refs = refs[LAYERS * len(SAVED) :]
    held, refs = refs[:8], refs[8:]
    keep, refs = dict(zip(SAVED, refs[: len(SAVED)])), refs[len(SAVED) :]
    x_s, pbias_s, qbias_s, wide_s, short_s, in_sem, out_sem, x_sem = refs
    wq_s, wk_s, wv_s, wo_s, wg_s, wu_s, wd_s, wp_s = held
    fetch = [pltpu.make_async_copy(a, b, in_sem.at[i]) for i, (a, b) in enumerate(zip(hbm, held))]
    for c in fetch:
        c.start()
    x_s[0, :qlen] = qx_ref[...].astype(F32)
    x_s[0, qlen:] = px_ref[...].astype(F32)
    bias_kernel(qlen, plen, lookup_ref, grid_ref, qseg_ref, pseg_ref, pbias_s, qbias_s, wide_s, short_s)

    def write(n, name):
        i = n * len(SAVED) + SAVED.index(name)
        return pltpu.make_async_copy(keep[name].at[n], outs[n][name], out_sem.at[i])

    def send(layer, *names):
        for n in range(LAYERS):

            @pl.when(layer == n)
            def _():
                for name in names:
                    write(n, name).start()

    def arrive(layer, *ids):
        @pl.when(layer == 0)
        def _():
            for i in ids:
                fetch[i].wait()

    def layer_step(layer, carry):
        x = x_s[layer]
        h = low(x * unit_scale(x) * gains_ref[0:1, :])
        keep["h"][layer] = h
        for i, (name, w) in enumerate((("q", wq_s), ("k", wk_s), ("v", wv_s))):
            arrive(layer, i)
            keep[name][layer] = low(product(h, w[...]))
        send(layer, "h", "q", "k", "v")
        at = {name: keep[name].at[layer] for name in SAVED}
        attend_kernel(qlen, at["q"], at["k"], at["v"], pbias_s, qbias_s, at["o"], at["pp"], at["pq"])
        send(layer, "o", "pp", "pq")
        arrive(layer, 3)
        x_mid = x_s[layer] + product(at["o"][...], wo_s[...])
        at["x_mid"][...] = x_mid
        normed = low(x_mid * unit_scale(x_mid) * gains_ref[1:2, :])
        at["normed"][...] = normed
        send(layer, "x_mid", "normed")
        arrive(layer, 4, 5)
        size = wg_s.shape[1] // n_tiles
        for t in range(n_tiles):
            lanes = slice(t * size, (t + 1) * size)
            a = product(normed, wg_s[:, lanes])
            b = product(normed, wu_s[:, lanes])
            u, da, db = gated_parts(a, b)
            at["u"][:, lanes] = u
            at["da"][:, lanes] = da
            at["db"][:, lanes] = db
        send(layer, "u", "da", "db")
        arrive(layer, 6)
        x_s[layer + 1] = at["x_mid"][...] + product(at["u"][...], wd_s[...])
        return carry

    lax.fori_loop(0, LAYERS, layer_step, 0)
    inner = pltpu.make_async_copy(x_s.at[1], x_mid_out, x_sem.at[0])
    outer = pltpu.make_async_copy(x_s.at[LAYERS], x_out, x_sem.at[1])
    inner.start()
    outer.start()
    fetch[7].wait()
    pool_kernel(
        x_s.at[LAYERS], gains_ref.at[2:3], qseg_ref, pseg_ref, label_ref, wp_s, packed_ref, vec_ref, e_ref, pooled_ref
    )
    for n in range(LAYERS):
        for name in SAVED:
            write(n, name).wait()
    inner.wait()
    outer.wait()


def saved_shapes(total, qlen, plen, feat, hidden, heads):
    tok, ff = ((total, feat), BF), ((total, hidden), BF)
    kinds = dict(h=tok, q=tok, k=tok, v=tok, o=tok, normed=tok, da=ff, db=ff, u=ff)
    kinds["pp"], kinds["pq"] = ((heads, plen, plen), BF), ((heads, qlen, qlen), BF)
    kinds["x_mid"] = ((total, feat), F32)
    return [kinds[name] for name in SAVED]


def forward(qx, px, lookup, grid, qseg, pseg, gains, labels, matrices):
    qlen, feat = qx.shape
    plen, heads, hidden = px.shape[0], grid.shape[0], matrices[4].shape[1]
    total = qlen + plen
    kinds = saved_shapes(total, qlen, plen, feat, hidden, heads)
    small = (PACK, feat)
    shapes = [(small, BF), (small, F32), (small, F32), (small, BF), ((total, feat), F32), ((total, feat), F32)]
    shapes += kinds * LAYERS
    anywhere = pl.BlockSpec(memory_space=pltpu.HBM)
    smem = pl.BlockSpec(memory_space=pltpu.SMEM)
    weights = sum(m.size for m in matrices)
    outs = pl.pallas_call(
        functools.partial(forward_kernel, qlen, plen, 4),
        out_shape=tuple(jax.ShapeDtypeStruct(*s) for s in shapes),
        in_specs=[whole()] * 7 + [smem] + [anywhere] * 8,
        out_specs=(whole(),) * 4 + (anywhere,) * (2 + LAYERS * len(SAVED)),
        scratch_shapes=[pltpu.VMEM(m.shape, BF) for m in matrices]
        + [pltpu.VMEM((LAYERS,) + shape, dtype) for shape, dtype in kinds]
        + [
            pltpu.VMEM((LAYERS + 1, total, feat), F32),
            pltpu.VMEM((heads, plen, plen), F32),
            pltpu.VMEM((heads, qlen, qlen), F32),
            pltpu.VMEM((1, 2 * plen), jnp.int32),
            pltpu.VMEM((1, 128), jnp.int32),
            pltpu.SemaphoreType.DMA((8,)),
            pltpu.SemaphoreType.DMA((LAYERS * len(SAVED),)),
            pltpu.SemaphoreType.DMA((2,)),
        ],
        name="forward",
        compiler_params=pltpu.CompilerParams(vmem_limit_bytes=56 << 20),
        cost_estimate=pl.CostEstimate(
            flops=2 * LAYERS * total * weights, bytes_accessed=2 * weights, transcendentals=LAYERS * total * hidden
        ),
    )(qx, px, lookup[None], grid, qseg, pseg, gains, labels, *matrices)
    saved = [dict(zip(SAVED, outs[6 + n * len(SAVED) : 6 + (n + 1) * len(SAVED)])) for n in range(LAYERS)]
    return outs[:6], saved


def loss_kernel(
    narrow, stages, me_ref, sharp_ref, here_ref, there_ref, vec_ref, e_ref, x_ref, gain_ref,
    qseg_ref, pseg_ref, wp_ref, gx_ref, ggain_ref, loss_ref, ge_ref, flat_s,
):
    half = here_ref.shape[0]
    flat_s[:half, :] = here_ref[...]
    flat_s[half:, :] = there_ref[...]
    size = 2 * half
    tile = min(size, 256)
    sharp = sharp_ref[0]
    lane = lax.broadcasted_iota(jnp.int32, (1, size), 1)
    block, slot = lax.shift_right_logical(lane, 3), lane & (PACK - 1)
    dw, dn = jnp.zeros_like(block), jnp.zeros_like(block)
    for k, (axis, bit) in enumerate(stages):
        on = (lax.shift_right_logical(block, k) & 1) * bit
        dw, dn = (dw + on, dn) if axis == "wide" else (dw, dn + on)
    device = (dw ^ me_ref[0]) * narrow + (dn ^ me_ref[1])
    is_passage = (slot >= QSEGS) & (slot < QSEGS + PSEGS)
    document = jnp.where(is_passage, device * PSEGS + slot - QSEGS, -2)
    row = lax.broadcasted_iota(jnp.int32, (tile, 1), 0)
    row_slot = row & (PACK - 1)
    is_query = row_slot < QSEGS
    across = lax.broadcasted_iota(jnp.int32, (tile, tile), 1)
    source = low((across == row - row_slot + PACK - 1).astype(F32))
    place = lax.broadcasted_iota(jnp.int32, (tile, 128), 1)
    weigh = jnp.where(place == row_slot, 32.0, 0.0) + jnp.where(place == row_slot + QSEGS, 1.0, 0.0)
    mine = lax.broadcasted_iota(jnp.int32, (1, 128), 1) < PACK
    grad = None
    for t in range(size // tile):
        rows = flat_s[t * tile : (t + 1) * tile, :]
        match = dot_nt(rows, flat_s[...]) / sharp
        match = jnp.where(is_passage, match, MASKED)
        label = jnp.sum(product(source, rows[:, :128]) * weigh, axis=1, keepdims=True)
        hit = (label.astype(jnp.int32) == document) & is_query
        top = jnp.max(match, axis=1, keepdims=True)
        ex = jnp.exp(match - top)
        line = jnp.sum(ex, axis=1, keepdims=True)
        g = (ex / line - hit.astype(F32)) / sharp
        g = low(jnp.where(is_query & is_passage, g, 0.0))
        back = dot_tn(jnp.where(mine, g[:, :128], jnp.zeros_like(g[:, :128])), rows)[:PACK]
        if t == 0:
            part = jnp.sum(jnp.where(hit, match, 0.0), axis=1, keepdims=True)
            part = jnp.where(is_query & (row < PACK), top + jnp.log(line) - part, 0.0)
            loss_ref[...] = jnp.broadcast_to(jnp.sum(part, axis=0, keepdims=True), loss_ref.shape)
            grad = product(g[:16], flat_s[...])[:PACK]
        grad = grad + back
    e, vec = e_ref[...], vec_ref[...]
    scale = lax.rsqrt(jnp.sum(e * e, axis=-1, keepdims=True) + EPSILON)
    ge = low((grad - vec * jnp.sum(vec * grad, axis=-1, keepdims=True)) * scale)
    ge_ref[...] = ge
    qt, pt = segment_table(qseg_ref, 0), segment_table(pseg_ref, QSEGS)
    sizes = jnp.sum(qt, axis=1, keepdims=True) + jnp.sum(pt, axis=1, keepdims=True)
    pooled = dot_nt(ge, wp_ref[...]) / jnp.maximum(sizes, 1.0)
    qlen = qseg_ref.shape[1]
    gain = gain_ref[...]
    total = None
    for table, start, count in ((qt, 0, qlen), (pt, qlen, pseg_ref.shape[1])):
        gz = dot_tn(table, pooled, HIGHEST)
        x = x_ref[start : start + count, :]
        r = lax.rsqrt(jnp.mean(x * x, axis=-1, keepdims=True) + EPSILON)
        unit = x * r
        scaled = gz * gain
        gx_ref[start : start + count, :] = r * (
            scaled - unit * jnp.mean(unit * scaled, axis=-1, keepdims=True)
        )
        part = jnp.sum(gz * unit, axis=0, keepdims=True)
        total = part if total is None else total + part
    ggain_ref[...] = total


BACK = ("grad_f", "ga", "gb", "gy", "gq", "gk", "gv", "ds", "grad_f1", "ga1", "gb1", "grad_x")


def through_norm(x, gain, grad):
    r = unit_scale(x)
    unit = x * r
    scaled = grad * gain
    back = r * (scaled - unit * jnp.mean(unit * scaled, axis=-1, keepdims=True))
    return back, jnp.sum(grad * unit, axis=0, keepdims=True)


def back_kernel(narrow, stages, qlen, n_tiles, n_held, *refs):
    me_ref, sharp_ref, here_ref, there_ref, vec_ref, e_ref, gains_ref, qseg_ref, pseg_ref = refs[:9]
    refs = refs[9:]
    hbm, refs = refs[:n_held], refs[n_held:]
    ggain_ref, loss_ref, ge_ref, gmid_ref, gin_ref = refs[:5]
    outs, refs = dict(zip(BACK, refs[5 : 5 + len(BACK)])), refs[5 + len(BACK) :]
    held, refs = refs[:n_held], refs[n_held:]
    keep, refs = dict(zip(BACK, refs[: len(BACK)])), refs[len(BACK) :]
    flat_s, gx_s, go_s, in_sem, out_sem = refs
    fetch = [pltpu.make_async_copy(a, b, in_sem.at[i]) for i, (a, b) in enumerate(zip(hbm, held))]
    for c in fetch:
        c.start()
    (x2_s, wp_s, wd_s, da_s, db_s, wg_s, wu_s, xm_s, wo_s, v_s, o_s, pp_s, k_s, q_s, pq_s) = held[:15]
    wq_s, wk_s, wv_s, x_s, da1_s, db1_s = held[15:]

    def send(*names):
        for name in names:
            pltpu.make_async_copy(keep[name], outs[name], out_sem.at[BACK.index(name)]).start()

    fetch[0].wait()
    fetch[1].wait()
    loss_kernel(
        narrow, stages, me_ref, sharp_ref, here_ref, there_ref, vec_ref, e_ref, x2_s, gains_ref.at[2:3],
        qseg_ref, pseg_ref, wp_s, gx_s, ggain_ref, loss_ref, ge_ref, flat_s,
    )

    def gated_back(x_ref, da, db, names):
        grad_f = low(x_ref[...])
        keep[names[0]][...] = grad_f
        size = da.shape[1] // n_tiles
        for t in range(n_tiles):
            lanes = slice(t * size, (t + 1) * size)
            gu = dot_nt(grad_f, wd_s[lanes, :])
            keep[names[1]][:, lanes] = low(gu * da[:, lanes].astype(F32))
            keep[names[2]][:, lanes] = low(gu * db[:, lanes].astype(F32))
        send(*names)

    for i in (2, 3, 4):
        fetch[i].wait()
    gated_back(gx_s, da_s, db_s, BACK[:3])
    for i in (5, 6, 7):
        fetch[i].wait()
    grad = dot_nt(keep["ga"][...], wg_s[...]) + dot_nt(keep["gb"][...], wu_s[...])
    back, gmid_ref[...] = through_norm(xm_s[...], gains_ref[1:2, :], grad)
    grad_mid = gx_s[...] + back
    gx_s[...] = grad_mid
    gy = low(grad_mid)
    keep["gy"][...] = gy
    send("gy")
    fetch[8].wait()
    go_s[...] = low(dot_nt(gy, wo_s[...]))
    for i in range(9, 15):
        fetch[i].wait()
    attend_back_kernel(
        qlen, q_s, k_s, v_s, o_s, go_s, pp_s, pq_s, None, keep["gq"], keep["gk"], keep["gv"], keep["ds"]
    )
    send("gq", "gk", "gv", "ds")
    for i in range(15, 19):
        fetch[i].wait()
    grad = dot_nt(keep["gq"][...], wq_s[...]) + dot_nt(keep["gk"][...], wk_s[...])
    grad = grad + dot_nt(keep["gv"][...], wv_s[...])
    back, gin_ref[...] = through_norm(x_s[...], gains_ref[0:1, :], grad)
    keep["grad_x"][...] = gx_s[...] + back
    send("grad_x")
    fetch[19].wait()
    fetch[20].wait()
    gated_back(keep["grad_x"], da1_s, db1_s, BACK[8:11])
    for name in BACK:
        pltpu.make_async_copy(keep[name], outs[name], out_sem.at[BACK.index(name)]).wait()


def loss_and_back(me, narrow, stages, sharp, here, there, vec, e, gains, qseg, pseg, x_last, x_in, first, second, matrices):
    wq, wk, wv, wo, wg, wu, wd, wp = matrices
    total, feat = x_last.shape
    qlen, plen = qseg.shape[1], pseg.shape[1]
    heads, hidden = second["pp"].shape[0], wd.shape[0]
    size = 2 * here.shape[0]
    t = second
    fetched = [x_last, wp, wd, t["da"], t["db"], wg, wu, t["x_mid"], wo, t["v"], t["o"], t["pp"], t["k"], t["q"], t["pq"]]
    fetched += [wq, wk, wv, x_in, first["da"], first["db"]]
    tok, ff = ((total, feat), BF), ((total, hidden), BF)
    kinds = [tok, ff, ff, tok, tok, tok, tok, ((heads, plen, plen), F32), tok, ff, ff, ((total, feat), F32)]
    small = [((1, feat), F32), ((1, 128), F32), ((PACK, feat), BF), ((1, feat), F32), ((1, feat), F32)]
    anywhere = pl.BlockSpec(memory_space=pltpu.HBM)
    smem = pl.BlockSpec(memory_space=pltpu.SMEM)
    weights = sum(m.size for m in matrices)
    outs = pl.pallas_call(
        functools.partial(back_kernel, narrow, stages, qlen, 4, len(fetched)),
        out_shape=tuple(jax.ShapeDtypeStruct(*s) for s in small + kinds),
        in_specs=[smem, smem] + [whole()] * 7 + [anywhere] * len(fetched),
        out_specs=(whole(),) * 5 + (anywhere,) * len(kinds),
        scratch_shapes=[pltpu.VMEM(a.shape, a.dtype) for a in fetched]
        + [pltpu.VMEM(*k) for k in kinds]
        + [
            pltpu.VMEM((size, feat), BF),
            pltpu.VMEM((total, feat), F32),
            pltpu.VMEM((total, feat), BF),
            pltpu.SemaphoreType.DMA((len(fetched),)),
            pltpu.SemaphoreType.DMA((len(kinds),)),
        ],
        name="loss_and_back",
        compiler_params=pltpu.CompilerParams(vmem_limit_bytes=56 << 20),
        cost_estimate=pl.CostEstimate(
            flops=3 * total * weights, bytes_accessed=2 * weights, transcendentals=0
        ),
    )(me, sharp, here, there, vec, e, gains, qseg, pseg, *fetched)
    return outs[:5], dict(zip(BACK, outs[5:]))


def join_kernel(*refs):
    ins, out_ref = refs[:-1], refs[-1]
    rows = ins[0].shape[0]
    for i, ref in enumerate(ins):
        out_ref[i * rows : (i + 1) * rows, :] = ref[...]


def join(*parts):
    a = parts[0]
    return pl.pallas_call(
        join_kernel,
        out_shape=jax.ShapeDtypeStruct((len(parts) * a.shape[0], a.shape[1]), a.dtype),
        in_specs=[whole()] * len(parts),
        out_specs=whole(),
        name="join",
        compiler_params=pltpu.CompilerParams(vmem_limit_bytes=4 << 20),
    )(*parts)


def stage_orders(wide, narrow):
    wbits = [1 << i for i in range(wide.bit_length() - 1)]
    nbits = [1 << i for i in range(narrow.bit_length() - 1)]
    w = lambda bits: [("wide", b) for b in bits]
    n = [("narrow", b) for b in nbits]
    tail = w(wbits[2:])
    return (w(wbits[:1]) + w(wbits[1:2]) + n + tail, w(wbits[:1]) + n + w(wbits[1:2]) + tail)


def place_of(order, dw, dn):
    place = 0
    for axis, bit in order:
        own = dw if axis == "wide" else dn
        place = place * 2 + (own // bit) % 2
    return place


def traced_place(order, dw, dn):
    place = 0
    for axis, bit in order:
        own = dw if axis == "wide" else dn
        place = place * 2 + (lax.shift_right_logical(own, bit.bit_length() - 1) & 1)
    return place


def wgrad_kernel(jobs, groups, n_ops, me_ref, *refs):
    ops, (keep_ref, send_ref) = refs[:n_ops], refs[n_ops : n_ops + 2]
    held = refs[n_ops + 2 : n_ops + 2 + len(groups)]
    turned_s, sems = refs[-2:]
    me_w, me_n = me_ref[0], me_ref[1]
    half = keep_ref.shape[0]
    copies = []
    for ids, buf in zip(groups, held):
        first, own = 0, []
        for i in ids:
            count = ops[i].shape[0]
            sem = sems.at[sum(len(c) for c in copies) + len(own)]
            own.append(pltpu.make_async_copy(ops[i], buf.at[first : first + count], sem))
            first += count
        copies.append(own)
    for own in copies:
        for c in own:
            c.start()
    ready = set()

    def arrive(g):
        if g not in ready:
            for c in copies[g]:
                c.wait()
            ready.add(g)

    def store(acc, job, w_first, n_first):
        row_axis, block_rows, block_lanes, targets = job[2:]
        blocks = [
            (bi, bj)
            for bi in range(acc.shape[0] // block_rows)
            for bj in range(acc.shape[1] // block_lanes)
        ]
        bases = [traced_place(t[0], w_first ^ me_w, n_first ^ me_n) for t in targets]
        for core in range(2):

            @pl.when((me_w & 1) == core)
            def _():
                for bi, bj in blocks:
                    w, n = (bi, bj) if row_axis == "wide" else (bj, bi)
                    out_ref = keep_ref if (w & 1) == core else send_ref
                    for (order, first, count, offset), base in zip(targets, bases):
                        at = (base ^ place_of(order, w, n)) & (half - 1)
                        for k in range(block_lanes // 128):
                            lane = bj * block_lanes + k * 128
                            row = bi * block_rows + first
                            out_ref[at, offset + k * count : offset + (k + 1) * count, :] = acc[
                                row : row + count, lane : lane + 128
                            ]

    for job in jobs:
        rg, lg, row_axis, block_rows, block_lanes, targets = job
        arrive(rg)
        arrive(lg)
        row_s, lane_s = held[rg], held[lg]
        depth, rows, lanes = row_s.shape[0], row_s.shape[1], lane_s.shape[1]
        tile_rows = 384
        tile_lanes = block_lanes
        while tile_lanes < 512 and lanes % (2 * tile_lanes) == 0:
            tile_lanes *= 2
        per_row, per_lane = tile_rows // block_rows, tile_lanes // block_lanes

        def row_step(rt, carry):
            mine = row_s[:, pl.ds(pl.multiple_of(rt * tile_rows, 128), tile_rows)]
            if depth > 16:
                turned_s[...] = mine.T

            def lane_step(lt, inner):
                part = lane_s[:, pl.ds(pl.multiple_of(lt * tile_lanes, 128), tile_lanes)]
                acc = product(turned_s[...], part) if depth > 16 else dot_tn(mine, part)
                if row_axis == "wide":
                    store(low(acc), job, rt * per_row, lt * per_lane)
                else:
                    store(low(acc), job, lt * per_lane, rt * per_row)
                return inner

            if lanes == tile_lanes:
                return lane_step(0, carry)
            return lax.fori_loop(0, lanes // tile_lanes, lane_step, carry)

        lax.fori_loop(0, rows // tile_rows, row_step, 0)


def wgrad(me, ops, groups, jobs, total_rows, wide, narrow, vmem):
    half = wide * narrow // 2
    width = lambda g: ops[groups[g][0]].shape[1]
    depth = [sum(ops[i].shape[0] for i in g) for g in groups]
    full = []
    for rg, lg, row_axis, targets in jobs:
        split = (wide, narrow) if row_axis == "wide" else (narrow, wide)
        full.append((rg, lg, row_axis, width(rg) // split[0], width(lg) // split[1], targets))
    flops = sum(2 * depth[j[0]] * width(j[0]) * width(j[1]) for j in full)
    return pl.pallas_call(
        functools.partial(wgrad_kernel, full, groups, len(ops)),
        out_shape=(jax.ShapeDtypeStruct((half, total_rows, 128), BF),) * 2,
        in_specs=[pl.BlockSpec(memory_space=pltpu.SMEM)]
        + [pl.BlockSpec(memory_space=pltpu.HBM)] * len(ops),
        out_specs=(whole(),) * 2,
        scratch_shapes=[pltpu.VMEM((d, width(g)), BF) for g, d in enumerate(depth)]
        + [pltpu.VMEM((384, max(depth)), BF), pltpu.SemaphoreType.DMA((sum(map(len, groups)),))],
        name="wgrad",
        compiler_params=pltpu.CompilerParams(vmem_limit_bytes=vmem << 20),
        cost_estimate=pl.CostEstimate(flops=flops, bytes_accessed=flops // 256, transcendentals=0),
    )(me, *ops)


def swap(a, *stage):
    dw = sum(bit for axis, bit in stage if axis == "wide")
    dn = sum(bit for axis, bit in stage if axis == "narrow")
    wide, narrow = lax.axis_size("wide"), lax.axis_size("narrow")
    if not dn:
        return lax.ppermute(a, "wide", [(i, i ^ dw) for i in range(wide)])
    if not dw:
        return lax.ppermute(a, "narrow", [(i, i ^ dn) for i in range(narrow)])
    pairs = [(i * narrow + j, (i ^ dw) * narrow + (j ^ dn)) for i in range(wide) for j in range(narrow)]
    return lax.ppermute(a, AXES, pairs)


def relatives(stage):
    if len(stage) == 1:
        return [stage]
    return [(stage[1],), (stage[0],), tuple(stage)]


def grouped(order, direct):
    if not direct:
        return [(s,) for s in order]
    return [(s,) for s in order[:-2]] + [tuple(order[-2:])]


class Chunk:
    def __init__(self, keep, send, split, orders, finals, direct=False):
        self.rows, self.split, self.finals = keep.shape[1], split, finals
        self.orders = [grouped(order, direct) for order in orders]
        self.stage, self.parts = 0, [(keep, send)]
        self.done = False

    def spans(self, stage):
        if self.orders[0][stage] == self.orders[1][stage] and (
            stage == 0 or self.orders[0][stage:] == self.orders[1][stage:]
        ):
            return [(0, self.rows, self.orders[0])]
        return [(0, self.split, self.orders[0]), (self.split, self.rows, self.orders[1])]

    def start(self):
        return [
            [swap(a, *to) for a, to in zip(part[1:], relatives(order[self.stage]))]
            for part, (_, _, order) in zip(self.parts, self.spans(self.stage))
        ]


def doubled(value, stages):
    for stage in stages:
        value = value + swap(value, stage)
    return value


def advance(flows):
    operands, shapes, steps = [], [], []
    for f in flows:
        now = f.spans(f.stage)
        last = f.stage == len(f.orders[0]) - 1
        first_in, first_out = len(operands), len(shapes)
        for part, got in zip(f.parts, f.got):
            operands += [part[0]] + got
        half = f.parts[0][0].shape[0] // 2
        if last:
            for kind, offset, rows, lanes in f.finals:
                shapes.append(jax.ShapeDtypeStruct((rows, lanes), F32))
            steps.append(("final", first_in, first_out, f.finals, len(f.got[0])))
        else:
            later = f.spans(f.stage + 1)
            ways = 2 ** len(f.orders[0][f.stage + 1])
            for lo, hi, _ in later:
                shapes += [jax.ShapeDtypeStruct((2 * half // ways, hi - lo, 128), BF)] * ways
            steps.append(
                ("halve", first_in, first_out, [n[:2] for n in now], [n[:2] for n in later], ways)
            )

    def whole_sum(ins, i, count, pick):
        total = pick(ins[i]) + pick(ins[i + 1])
        return total if count == 1 else total + (pick(ins[i + 2]) + pick(ins[i + 3]))

    def body(*refs):
        ins, outs = refs[: len(operands)], refs[len(operands) :]
        for step in steps:
            kind, i, o = step[:3]
            if kind == "final":
                for n, (_, offset, rows, lanes) in enumerate(step[3]):
                    for k in range(lanes // 128):
                        span = pl.ds(offset + k * rows, rows)
                        value = whole_sum(ins, i, step[4], lambda ref: ref[0, span, :].astype(F32))
                        outs[o + n][:, k * 128 : (k + 1) * 128] = value
            else:
                ways = step[5]
                for p, (lo, hi) in enumerate(step[3]):
                    for q, (lo2, hi2) in enumerate(step[4]):
                        a, b = max(lo, lo2), min(hi, hi2)
                        if a >= b:
                            continue
                        keep_ref, got_ref = ins[i + 2 * p], ins[i + 2 * p + 1]
                        count = keep_ref.shape[0] // ways
                        for side in range(ways):
                            out_ref = outs[o + ways * q + side]

                            def block(n, carry):
                                src = pl.ds(a - lo, b - a)
                                value = keep_ref[side * count + n, src, :].astype(F32)
                                value = value + got_ref[side * count + n, src, :].astype(F32)
                                out_ref[n, a - lo2 : b - lo2, :] = low(value)
                                return carry

                            if count == 1:
                                block(0, 0)
                            else:
                                lax.fori_loop(0, count, block, 0)

    room = (1 << 20) + sum(a.size * a.dtype.itemsize for a in operands + shapes)
    outs = pl.pallas_call(
        body,
        out_shape=tuple(shapes),
        in_specs=[whole()] * len(operands),
        out_specs=(whole(),) * len(shapes),
        name="advance",
        compiler_params=pltpu.CompilerParams(vmem_limit_bytes=room),
    )(*operands)
    at = 0
    for f, step in zip(flows, steps):
        f.stage += 1
        if step[0] == "final":
            f.result = [
                out.T if final[0] == "turn" else out
                for out, final in zip(outs[at : at + len(step[3])], step[3])
            ]
            at += len(step[3])
            f.done = True
        else:
            ways = step[5]
            f.parts = [tuple(outs[at + ways * q : at + ways * (q + 1)]) for q in range(len(step[4]))]
            at += ways * len(step[4])


def exchange(begin, compute, inputs):
    sent, inputs = lax.optimization_barrier(([f.parts for f in begin], inputs))
    for f, value in zip(begin, sent):
        f.parts = value
    for f in begin:
        f.got = f.start()
    got, made = lax.optimization_barrier(([f.got for f in begin], compute(*inputs)))
    for f, value in zip(begin, got):
        f.got = value
    advance(begin)
    return made


def gather_stages(order):
    far, near = order[3:], order[1:3]
    return [far[i : i + 2] for i in range(0, len(far), 2)] + [near] + [order[:1]]


def gather_all(rows, stages):
    for stage in stages[:-1]:
        got = [swap(rows, *to) for to in ([stage] if len(stage) == 1 else [stage[:1], stage[1:], stage])]
        rows = join(rows, *got)
    return rows, swap(rows, *stages[-1])


def local(
    wide,
    narrow,
    query_x,
    query_seg,
    passage_x,
    passage_seg,
    labels,
    lookup,
    softness,
    bias_grid,
    gains,
    wq,
    wk,
    wv,
    wo,
    wg,
    wu,
    wd,
    wp,
):
    qrows, qlen, feat = query_x.shape
    prows, plen, _ = passage_x.shape
    buckets, heads = bias_grid.shape
    order_a, order_b = stage_orders(wide, narrow)
    me_w, me_n = lax.axis_index("wide"), lax.axis_index("narrow")
    me = jnp.stack([me_w, me_n]).astype(jnp.int32)

    hidden = wd.shape[0]
    block, cols, ff_block, ff_cols = feat // wide, feat // narrow, hidden // wide, hidden // narrow
    matrices = (wq, wk, wv, wo, wg, wu, wd, wp)
    (packed, vectors, e, pooled, x_between, x_last), (first, second) = forward(
        query_x.reshape(-1, feat),
        passage_x.reshape(-1, feat),
        lookup,
        bias_grid.T,
        query_seg,
        passage_seg,
        gains,
        labels,
        matrices,
    )
    groups = gather_stages(order_a)
    stages = [bit for group in groups for bit in group]
    here, there = gather_all(packed, groups)
    (gain_final, loss_part, grad_e, gain_mid, gain_in), back = loss_and_back(
        me, narrow, stages, softness, here, there, vectors, e, gains, query_seg, passage_seg,
        x_last, x_between, first, second, matrices,
    )
    gain_mid, gain_in = gain_mid[0], gain_in[0]
    ffn_2 = (back["grad_f"], back["ga"], back["gb"])
    att_2 = (back["gy"], back["gq"], back["gk"], back["gv"])
    acc, grad_x = back["ds"], back["grad_x"]
    grad_f, grad_a, grad_b = back["grad_f1"], back["ga1"], back["gb1"]
    h, q, k, v, pp, pq, o, x_mid, normed, _, _, u = (first[name] for name in SAVED)
    h_2, o_2, normed_2, u_2 = second["h"], second["o"], second["normed"], second["u"]

    def attention_back(grad_a, grad_b):
        grad_normed = dot_nt(grad_a, wg) + dot_nt(grad_b, wu)
        back_mid, more = norm_back(x_mid, gains[1], grad_normed)
        grad_mid = grad_x + back_mid
        grad_y = low(grad_mid)
        grad_o = low(dot_nt(grad_y, wo))
        grad_q, grad_k, grad_v, total = attend_back(q, k, v, o, grad_o, pp, pq, acc)
        return grad_mid, gain_mid + more, grad_y, grad_q, grad_k, grad_v, total

    def input_back(grad_q, grad_k, grad_v, grad_mid, gain_mid, acc):
        grad_h = dot_nt(grad_q, wq) + dot_nt(grad_k, wk) + dot_nt(grad_v, wv)
        x = jnp.concatenate([query_x.reshape(-1, feat), passage_x.reshape(-1, feat)], axis=0).astype(F32)
        back_in, more = norm_back(x, gains[0], grad_h)
        sums = small_sums(
            acc, lookup, buckets, (gain_in + more)[None], gain_mid[None], gain_final, loss_part
        )
        return grad_mid + back_in, sums

    if cols % 128 or ff_block % 128 or block % 16:
        grad_mid, gain_mid, grad_y, grad_q, grad_k, grad_v, acc = attention_back(grad_a, grad_b)
        grad_x, sums = input_back(grad_q, grad_k, grad_v, grad_mid, gain_mid, acc)
        sums = doubled(sums, order_a)

        def scatter(*pairs):
            full = low(sum(dot_tn(left, right) for left, right in pairs))
            full = lax.psum_scatter(full, "wide", scatter_dimension=1, tiled=True)
            return lax.psum_scatter(full, "narrow", scatter_dimension=0, tiled=True).astype(F32)

        grad_query = scatter((h, grad_q), (h_2, att_2[1]))
        grad_key = scatter((h, grad_k), (h_2, att_2[2]))
        grad_value = scatter((h, grad_v), (h_2, att_2[3]))
        grad_out = scatter((o, grad_y), (o_2, att_2[0]))
        grad_gate = scatter((normed, grad_a), (normed_2, ffn_2[1]))
        grad_up = scatter((normed, grad_b), (normed_2, ffn_2[2]))
        grad_down = scatter((u, grad_f), (u_2, ffn_2[0]))
        grad_proj = scatter((pooled, grad_e))
    else:
        orders = (order_a, order_b)
        down_rows, att_rows = block * ff_cols // 128, block * cols // 128
        parts = wgrad(
            me,
            [grad_f, ffn_2[0], u, u_2, normed, normed_2, grad_a, ffn_2[1]],
            [(0, 1), (2, 3), (4, 5), (6, 7)],
            [
                (0, 1, "wide", [(order_a, 0, block, 0)]),
                (2, 3, "narrow", [(order_b, 0, cols, down_rows)]),
            ],
            down_rows + cols,
            wide,
            narrow,
            16,
        )
        finals = [("turn", 0, block, ff_cols), ("keep", down_rows, cols, ff_block)]
        ffn = Chunk(*parts, down_rows, orders, finals)

        cut = (cols + att_rows) // 2 // 16 * 16

        def make_up(grad_b, *rest):
            return wgrad(
                me,
                [normed, normed_2, grad_b, ffn_2[2], grad_e, pooled],
                [(0, 1), (2, 3), (4,), (5,)],
                [
                    (0, 1, "narrow", [(order_a, 0, cut, 0), (order_b, cut, cols - cut, cut)]),
                    (2, 3, "wide", [(order_b, 0, block, cols)]),
                ],
                cols + att_rows,
                wide,
                narrow,
                12,
            )

        parts = exchange([ffn], make_up, (grad_b, normed, normed_2, grad_a))
        finals = [("keep", 0, cols, ff_block), ("turn", cols, block, cols)]
        up = Chunk(*parts, cut, orders, finals)

        def rest_back(grad_a, grad_b):
            grad_mid, gain_mid, grad_y, grad_q, grad_k, grad_v, acc = attention_back(grad_a, grad_b)
            grad_x, sums = input_back(grad_q, grad_k, grad_v, grad_mid, gain_mid, acc)
            return grad_x, sums, grad_y, grad_q, grad_k, grad_v

        grad_x, sums, *grads = exchange([ffn, up], rest_back, (grad_a, grad_b))

        def make_rest(sums, grad_y, grad_q, grad_k, grad_v):
            got = [swap(sums, *to) for to in relatives(order_a[-2:])]
            parts = wgrad(
                me,
                [grad_y, att_2[0], o, o_2, grad_q, att_2[1], h, h_2, grad_k, att_2[2], grad_v, att_2[3]],
                [(0, 1), (2, 3), (4, 5), (6, 7), (8, 9), (10, 11)],
                [
                    (0, 1, "wide", [(order_a, 0, block, 0)]),
                    (2, 3, "wide", [(order_a, 0, block, att_rows)]),
                    (4, 3, "wide", [(order_b, 0, block, 2 * att_rows)]),
                    (5, 3, "wide", [(order_b, 0, block, 3 * att_rows)]),
                ],
                4 * att_rows,
                wide,
                narrow,
                12,
            )
            got, parts = lax.optimization_barrier((got, parts))
            return parts, (sums + got[0]) + (got[1] + got[2])

        parts, sums = exchange([ffn, up], make_rest, (sums, *grads))
        att = Chunk(*parts, 2 * att_rows, orders, [("turn", i * att_rows, block, cols) for i in range(4)], True)
        for n in range(3):
            live = [f for f in (att, up, ffn) if not f.done]
            sums = exchange(live, lambda value: doubled(value, order_a[n : n + 1]), (sums,))
        exchange([att], lambda: (), ())
        grad_down, grad_gate = ffn.result
        grad_up, grad_proj = up.result
        grad_out, grad_query, grad_key, grad_value = att.result
    gain_total, bucket_total = sums[:3], sums[4 : 4 + heads, :buckets]
    mean_loss = sums[3, :1] / (qrows * QSEGS * wide * narrow)
    return (
        mean_loss,
        vectors[:QSEGS],
        vectors[QSEGS : QSEGS + PSEGS],
        grad_x[:qlen].reshape(1, qlen, feat),
        grad_x[qlen:].reshape(1, plen, feat),
        gain_total,
        bucket_total.T,
        grad_query,
        grad_key,
        grad_value,
        grad_out,
        grad_gate,
        grad_up,
        grad_down,
        grad_proj,
    )


def solution(mesh):
    rows3, rows2, rows1 = P(AXES, None, None), P(AXES, None), P(AXES)
    return jax.shard_map(
        functools.partial(local, mesh.shape["wide"], mesh.shape["narrow"]),
        mesh=mesh,
        in_specs=(rows3, rows2, rows3, rows2, rows1) + (P(),) * 12,
        out_specs=(P(), rows2, rows2, rows3, rows3, P(), P()) + (P("narrow", "wide"),) * 8,
        check_vma=False,
    )
```

```python
import functools

import jax
import jax.numpy as jnp
from jax import lax
from jax.experimental import pallas as pl
from jax.experimental.pallas import tpu as pltpu
from jax.sharding import PartitionSpec as P

LAYERS = 2
QSEGS = 3
PSEGS = 4
HDIM = 64
PACK = 8

HIGHEST = lax.Precision.HIGHEST
EPSILON = 1e-06
MASKED = -1000000000.0
BF = jnp.bfloat16
F32 = jnp.float32
AXES = ("wide", "narrow")


def low(a):
    return a.astype(BF)


def product(a, b):
    return jnp.dot(a, b, preferred_element_type=F32)


def dot_tn(a, b, precision=None):
    return lax.dot_general(
        a, b, (((0,), (0,)), ((), ())), preferred_element_type=F32, precision=precision
    )


def dot_nt(a, b, precision=None):
    return lax.dot_general(
        a, b, (((1,), (1,)), ((), ())), preferred_element_type=F32, precision=precision
    )


def whole():
    return pl.BlockSpec(memory_space=pltpu.VMEM)


def bias_kernel(qlen, plen, lookup_ref, grid_ref, qseg_ref, pseg_ref, pbias_ref, qbias_ref, wide_s, short_s):
    heads, buckets = grid_ref.shape
    width = 2 * plen
    wide_s[...] = jnp.full((1, width), -1, jnp.int32)
    wide_s[:, : lookup_ref.shape[1]] = lookup_ref[...]
    onehot = (
        lax.broadcasted_iota(jnp.int32, (buckets, width), 0)
        == jnp.broadcast_to(wide_s[...], (buckets, width))
    ).astype(F32)
    table = jnp.dot(grid_ref[...], onehot, precision=HIGHEST, preferred_element_type=F32)
    pcol = jnp.transpose(jnp.broadcast_to(pseg_ref[...], (plen, plen)))
    psame = pcol == jnp.broadcast_to(pseg_ref[...], (plen, plen))
    short_s[...] = jnp.full((1, 128), -1, jnp.int32)
    short_s[:, :qlen] = qseg_ref[...]
    qcol = jnp.transpose(jnp.broadcast_to(short_s[...], (128, 128)))
    qsame = (qcol == jnp.broadcast_to(short_s[...], (128, 128)))[:qlen, :qlen]
    for head in range(heads):
        rows = jnp.broadcast_to(table[head : head + 1, :], (plen, width))
        rolled = pltpu.roll(rows, width - (plen - 1), 1, stride=1, stride_axis=0)
        block = rolled[:, :plen]
        pbias_ref[head] = jnp.where(psame, block, MASKED)
        qbias_ref[head] = jnp.where(qsame, block[:qlen, :qlen], MASKED)


def half_mask(lanes, side):
    return (lax.broadcasted_iota(jnp.int32, (1, lanes), 1) // HDIM) == side


def attend_kernel(qlen, q_ref, k_ref, v_ref, pbias_ref, qbias_ref, o_ref, pp_ref, pq_ref):
    pairs = q_ref.shape[1] // 128
    spans = ((0, qlen, qbias_ref, pq_ref), (qlen, q_ref.shape[0] - qlen, pbias_ref, pp_ref))

    def pair(i, carry):
        lanes = pl.ds(pl.multiple_of(i * 128, 128), 128)
        for start, length, bias_ref, keep_ref in spans:
            rows = pl.ds(start, length)
            q2, k2, v2 = q_ref[rows, lanes], k_ref[rows, lanes], v_ref[rows, lanes]
            total = None
            for side in range(2):
                mine = half_mask(128, side)
                zero = jnp.zeros_like(k2)
                s = dot_nt(q2, jnp.where(mine, k2, zero)) + bias_ref[2 * i + side]
                top = jnp.max(s, axis=-1, keepdims=True)
                e = jnp.exp(s - top)
                p = low(e * (1.0 / jnp.sum(e, axis=-1, keepdims=True)))
                keep_ref[2 * i + side] = p
                part = product(p, jnp.where(mine, v2, zero))
                total = part if total is None else total + part
            o_ref[rows, lanes] = low(total)
        return carry

    lax.fori_loop(0, pairs, pair, 0, unroll=2)


def attend_back_kernel(
    qlen, q_ref, k_ref, v_ref, o_ref, go_ref, pp_ref, pq_ref, acc_ref, gq_ref, gk_ref, gv_ref, ds_ref
):
    pairs = q_ref.shape[1] // 128
    plen = q_ref.shape[0] - qlen

    def pair(i, carry):
        lanes = pl.ds(pl.multiple_of(i * 128, 128), 128)
        for start, length, keep_ref in ((qlen, plen, pp_ref), (0, qlen, pq_ref)):
            rows = pl.ds(start, length)
            q2, k2, v2 = q_ref[rows, lanes], k_ref[rows, lanes], v_ref[rows, lanes]
            o2, go2 = o_ref[rows, lanes], go_ref[rows, lanes]
            prod = o2.astype(F32) * go2.astype(F32)
            gq, gk, gv = None, None, None
            for side in range(2):
                mine = half_mask(128, side)
                zero = jnp.zeros_like(k2)
                p = keep_ref[2 * i + side]
                gp = dot_nt(go2, jnp.where(mine, v2, zero))
                delta = jnp.sum(jnp.where(mine, prod, 0.0), axis=-1, keepdims=True)
                ds = p.astype(F32) * (gp - delta)
                if start == qlen:
                    if acc_ref is None:
                        ds_ref[2 * i + side] = ds
                    else:
                        ds_ref[2 * i + side] = ds + acc_ref[2 * i + side]
                else:
                    ds_ref[2 * i + side, :length, :length] += ds
                dsl = low(ds)
                a = product(dsl, jnp.where(mine, k2, zero))
                b = dot_tn(dsl, jnp.where(mine, q2, zero))
                c = dot_tn(p, jnp.where(mine, go2, zero))
                gq = a if gq is None else gq + a
                gk = b if gk is None else gk + b
                gv = c if gv is None else gv + c
            gq_ref[rows, lanes] = low(gq)
            gk_ref[rows, lanes] = low(gk)
            gv_ref[rows, lanes] = low(gv)
        return carry

    lax.fori_loop(0, pairs, pair, 0, unroll=2)


def small_kernel(
    buckets, ds_ref, lookup_ref, in_ref, mid_ref, final_ref, loss_ref, out_ref, diag_ref, wide_s
):
    heads, plen, _ = ds_ref.shape
    out_ref[...] = jnp.zeros_like(out_ref)
    out_ref[0:1, :] = in_ref[...]
    out_ref[1:2, :] = mid_ref[...]
    out_ref[2:3, :] = final_ref[...]
    out_ref[3:4, :128] = loss_ref[...]
    width = 2 * plen
    wide_s[...] = jnp.full((1, width), -1, jnp.int32)
    wide_s[:, : lookup_ref.shape[1]] = lookup_ref[...]
    for head in range(heads):
        block = ds_ref[head]
        wide_block = jnp.concatenate([block, jnp.zeros_like(block)], axis=1)
        rows = plen
        while rows > 8:
            rows //= 2
            wide_block = wide_block[:rows] + pltpu.roll(wide_block[rows:], width - rows, 1)
        at = lax.broadcasted_iota(jnp.int32, (8, width), 0)
        for bit in (4, 2, 1):
            moved = pltpu.roll(wide_block, width - bit, 1)
            wide_block = jnp.where((at & bit) != 0, moved, wide_block)
        rolled = pltpu.roll(wide_block, plen - 1, 1)
        diag_ref[head : head + 1, :] = jnp.sum(rolled, axis=0, keepdims=True)
    onehot = (
        lax.broadcasted_iota(jnp.int32, (buckets, width), 0)
        == jnp.broadcast_to(wide_s[...], (buckets, width))
    ).astype(F32)
    out_ref[4 : 4 + heads, :buckets] = dot_nt(diag_ref[...], onehot, HIGHEST)


def segment_table(seg_ref, first):
    rows, length = PACK, seg_ref.shape[1]
    slot = lax.broadcasted_iota(jnp.int32, (rows, length), 0)
    return (slot == jnp.broadcast_to(seg_ref[...], (rows, length)) + first).astype(F32)


def pool_kernel(
    x_ref, gain_ref, qseg_ref, pseg_ref, label_ref, wp_ref, packed_ref, vec_ref, e_ref, pooled_ref
):
    qlen = qseg_ref.shape[1]
    x = x_ref[...]
    z = x * lax.rsqrt(jnp.mean(x * x, axis=-1, keepdims=True) + EPSILON) * gain_ref[...]
    qt, pt = segment_table(qseg_ref, 0), segment_table(pseg_ref, QSEGS)
    sizes = jnp.sum(qt, axis=1, keepdims=True) + jnp.sum(pt, axis=1, keepdims=True)
    sums = jnp.dot(qt, z[:qlen], precision=HIGHEST, preferred_element_type=F32) + jnp.dot(
        pt, z[qlen:], precision=HIGHEST, preferred_element_type=F32
    )
    pooled = low(sums / jnp.maximum(sizes, 1.0))
    pooled_ref[...] = pooled
    e = product(pooled, wp_ref[...])
    e_ref[...] = e
    vec = e * lax.rsqrt(jnp.sum(e * e, axis=-1, keepdims=True) + EPSILON)
    vec_ref[...] = vec
    at = lax.broadcasted_iota(jnp.int32, vec.shape, 1)
    row = lax.broadcasted_iota(jnp.int32, vec.shape, 0)
    code = jnp.zeros(vec.shape, F32)
    for i in range(QSEGS):
        label = label_ref[i]
        high = lax.shift_right_logical(label, 5).astype(F32)
        rest = (label & 31).astype(F32)
        code = jnp.where(at == i, high, jnp.where(at == QSEGS + i, rest, code))
    packed_ref[...] = low(jnp.where(row == PACK - 1, code, vec))


SLOPE = 0.7978845608028654
CUBE = 0.044715
SAVED = ("h", "q", "k", "v", "pp", "pq", "o", "x_mid", "normed", "da", "db", "u")


def unit_scale(x):
    return lax.rsqrt(jnp.mean(x * x, axis=-1, keepdims=True) + EPSILON)


def gated_parts(a, b):
    square = a * a
    th = jnp.tanh(a * (SLOPE + (SLOPE * CUBE) * square))
    half = 0.5 + 0.5 * th
    value = a * half
    slope = half + (0.5 * a) * (1.0 - th * th) * (SLOPE + (3.0 * SLOPE * CUBE) * square)
    return low(value * b), low(b * slope), low(value)


def forward_kernel(qlen, plen, n_tiles, *refs):
    (qx_ref, px_ref, lookup_ref, grid_ref, qseg_ref, pseg_ref, gains_ref, label_ref), refs = refs[:8], refs[8:]
    hbm, refs = refs[:8], refs[8:]
    packed_ref, vec_ref, e_ref, pooled_ref, x_mid_out, x_out = refs[:6]
    refs = refs[6:]
    outs = [dict(zip(SAVED, refs[n * len(SAVED) : (n + 1) * len(SAVED)])) for n in range(LAYERS)]
    refs = refs[LAYERS * len(SAVED) :]
    held, refs = refs[:8], refs[8:]
    keep, refs = dict(zip(SAVED, refs[: len(SAVED)])), refs[len(SAVED) :]
    x_s, pbias_s, qbias_s, wide_s, short_s, in_sem, out_sem, x_sem = refs
    wq_s, wk_s, wv_s, wo_s, wg_s, wu_s, wd_s, wp_s = held
    fetch = [pltpu.make_async_copy(a, b, in_sem.at[i]) for i, (a, b) in enumerate(zip(hbm, held))]
    for c in fetch:
        c.start()
    x_s[0, :qlen] = qx_ref[...].astype(F32)
    x_s[0, qlen:] = px_ref[...].astype(F32)
    bias_kernel(qlen, plen, lookup_ref, grid_ref, qseg_ref, pseg_ref, pbias_s, qbias_s, wide_s, short_s)

    def write(n, name):
        i = n * len(SAVED) + SAVED.index(name)
        return pltpu.make_async_copy(keep[name].at[n], outs[n][name], out_sem.at[i])

    def send(layer, *names):
        for n in range(LAYERS):

            @pl.when(layer == n)
            def _():
                for name in names:
                    write(n, name).start()

    def arrive(layer, *ids):
        @pl.when(layer == 0)
        def _():
            for i in ids:
                fetch[i].wait()

    def layer_step(layer, carry):
        x = x_s[layer]
        h = low(x * unit_scale(x) * gains_ref[0:1, :])
        keep["h"][layer] = h
        for i, (name, w) in enumerate((("q", wq_s), ("k", wk_s), ("v", wv_s))):
            arrive(layer, i)
            keep[name][layer] = low(product(h, w[...]))
        send(layer, "h", "q", "k", "v")
        at = {name: keep[name].at[layer] for name in SAVED}
        attend_kernel(qlen, at["q"], at["k"], at["v"], pbias_s, qbias_s, at["o"], at["pp"], at["pq"])
        send(layer, "o", "pp", "pq")
        arrive(layer, 3)
        x_mid = x_s[layer] + product(at["o"][...], wo_s[...])
        at["x_mid"][...] = x_mid
        normed = low(x_mid * unit_scale(x_mid) * gains_ref[1:2, :])
        at["normed"][...] = normed
        send(layer, "x_mid", "normed")
        arrive(layer, 4, 5)
        size = wg_s.shape[1] // n_tiles
        for t in range(n_tiles):
            lanes = slice(t * size, (t + 1) * size)
            a = product(normed, wg_s[:, lanes])
            b = product(normed, wu_s[:, lanes])
            u, da, db = gated_parts(a, b)
            at["u"][:, lanes] = u
            at["da"][:, lanes] = da
            at["db"][:, lanes] = db
        send(layer, "u", "da", "db")
        arrive(layer, 6)
        x_s[layer + 1] = at["x_mid"][...] + product(at["u"][...], wd_s[...])
        return carry

    lax.fori_loop(0, LAYERS, layer_step, 0)
    inner = pltpu.make_async_copy(x_s.at[1], x_mid_out, x_sem.at[0])
    outer = pltpu.make_async_copy(x_s.at[LAYERS], x_out, x_sem.at[1])
    inner.start()
    outer.start()
    fetch[7].wait()
    pool_kernel(
        x_s.at[LAYERS], gains_ref.at[2:3], qseg_ref, pseg_ref, label_ref, wp_s, packed_ref, vec_ref, e_ref, pooled_ref
    )
    for n in range(LAYERS):
        for name in SAVED:
            write(n, name).wait()
    inner.wait()
    outer.wait()


def saved_shapes(total, qlen, plen, feat, hidden, heads):
    tok, ff = ((total, feat), BF), ((total, hidden), BF)
    kinds = dict(h=tok, q=tok, k=tok, v=tok, o=tok, normed=tok, da=ff, db=ff, u=ff)
    kinds["pp"], kinds["pq"] = ((heads, plen, plen), BF), ((heads, qlen, qlen), BF)
    kinds["x_mid"] = ((total, feat), F32)
    return [kinds[name] for name in SAVED]


def forward(qx, px, lookup, grid, qseg, pseg, gains, labels, matrices):
    qlen, feat = qx.shape
    plen, heads, hidden = px.shape[0], grid.shape[0], matrices[4].shape[1]
    total = qlen + plen
    kinds = saved_shapes(total, qlen, plen, feat, hidden, heads)
    small = (PACK, feat)
    shapes = [(small, BF), (small, F32), (small, F32), (small, BF), ((total, feat), F32), ((total, feat), F32)]
    shapes += kinds * LAYERS
    anywhere = pl.BlockSpec(memory_space=pltpu.HBM)
    smem = pl.BlockSpec(memory_space=pltpu.SMEM)
    weights = sum(m.size for m in matrices)
    outs = pl.pallas_call(
        functools.partial(forward_kernel, qlen, plen, 4),
        out_shape=tuple(jax.ShapeDtypeStruct(*s) for s in shapes),
        in_specs=[whole()] * 7 + [smem] + [anywhere] * 8,
        out_specs=(whole(),) * 4 + (anywhere,) * (2 + LAYERS * len(SAVED)),
        scratch_shapes=[pltpu.VMEM(m.shape, BF) for m in matrices]
        + [pltpu.VMEM((LAYERS,) + shape, dtype) for shape, dtype in kinds]
        + [
            pltpu.VMEM((LAYERS + 1, total, feat), F32),
            pltpu.VMEM((heads, plen, plen), F32),
            pltpu.VMEM((heads, qlen, qlen), F32),
            pltpu.VMEM((1, 2 * plen), jnp.int32),
            pltpu.VMEM((1, 128), jnp.int32),
            pltpu.SemaphoreType.DMA((8,)),
            pltpu.SemaphoreType.DMA((LAYERS * len(SAVED),)),
            pltpu.SemaphoreType.DMA((2,)),
        ],
        name="forward",
        compiler_params=pltpu.CompilerParams(vmem_limit_bytes=56 << 20),
        cost_estimate=pl.CostEstimate(
            flops=2 * LAYERS * total * weights, bytes_accessed=2 * weights, transcendentals=LAYERS * total * hidden
        ),
    )(qx, px, lookup[None], grid, qseg, pseg, gains, labels, *matrices)
    saved = [dict(zip(SAVED, outs[6 + n * len(SAVED) : 6 + (n + 1) * len(SAVED)])) for n in range(LAYERS)]
    return outs[:6], saved


def loss_kernel(
    narrow, stages, me_ref, sharp_ref, here_ref, there_ref, e_ref, x_ref, gain_ref,
    qseg_ref, pseg_ref, wp_ref, gx_ref, ggain_ref, loss_ref, ge_ref, flat_s,
):
    half = here_ref.shape[0]
    flat_s[:half, :] = here_ref[...]
    flat_s[half:, :] = there_ref[...]
    size = 2 * half
    tile = min(size, 256)
    sharp = sharp_ref[0]
    lane = lax.broadcasted_iota(jnp.int32, (1, size), 1)
    block, slot = lax.shift_right_logical(lane, 3), lane & (PACK - 1)
    dw, dn = jnp.zeros_like(block), jnp.zeros_like(block)
    for k, (axis, bit) in enumerate(stages):
        on = (lax.shift_right_logical(block, k) & 1) * bit
        dw, dn = (dw + on, dn) if axis == "wide" else (dw, dn + on)
    device = (dw ^ me_ref[0]) * narrow + (dn ^ me_ref[1])
    is_passage = (slot >= QSEGS) & (slot < QSEGS + PSEGS)
    document = jnp.where(is_passage, device * PSEGS + slot - QSEGS, -2)
    row = lax.broadcasted_iota(jnp.int32, (tile, 1), 0)
    row_slot = row & (PACK - 1)
    is_query = row_slot < QSEGS
    across = lax.broadcasted_iota(jnp.int32, (tile, tile), 1)
    source = low((across == row - row_slot + PACK - 1).astype(F32))
    place = lax.broadcasted_iota(jnp.int32, (tile, 128), 1)
    weigh = jnp.where(place == row_slot, 32.0, 0.0) + jnp.where(place == row_slot + QSEGS, 1.0, 0.0)
    mine = lax.broadcasted_iota(jnp.int32, (1, 128), 1) < PACK
    grad = None
    for t in range(size // tile):
        rows = flat_s[t * tile : (t + 1) * tile, :]
        match = dot_nt(rows, flat_s[...]) / sharp
        match = jnp.where(is_passage, match, MASKED)
        label = jnp.sum(product(source, rows[:, :128]) * weigh, axis=1, keepdims=True)
        hit = (label.astype(jnp.int32) == document) & is_query
        top = jnp.max(match, axis=1, keepdims=True)
        ex = jnp.exp(match - top)
        line = jnp.sum(ex, axis=1, keepdims=True)
        g = (ex / line - hit.astype(F32)) / sharp
        g = low(jnp.where(is_query & is_passage, g, 0.0))
        back = dot_tn(jnp.where(mine, g[:, :128], jnp.zeros_like(g[:, :128])), rows)[:PACK]
        if t == 0:
            part = jnp.sum(jnp.where(hit, match, 0.0), axis=1, keepdims=True)
            part = jnp.where(is_query & (row < PACK), top + jnp.log(line) - part, 0.0)
            loss_ref[...] = jnp.broadcast_to(jnp.sum(part, axis=0, keepdims=True), loss_ref.shape)
            grad = product(g[:16], flat_s[...])[:PACK]
        grad = grad + back
    e = e_ref[...]
    scale = lax.rsqrt(jnp.sum(e * e, axis=-1, keepdims=True) + EPSILON)
    vec = e * scale
    ge = low((grad - vec * jnp.sum(vec * grad, axis=-1, keepdims=True)) * scale)
    ge_ref[...] = ge
    qt, pt = segment_table(qseg_ref, 0), segment_table(pseg_ref, QSEGS)
    sizes = jnp.sum(qt, axis=1, keepdims=True) + jnp.sum(pt, axis=1, keepdims=True)
    pooled = dot_nt(ge, wp_ref[...]) / jnp.maximum(sizes, 1.0)
    qlen = qseg_ref.shape[1]
    gain = gain_ref[...]
    total = None
    for table, start, count in ((qt, 0, qlen), (pt, qlen, pseg_ref.shape[1])):
        gz = dot_tn(table, pooled, HIGHEST)
        x = x_ref[start : start + count, :]
        r = lax.rsqrt(jnp.mean(x * x, axis=-1, keepdims=True) + EPSILON)
        unit = x * r
        scaled = gz * gain
        gx_ref[start : start + count, :] = r * (
            scaled - unit * jnp.mean(unit * scaled, axis=-1, keepdims=True)
        )
        part = jnp.sum(gz * unit, axis=0, keepdims=True)
        total = part if total is None else total + part
    ggain_ref[...] = total


PAIRED = ("grad_f", "ga", "grad_f1", "ga1")
BACK = ("grad_f", "ga", "gb", "gy", "gq", "gk", "gv", "ds", "grad_f1", "ga1", "gb1", "grad_x")


def through_norm(x, gain, grad):
    r = unit_scale(x)
    unit = x * r
    scaled = grad * gain
    back = r * (scaled - unit * jnp.mean(unit * scaled, axis=-1, keepdims=True))
    return back, jnp.sum(grad * unit, axis=0, keepdims=True)


def back_kernel(narrow, stages, qlen, n_tiles, n_held, names, jobs, *refs):
    me_ref, sharp_ref, here_ref, there_ref, e_ref, gains_ref, qseg_ref, pseg_ref = refs[:8]
    refs = refs[8:]
    n_fetch = n_held + (4 if jobs else 0)
    hbm, refs = refs[:n_fetch], refs[n_fetch:]
    ggain_ref, loss_ref, ge_ref, gmid_ref, gin_ref = refs[:5]
    outs, refs = dict(zip(names, refs[5 : 5 + len(names)])), refs[5 + len(names) :]
    if jobs:
        (keep_ref, send_ref), refs = refs[:2], refs[2:]
    held, refs = list(refs[: n_held - 4]), refs[n_held - 4 :]
    singles = [n for n in BACK if n not in PAIRED and n != "grad_x"]
    keep, refs = dict(zip(singles, refs[: len(singles)])), refs[len(singles) :]
    gf_s, ga_s, wide_s, row_s, flat_s, gx_s, go_s, in_sem, out_sem = refs[:9]
    total = gx_s.shape[0]
    keep["grad_x"] = gx_s
    halves = [buf.at[i * total : (i + 1) * total] for buf in (wide_s, row_s) for i in range(2)]
    held = held[:3] + halves[:2] + held[3:7] + halves[2:] + held[7:] + halves
    for i, (name, buf) in enumerate((("grad_f1", gf_s), ("ga1", ga_s), ("grad_f", gf_s), ("ga", ga_s))):
        keep[name] = buf.at[i // 2 * total : (i // 2 + 1) * total]
    fetch = [pltpu.make_async_copy(a, b, in_sem.at[i]) for i, (a, b) in enumerate(zip(hbm, held))]
    for c in fetch[:21]:
        c.start()
    (x2_s, wp_s, wd_s, da_s, db_s, wg_s, wu_s, xm_s, wo_s, v_s, o_s, pp_s, k_s, q_s, pq_s) = held[:15]
    wq_s, wk_s, wv_s, x_s, da1_s, db1_s = held[15:21]

    def write(name):
        return pltpu.make_async_copy(keep[name], outs[name], out_sem.at[names.index(name)])

    def send(*ready):
        for name in ready:
            if name in outs:
                write(name).start()

    fetch[0].wait()
    fetch[1].wait()
    loss_kernel(
        narrow, stages, me_ref, sharp_ref, here_ref, there_ref, e_ref, x2_s, gains_ref.at[2:3],
        qseg_ref, pseg_ref, wp_s, gx_s, ggain_ref, loss_ref, ge_ref, flat_s,
    )

    def gated_back(x_ref, da, db, made):
        grad_f = low(x_ref[...])
        keep[made[0]][...] = grad_f
        size = da.shape[1] // n_tiles
        for t in range(n_tiles):
            lanes = slice(t * size, (t + 1) * size)
            gu = dot_nt(grad_f, wd_s[lanes, :])
            keep[made[1]][:, lanes] = low(gu * da[:, lanes].astype(F32))
            keep[made[2]][:, lanes] = low(gu * db[:, lanes].astype(F32))
        send(*made)

    for i in (2, 3, 4):
        fetch[i].wait()
    gated_back(gx_s, da_s, db_s, BACK[:3])
    for c in fetch[21:23]:
        c.start()
    for i in (5, 6, 7):
        fetch[i].wait()
    grad = dot_nt(keep["ga"][...], wg_s[...]) + dot_nt(keep["gb"][...], wu_s[...])
    back, gmid_ref[...] = through_norm(xm_s[...], gains_ref[1:2, :], grad)
    grad_mid = gx_s[...] + back
    gx_s[...] = grad_mid
    gy = low(grad_mid)
    keep["gy"][...] = gy
    send("gy")
    fetch[8].wait()
    go_s[...] = low(dot_nt(gy, wo_s[...]))
    for i in range(9, 15):
        fetch[i].wait()
    attend_back_kernel(
        qlen, q_s, k_s, v_s, o_s, go_s, pp_s, pq_s, None, keep["gq"], keep["gk"], keep["gv"], keep["ds"]
    )
    send("gq", "gk", "gv", "ds")
    for c in fetch[23:]:
        c.start()
    for i in range(15, 19):
        fetch[i].wait()
    grad = dot_nt(keep["gq"][...], wq_s[...]) + dot_nt(keep["gk"][...], wk_s[...])
    grad = grad + dot_nt(keep["gv"][...], wv_s[...])
    back, gin_ref[...] = through_norm(x_s[...], gains_ref[0:1, :], grad)
    gx_s[...] = gx_s[...] + back
    send("grad_x")
    fetch[19].wait()
    fetch[20].wait()
    gated_back(gx_s, da1_s, db1_s, BACK[8:11])
    if jobs:
        for i in range(21, 25):
            fetch[i].wait()
        weight_products(jobs, (gf_s, wide_s, row_s, ga_s), lambda g: None, me_ref, keep_ref, send_ref, refs[9])
    for name in names:
        write(name).wait()


def loss_and_back(me, narrow, stages, sharp, here, there, e, gains, qseg, pseg, x_last, x_in, first, second, matrices, wide, jobs, total_rows):
    wq, wk, wv, wo, wg, wu, wd, wp = matrices
    total, feat = x_last.shape
    qlen, plen = qseg.shape[1], pseg.shape[1]
    heads, hidden = second["pp"].shape[0], wd.shape[0]
    size = 2 * here.shape[0]
    t = second
    fetched = [x_last, wp, wd, t["da"], t["db"], wg, wu, t["x_mid"], wo, t["v"], t["o"], t["pp"], t["k"], t["q"], t["pq"]]
    fetched += [wq, wk, wv, x_in, first["da"], first["db"]]
    tok, ff = ((total, feat), BF), ((total, hidden), BF)
    kinds = [tok, ff, ff, tok, tok, tok, tok, ((heads, plen, plen), F32), tok, ff, ff, ((total, feat), F32)]
    kinds = dict(zip(BACK, kinds))
    names = [n for n in BACK if not (jobs and n in ("grad_f", "ga", "grad_f1"))]
    held = [pltpu.VMEM(a.shape, a.dtype) for i, a in enumerate(fetched) if i not in (3, 4, 9, 10)]
    n_held = len(fetched)
    blocks, late = [], []
    if jobs:
        fetched += [first["u"], second["u"], first["normed"], second["normed"]]
        blocks = [((wide * narrow // 2, total_rows, 128), BF)] * 2
        late = [pltpu.VMEM((384, 2 * total), BF)]
        widths = (feat, hidden, feat, hidden)
        jobs = with_blocks(jobs, lambda g: widths[g], wide, narrow)
    small = [((1, feat), F32), ((1, 128), F32), ((PACK, feat), BF), ((1, feat), F32), ((1, feat), F32)]
    anywhere = pl.BlockSpec(memory_space=pltpu.HBM)
    smem = pl.BlockSpec(memory_space=pltpu.SMEM)
    weights = sum(m.size for m in matrices)
    outs = pl.pallas_call(
        functools.partial(back_kernel, narrow, stages, qlen, 4, n_held, names, jobs),
        out_shape=tuple(jax.ShapeDtypeStruct(*s) for s in small + [kinds[n] for n in names] + blocks),
        in_specs=[smem, smem] + [whole()] * 6 + [anywhere] * len(fetched),
        out_specs=(whole(),) * 5 + (anywhere,) * len(names) + (whole(),) * len(blocks),
        scratch_shapes=held
        + [pltpu.VMEM(*kinds[n]) for n in BACK if n not in PAIRED and n != "grad_x"]
        + [
            pltpu.VMEM((2 * total, feat), BF),
            pltpu.VMEM((2 * total, hidden), BF),
            pltpu.VMEM((2 * total, hidden), BF),
            pltpu.VMEM((2 * total, feat), BF),
            pltpu.VMEM((size, feat), BF),
            pltpu.VMEM((total, feat), F32),
            pltpu.VMEM((total, feat), BF),
            pltpu.SemaphoreType.DMA((len(fetched),)),
            pltpu.SemaphoreType.DMA((len(names),)),
        ]
        + late,
        name="loss_and_back",
        compiler_params=pltpu.CompilerParams(vmem_limit_bytes=(54 if jobs else 56) << 20),
        cost_estimate=pl.CostEstimate(
            flops=3 * total * weights, bytes_accessed=2 * weights, transcendentals=0
        ),
    )(me, sharp, here, there, e, gains, qseg, pseg, *fetched)
    return outs[:5], dict(zip(names, outs[5:])), outs[5 + len(names) :]


REST = ("gy", "gq", "gk", "gv", "grad_x")


def rest_kernel(qlen, buckets, n_held, *refs):
    gains_ref, lookup_ref, gin_ref, gmid_ref, gfin_ref, loss_ref = refs[:6]
    refs = refs[6:]
    hbm, refs = refs[:n_held], refs[n_held:]
    sums_ref, outs, refs = refs[0], dict(zip(REST, refs[1:6])), refs[6:]
    held, refs = refs[:n_held], refs[n_held:]
    keep, refs = dict(zip(REST, refs[:5])), refs[5:]
    go_s, row_s, diag_s, wide_s, in_sem, out_sem = refs
    (ga_s, wg_s, gb_s, wu_s, xm_s, gx_s, wo_s, q_s, k_s, v_s, o_s, pp_s, pq_s, ds_s) = held[:14]
    wq_s, wk_s, wv_s, qx_s, px_s = held[14:]
    fetch = [pltpu.make_async_copy(a, b, in_sem.at[i]) for i, (a, b) in enumerate(zip(hbm, held))]
    for c in fetch:
        c.start()

    def arrive(first, last):
        for i in range(first, last):
            fetch[i].wait()

    def write(name):
        return pltpu.make_async_copy(keep[name], outs[name], out_sem.at[REST.index(name)])

    arrive(0, 2)
    grad = dot_nt(ga_s[...], wg_s[...])
    arrive(2, 6)
    grad = grad + dot_nt(gb_s[...], wu_s[...])
    back, part = through_norm(xm_s[...], gains_ref[1:2, :], grad)
    row_s[1:2, :] = gmid_ref[...] + part
    grad_mid = gx_s[...] + back
    gx_s[...] = grad_mid
    gy = low(grad_mid)
    keep["gy"][...] = gy
    write("gy").start()
    arrive(6, 7)
    go_s[...] = low(dot_nt(gy, wo_s[...]))
    arrive(7, 14)
    attend_back_kernel(
        qlen, q_s, k_s, v_s, o_s, go_s, pp_s, pq_s, ds_s, keep["gq"], keep["gk"], keep["gv"], ds_s
    )
    for name in REST[1:4]:
        write(name).start()
    arrive(14, 19)
    grad = dot_nt(keep["gq"][...], wq_s[...]) + dot_nt(keep["gk"][...], wk_s[...])
    grad = grad + dot_nt(keep["gv"][...], wv_s[...])
    x = jnp.concatenate([qx_s[...], px_s[...]], axis=0).astype(F32)
    back, part = through_norm(x, gains_ref[0:1, :], grad)
    row_s[0:1, :] = gin_ref[...] + part
    keep["grad_x"][...] = gx_s[...] + back
    write("grad_x").start()
    small_kernel(
        buckets, ds_s, lookup_ref, row_s.at[0:1], row_s.at[1:2], gfin_ref, loss_ref, sums_ref, diag_s, wide_s
    )
    for name in REST:
        write(name).wait()


def rest_back(gains, lookup, buckets, small, ga, gb, gx, acc, first, matrices, qx, px):
    wq, wk, wv, wo, wg, wu = matrices[:6]
    total, feat = gx.shape
    heads, plen, _ = acc.shape
    qlen = qx.shape[0]
    t = first
    fetched = [ga, wg, gb, wu, t["x_mid"], gx, wo, t["q"], t["k"], t["v"], t["o"], t["pp"], t["pq"], acc]
    fetched += [wq, wk, wv, qx, px]
    kinds = [((total, feat), BF)] * 4 + [((total, feat), F32)]
    anywhere = pl.BlockSpec(memory_space=pltpu.HBM)
    weights = sum(m.size for m in matrices[:6])
    outs = pl.pallas_call(
        functools.partial(rest_kernel, qlen, buckets, len(fetched)),
        out_shape=tuple(jax.ShapeDtypeStruct(*k) for k in [((4 + heads, feat), F32)] + kinds),
        in_specs=[whole()] * 6 + [anywhere] * len(fetched),
        out_specs=(whole(),) + (anywhere,) * len(kinds),
        scratch_shapes=[pltpu.VMEM(a.shape, a.dtype) for a in fetched]
        + [pltpu.VMEM(*k) for k in kinds]
        + [
            pltpu.VMEM((total, feat), BF),
            pltpu.VMEM((8, feat), F32),
            pltpu.VMEM((heads, 2 * plen), F32),
            pltpu.VMEM((1, 2 * plen), jnp.int32),
            pltpu.SemaphoreType.DMA((len(fetched),)),
            pltpu.SemaphoreType.DMA((len(kinds),)),
        ],
        name="rest_back",
        compiler_params=pltpu.CompilerParams(vmem_limit_bytes=50 << 20),
        cost_estimate=pl.CostEstimate(
            flops=3 * total * weights, bytes_accessed=2 * weights, transcendentals=0
        ),
    )(gains, lookup[None], *small, *fetched)
    return outs


def join_kernel(*refs):
    ins, out_ref = refs[:-1], refs[-1]
    rows = ins[0].shape[0]
    for i, ref in enumerate(ins):
        out_ref[i * rows : (i + 1) * rows, :] = ref[...]


def join(*parts):
    a = parts[0]
    return pl.pallas_call(
        join_kernel,
        out_shape=jax.ShapeDtypeStruct((len(parts) * a.shape[0], a.shape[1]), a.dtype),
        in_specs=[whole()] * len(parts),
        out_specs=whole(),
        name="join",
        compiler_params=pltpu.CompilerParams(vmem_limit_bytes=4 << 20),
    )(*parts)


def stage_orders(wide, narrow):
    wbits = [1 << i for i in range(wide.bit_length() - 1)]
    nbits = [1 << i for i in range(narrow.bit_length() - 1)]
    w = lambda bits: [("wide", b) for b in bits]
    n = [("narrow", b) for b in nbits]
    tail = w(wbits[2:])
    return (w(wbits[:1]) + w(wbits[1:2]) + n + tail, w(wbits[:1]) + n + w(wbits[1:2]) + tail)


def place_of(order, dw, dn):
    place = 0
    for axis, bit in order:
        own = dw if axis == "wide" else dn
        place = place * 2 + (own // bit) % 2
    return place


def traced_place(order, dw, dn):
    place = 0
    for axis, bit in order:
        own = dw if axis == "wide" else dn
        place = place * 2 + (lax.shift_right_logical(own, bit.bit_length() - 1) & 1)
    return place


def weight_products(jobs, held, arrive, me_ref, keep_ref, send_ref, turned_s):
    me_w, me_n = me_ref[0], me_ref[1]
    half = keep_ref.shape[0]

    def store(acc, job, w_first, n_first):
        row_axis, block_rows, block_lanes, targets = job[2:]
        blocks = [
            (bi, bj)
            for bi in range(acc.shape[0] // block_rows)
            for bj in range(acc.shape[1] // block_lanes)
        ]
        bases = [traced_place(t[0], w_first ^ me_w, n_first ^ me_n) for t in targets]
        for core in range(2):

            @pl.when((me_w & 1) == core)
            def _():
                for bi, bj in blocks:
                    w, n = (bi, bj) if row_axis == "wide" else (bj, bi)
                    out_ref = keep_ref if (w & 1) == core else send_ref
                    for (order, first, count, offset), base in zip(targets, bases):
                        at = (base ^ place_of(order, w, n)) & (half - 1)
                        for k in range(block_lanes // 128):
                            lane = bj * block_lanes + k * 128
                            row = bi * block_rows + first
                            out_ref[at, offset + k * count : offset + (k + 1) * count, :] = acc[
                                row : row + count, lane : lane + 128
                            ]

    for job in jobs:
        rg, lg, row_axis, block_rows, block_lanes, targets = job
        arrive(rg)
        arrive(lg)
        row_s, lane_s = held[rg], held[lg]
        depth, rows, lanes = row_s.shape[0], row_s.shape[1], lane_s.shape[1]
        tile_rows = 384
        tile_lanes = block_lanes
        while tile_lanes < 512 and lanes % (2 * tile_lanes) == 0:
            tile_lanes *= 2
        per_row, per_lane = tile_rows // block_rows, tile_lanes // block_lanes

        def row_step(rt, carry):
            mine = row_s[:, pl.ds(pl.multiple_of(rt * tile_rows, 128), tile_rows)]
            if depth > 16:
                turned_s[...] = mine.T

            def lane_step(lt, inner):
                part = lane_s[:, pl.ds(pl.multiple_of(lt * tile_lanes, 128), tile_lanes)]
                acc = product(turned_s[...], part) if depth > 16 else dot_tn(mine, part)
                if row_axis == "wide":
                    store(low(acc), job, rt * per_row, lt * per_lane)
                else:
                    store(low(acc), job, lt * per_lane, rt * per_row)
                return inner

            if lanes == tile_lanes:
                return lane_step(0, carry)
            return lax.fori_loop(0, lanes // tile_lanes, lane_step, carry)

        lax.fori_loop(0, rows // tile_rows, row_step, 0)


def wgrad_kernel(jobs, groups, n_ops, me_ref, *refs):
    ops, (keep_ref, send_ref) = refs[:n_ops], refs[n_ops : n_ops + 2]
    held = refs[n_ops + 2 : n_ops + 2 + len(groups)]
    turned_s, sems = refs[-2:]
    copies = []
    for ids, buf in zip(groups, held):
        first, own = 0, []
        for i in ids:
            count = ops[i].shape[0]
            sem = sems.at[sum(len(c) for c in copies) + len(own)]
            own.append(pltpu.make_async_copy(ops[i], buf.at[first : first + count], sem))
            first += count
        copies.append(own)
    for own in copies:
        for c in own:
            c.start()
    ready = set()

    def arrive(g):
        if g not in ready:
            for c in copies[g]:
                c.wait()
            ready.add(g)

    weight_products(jobs, held, arrive, me_ref, keep_ref, send_ref, turned_s)


def with_blocks(jobs, width, wide, narrow):
    full = []
    for rg, lg, row_axis, targets in jobs:
        split = (wide, narrow) if row_axis == "wide" else (narrow, wide)
        full.append((rg, lg, row_axis, width(rg) // split[0], width(lg) // split[1], targets))
    return full


def wgrad(me, ops, groups, jobs, total_rows, wide, narrow, vmem):
    half = wide * narrow // 2
    width = lambda g: ops[groups[g][0]].shape[1]
    depth = [sum(ops[i].shape[0] for i in g) for g in groups]
    full = with_blocks(jobs, width, wide, narrow)
    flops = sum(2 * depth[j[0]] * width(j[0]) * width(j[1]) for j in full)
    return pl.pallas_call(
        functools.partial(wgrad_kernel, full, groups, len(ops)),
        out_shape=(jax.ShapeDtypeStruct((half, total_rows, 128), BF),) * 2,
        in_specs=[pl.BlockSpec(memory_space=pltpu.SMEM)]
        + [pl.BlockSpec(memory_space=pltpu.HBM)] * len(ops),
        out_specs=(whole(),) * 2,
        scratch_shapes=[pltpu.VMEM((d, width(g)), BF) for g, d in enumerate(depth)]
        + [pltpu.VMEM((384, max(depth)), BF), pltpu.SemaphoreType.DMA((sum(map(len, groups)),))],
        name="wgrad",
        compiler_params=pltpu.CompilerParams(vmem_limit_bytes=vmem << 20),
        cost_estimate=pl.CostEstimate(flops=flops, bytes_accessed=flops // 256, transcendentals=0),
    )(me, *ops)


def swap(a, *stage):
    dw = sum(bit for axis, bit in stage if axis == "wide")
    dn = sum(bit for axis, bit in stage if axis == "narrow")
    wide, narrow = lax.axis_size("wide"), lax.axis_size("narrow")
    if not dn:
        return lax.ppermute(a, "wide", [(i, i ^ dw) for i in range(wide)])
    if not dw:
        return lax.ppermute(a, "narrow", [(i, i ^ dn) for i in range(narrow)])
    pairs = [(i * narrow + j, (i ^ dw) * narrow + (j ^ dn)) for i in range(wide) for j in range(narrow)]
    return lax.ppermute(a, AXES, pairs)


def relatives(stage):
    if len(stage) == 1:
        return [stage]
    return [(stage[1],), (stage[0],), tuple(stage)]


def grouped(order, direct):
    if not direct:
        return [(s,) for s in order]
    return [(s,) for s in order[:-2]] + [tuple(order[-2:])]


class Chunk:
    def __init__(self, keep, send, split, orders, finals, direct=False):
        self.rows, self.split, self.finals = keep.shape[1], split, finals
        self.orders = [grouped(order, direct) for order in orders]
        self.stage, self.parts = 0, [(keep, send)]
        self.done = False

    def spans(self, stage):
        if self.orders[0][stage] == self.orders[1][stage] and (
            stage == 0 or self.orders[0][stage:] == self.orders[1][stage:]
        ):
            return [(0, self.rows, self.orders[0])]
        return [(0, self.split, self.orders[0]), (self.split, self.rows, self.orders[1])]

    def start(self):
        return [
            [swap(a, *to) for a, to in zip(part[1:], relatives(order[self.stage]))]
            for part, (_, _, order) in zip(self.parts, self.spans(self.stage))
        ]


def doubled(value, stages):
    for stage in stages:
        value = value + swap(value, stage)
    return value


def advance(flows):
    operands, shapes, steps = [], [], []
    for f in flows:
        now = f.spans(f.stage)
        last = f.stage == len(f.orders[0]) - 1
        first_in, first_out = len(operands), len(shapes)
        for part, got in zip(f.parts, f.got):
            operands += [part[0]] + got
        half = f.parts[0][0].shape[0] // 2
        if last:
            for kind, offset, rows, lanes in f.finals:
                shapes.append(jax.ShapeDtypeStruct((rows, lanes), F32))
            steps.append(("final", first_in, first_out, f.finals, len(f.got[0])))
        else:
            later = f.spans(f.stage + 1)
            ways = 2 ** len(f.orders[0][f.stage + 1])
            for lo, hi, _ in later:
                shapes += [jax.ShapeDtypeStruct((2 * half // ways, hi - lo, 128), BF)] * ways
            steps.append(
                ("halve", first_in, first_out, [n[:2] for n in now], [n[:2] for n in later], ways)
            )

    def whole_sum(ins, i, count, pick):
        total = pick(ins[i]) + pick(ins[i + 1])
        return total if count == 1 else total + (pick(ins[i + 2]) + pick(ins[i + 3]))

    def body(*refs):
        ins, outs = refs[: len(operands)], refs[len(operands) :]
        for step in steps:
            kind, i, o = step[:3]
            if kind == "final":
                for n, (_, offset, rows, lanes) in enumerate(step[3]):
                    for k in range(lanes // 128):
                        span = pl.ds(offset + k * rows, rows)
                        value = whole_sum(ins, i, step[4], lambda ref: ref[0, span, :].astype(F32))
                        outs[o + n][:, k * 128 : (k + 1) * 128] = value
            else:
                ways = step[5]
                for p, (lo, hi) in enumerate(step[3]):
                    for q, (lo2, hi2) in enumerate(step[4]):
                        a, b = max(lo, lo2), min(hi, hi2)
                        if a >= b:
                            continue
                        keep_ref, got_ref = ins[i + 2 * p], ins[i + 2 * p + 1]
                        count = keep_ref.shape[0] // ways
                        for side in range(ways):
                            out_ref = outs[o + ways * q + side]

                            def block(n, carry):
                                src = pl.ds(a - lo, b - a)
                                value = keep_ref[side * count + n, src, :].astype(F32)
                                value = value + got_ref[side * count + n, src, :].astype(F32)
                                out_ref[n, a - lo2 : b - lo2, :] = low(value)
                                return carry

                            if count == 1:
                                block(0, 0)
                            else:
                                lax.fori_loop(0, count, block, 0)

    room = (1 << 20) + sum(a.size * a.dtype.itemsize for a in operands + shapes)
    outs = pl.pallas_call(
        body,
        out_shape=tuple(shapes),
        in_specs=[whole()] * len(operands),
        out_specs=(whole(),) * len(shapes),
        name="advance",
        compiler_params=pltpu.CompilerParams(vmem_limit_bytes=room),
    )(*operands)
    at = 0
    for f, step in zip(flows, steps):
        f.stage += 1
        if step[0] == "final":
            f.result = [
                out.T if final[0] == "turn" else out
                for out, final in zip(outs[at : at + len(step[3])], step[3])
            ]
            at += len(step[3])
            f.done = True
        else:
            ways = step[5]
            f.parts = [tuple(outs[at + ways * q : at + ways * (q + 1)]) for q in range(len(step[4]))]
            at += ways * len(step[4])


def exchange(begin, compute, inputs):
    sent, inputs = lax.optimization_barrier(([f.parts for f in begin], inputs))
    for f, value in zip(begin, sent):
        f.parts = value
    for f in begin:
        f.got = f.start()
    got, made = lax.optimization_barrier(([f.got for f in begin], compute(*inputs)))
    for f, value in zip(begin, got):
        f.got = value
    advance(begin)
    return made


def gather_stages(order):
    far, near = order[3:], order[1:3]
    return [far[i : i + 2] for i in range(0, len(far), 2)] + [near] + [order[:1]]


def gather_all(rows, stages):
    for stage in stages[:-1]:
        got = [swap(rows, *to) for to in ([stage] if len(stage) == 1 else [stage[:1], stage[1:], stage])]
        rows = join(rows, *got)
    return rows, swap(rows, *stages[-1])


def local(
    wide,
    narrow,
    query_x,
    query_seg,
    passage_x,
    passage_seg,
    labels,
    lookup,
    softness,
    bias_grid,
    gains,
    wq,
    wk,
    wv,
    wo,
    wg,
    wu,
    wd,
    wp,
):
    qrows, qlen, feat = query_x.shape
    prows, plen, _ = passage_x.shape
    buckets, heads = bias_grid.shape
    order_a, order_b = stage_orders(wide, narrow)
    me_w, me_n = lax.axis_index("wide"), lax.axis_index("narrow")
    me = jnp.stack([me_w, me_n]).astype(jnp.int32)

    hidden = wd.shape[0]
    block, cols, ff_block, ff_cols = feat // wide, feat // narrow, hidden // wide, hidden // narrow
    matrices = (wq, wk, wv, wo, wg, wu, wd, wp)
    (packed, vectors, e, pooled, x_between, x_last), (first, second) = forward(
        query_x.reshape(-1, feat),
        passage_x.reshape(-1, feat),
        lookup,
        bias_grid.T,
        query_seg,
        passage_seg,
        gains,
        labels,
        matrices,
    )
    down_rows, att_rows = block * ff_cols // 128, block * cols // 128
    jobs = None
    if not (cols % 128 or ff_block % 128 or block % 16):
        jobs = [
            (0, 1, "wide", [(order_a, 0, block, 0)]),
            (2, 3, "narrow", [(order_b, 0, cols, down_rows)]),
        ]
    groups = gather_stages(order_a)
    stages = [bit for group in groups for bit in group]
    here, there = gather_all(packed, groups)
    (gain_final, loss_part, grad_e, gain_mid, gain_in), back, parts = loss_and_back(
        me, narrow, stages, softness, here, there, e, gains, query_seg, passage_seg,
        x_last, x_between, first, second, matrices, wide, jobs, down_rows + cols,
    )
    grad_b, grad_b_2 = back["gb1"], back["gb"]
    att_2 = (back["gy"], back["gq"], back["gk"], back["gv"])
    h, o, normed, u = (first[name] for name in ("h", "o", "normed", "u"))
    h_2, o_2, normed_2, u_2 = (second[name] for name in ("h", "o", "normed", "u"))

    def split_sums(value):
        return value[:3], value[4 : 4 + heads, :buckets], value[3, :1]

    def finish(grad_a, grad_b):
        return rest_back(
            gains, lookup, buckets, (gain_in, gain_mid, gain_final, loss_part), grad_a, grad_b,
            back["grad_x"], back["ds"], first, matrices, query_x.reshape(-1, feat), passage_x.reshape(-1, feat),
        )

    if jobs is None:
        grad_f, grad_a = back["grad_f1"], back["ga1"]
        ffn_2 = (back["grad_f"], back["ga"], grad_b_2)
        sums, grad_y, grad_q, grad_k, grad_v, grad_x = finish(grad_a, grad_b)
        outs = split_sums(doubled(sums, order_a))

        def scatter(*pairs):
            full = low(sum(dot_tn(left, right) for left, right in pairs))
            full = lax.psum_scatter(full, "wide", scatter_dimension=1, tiled=True)
            return lax.psum_scatter(full, "narrow", scatter_dimension=0, tiled=True).astype(F32)

        grad_query = scatter((h, grad_q), (h_2, att_2[1]))
        grad_key = scatter((h, grad_k), (h_2, att_2[2]))
        grad_value = scatter((h, grad_v), (h_2, att_2[3]))
        grad_out = scatter((o, grad_y), (o_2, att_2[0]))
        grad_gate = scatter((normed, grad_a), (normed_2, ffn_2[1]))
        grad_up = scatter((normed, grad_b), (normed_2, ffn_2[2]))
        grad_down = scatter((u, grad_f), (u_2, ffn_2[0]))
        grad_proj = scatter((pooled, grad_e))
    else:
        orders = (order_a, order_b)
        finals = [("turn", 0, block, ff_cols), ("keep", down_rows, cols, ff_block)]
        ffn = Chunk(*parts, down_rows, orders, finals)

        cut = (cols + att_rows) // 2 // 16 * 16

        def make_up(grad_b, grad_b_2):
            return wgrad(
                me,
                [normed, normed_2, grad_b, grad_b_2, grad_e, pooled],
                [(0, 1), (2, 3), (4,), (5,)],
                [
                    (0, 1, "narrow", [(order_a, 0, cut, 0), (order_b, cut, cols - cut, cut)]),
                    (2, 3, "wide", [(order_b, 0, block, cols)]),
                ],
                cols + att_rows,
                wide,
                narrow,
                48,
            )

        parts = exchange([ffn], make_up, (grad_b, grad_b_2))
        finals = [("keep", 0, cols, ff_block), ("turn", cols, block, cols)]
        up = Chunk(*parts, cut, orders, finals)

        sums, *grads, grad_x = exchange([ffn, up], finish, (back["ga1"], grad_b))

        def make_rest(sums, grad_y, grad_q, grad_k, grad_v):
            got = swap(sums, order_a[-2])
            parts = wgrad(
                me,
                [grad_y, att_2[0], o, o_2, grad_q, att_2[1], h, h_2, grad_k, att_2[2], grad_v, att_2[3]],
                [(0, 1), (2, 3), (4, 5), (6, 7), (8, 9), (10, 11)],
                [
                    (0, 1, "wide", [(order_a, 0, block, 0)]),
                    (2, 3, "wide", [(order_a, 0, block, att_rows)]),
                    (4, 3, "wide", [(order_b, 0, block, 2 * att_rows)]),
                    (5, 3, "wide", [(order_b, 0, block, 3 * att_rows)]),
                ],
                4 * att_rows,
                wide,
                narrow,
                12,
            )
            got, parts = lax.optimization_barrier((got, parts))
            return parts, sums + got

        parts, sums = exchange([ffn, up], make_rest, (sums, *grads))
        att = Chunk(*parts, 2 * att_rows, orders, [("turn", i * att_rows, block, cols) for i in range(4)], True)
        for stage in order_a[-1:] + order_a[:2]:
            live = [f for f in (att, up, ffn) if not f.done]
            sums = exchange(live, lambda value: doubled(value, [stage]), (sums,))
        outs = exchange([att], lambda value: split_sums(doubled(value, order_a[2:-2])), (sums,))
        grad_down, grad_gate = ffn.result
        grad_up, grad_proj = up.result
        grad_out, grad_query, grad_key, grad_value = att.result
    gain_total, bucket_total, loss_total = outs
    mean_loss = loss_total / (qrows * QSEGS * wide * narrow)
    return (
        mean_loss,
        vectors[:QSEGS],
        vectors[QSEGS : QSEGS + PSEGS],
        grad_x[:qlen].reshape(1, qlen, feat),
        grad_x[qlen:].reshape(1, plen, feat),
        gain_total,
        bucket_total.T,
        grad_query,
        grad_key,
        grad_value,
        grad_out,
        grad_gate,
        grad_up,
        grad_down,
        grad_proj,
    )


def solution(mesh):
    rows3, rows2, rows1 = P(AXES, None, None), P(AXES, None), P(AXES)
    return jax.shard_map(
        functools.partial(local, mesh.shape["wide"], mesh.shape["narrow"]),
        mesh=mesh,
        in_specs=(rows3, rows2, rows3, rows2, rows1) + (P(),) * 12,
        out_specs=(P(), rows2, rows2, rows3, rows3, P(), P()) + (P("narrow", "wide"),) * 8,
        check_vma=False,
    )
```

```python
import functools

import jax
import jax.numpy as jnp
from jax import lax
from jax.experimental import pallas as pl
from jax.experimental.pallas import tpu as pltpu
from jax.sharding import PartitionSpec as P

LAYERS = 2
QSEGS = 3
PSEGS = 4
HDIM = 64
PACK = 8

HIGHEST = lax.Precision.HIGHEST
EPSILON = 1e-06
MASKED = -1000000000.0
BF = jnp.bfloat16
F32 = jnp.float32
AXES = ("wide", "narrow")


def low(a):
    return a.astype(BF)


def product(a, b):
    return jnp.dot(a, b, preferred_element_type=F32)


def dot_tn(a, b, precision=None):
    return lax.dot_general(
        a, b, (((0,), (0,)), ((), ())), preferred_element_type=F32, precision=precision
    )


def dot_nt(a, b, precision=None):
    return lax.dot_general(
        a, b, (((1,), (1,)), ((), ())), preferred_element_type=F32, precision=precision
    )


def whole():
    return pl.BlockSpec(memory_space=pltpu.VMEM)


def bias_kernel(qlen, plen, lookup_ref, grid_ref, qseg_ref, pseg_ref, pbias_ref, qbias_ref, wide_s, short_s):
    heads, buckets = grid_ref.shape
    width = 2 * plen
    wide_s[...] = jnp.full((1, width), -1, jnp.int32)
    wide_s[:, : lookup_ref.shape[1]] = lookup_ref[...]
    onehot = (
        lax.broadcasted_iota(jnp.int32, (buckets, width), 0)
        == jnp.broadcast_to(wide_s[...], (buckets, width))
    ).astype(F32)
    table = jnp.dot(grid_ref[...], onehot, precision=HIGHEST, preferred_element_type=F32)
    pcol = jnp.transpose(jnp.broadcast_to(pseg_ref[...], (plen, plen)))
    psame = pcol == jnp.broadcast_to(pseg_ref[...], (plen, plen))
    short_s[...] = jnp.full((1, 128), -1, jnp.int32)
    short_s[:, :qlen] = qseg_ref[...]
    qcol = jnp.transpose(jnp.broadcast_to(short_s[...], (128, 128)))
    qsame = (qcol == jnp.broadcast_to(short_s[...], (128, 128)))[:qlen, :qlen]
    for head in range(heads):
        rows = jnp.broadcast_to(table[head : head + 1, :], (plen, width))
        rolled = pltpu.roll(rows, width - (plen - 1), 1, stride=1, stride_axis=0)
        block = rolled[:, :plen]
        pbias_ref[head] = jnp.where(psame, block, MASKED)
        qbias_ref[head] = jnp.where(qsame, block[:qlen, :qlen], MASKED)


def half_mask(lanes, side):
    return (lax.broadcasted_iota(jnp.int32, (1, lanes), 1) // HDIM) == side


def attend_kernel(qlen, q_ref, k_ref, v_ref, pbias_ref, qbias_ref, o_ref, pp_ref, pq_ref):
    pairs = q_ref.shape[1] // 128
    spans = ((0, qlen, qbias_ref, pq_ref), (qlen, q_ref.shape[0] - qlen, pbias_ref, pp_ref))

    def pair(i, carry):
        lanes = pl.ds(pl.multiple_of(i * 128, 128), 128)
        for start, length, bias_ref, keep_ref in spans:
            rows = pl.ds(start, length)
            q2, k2, v2 = q_ref[rows, lanes], k_ref[rows, lanes], v_ref[rows, lanes]
            total = None
            for side in range(2):
                mine = half_mask(128, side)
                zero = jnp.zeros_like(k2)
                s = dot_nt(q2, jnp.where(mine, k2, zero)) + bias_ref[2 * i + side]
                top = jnp.max(s, axis=-1, keepdims=True)
                e = jnp.exp(s - top)
                p = low(e * (1.0 / jnp.sum(e, axis=-1, keepdims=True)))
                keep_ref[2 * i + side] = p
                part = product(p, jnp.where(mine, v2, zero))
                total = part if total is None else total + part
            o_ref[rows, lanes] = low(total)
        return carry

    lax.fori_loop(0, pairs, pair, 0, unroll=2)


def attend_back_kernel(
    qlen, q_ref, k_ref, v_ref, o_ref, go_ref, pp_ref, pq_ref, acc_ref, gq_ref, gk_ref, gv_ref, ds_ref
):
    pairs = q_ref.shape[1] // 128
    plen = q_ref.shape[0] - qlen

    def pair(i, carry):
        lanes = pl.ds(pl.multiple_of(i * 128, 128), 128)
        for start, length, keep_ref in ((qlen, plen, pp_ref), (0, qlen, pq_ref)):
            rows = pl.ds(start, length)
            q2, k2, v2 = q_ref[rows, lanes], k_ref[rows, lanes], v_ref[rows, lanes]
            o2, go2 = o_ref[rows, lanes], go_ref[rows, lanes]
            prod = o2.astype(F32) * go2.astype(F32)
            gq, gk, gv = None, None, None
            for side in range(2):
                mine = half_mask(128, side)
                zero = jnp.zeros_like(k2)
                p = keep_ref[2 * i + side]
                gp = dot_nt(go2, jnp.where(mine, v2, zero))
                delta = jnp.sum(jnp.where(mine, prod, 0.0), axis=-1, keepdims=True)
                ds = p.astype(F32) * (gp - delta)
                if start == qlen:
                    if acc_ref is None:
                        ds_ref[2 * i + side] = ds
                    else:
                        ds_ref[2 * i + side] = ds + acc_ref[2 * i + side]
                else:
                    ds_ref[2 * i + side, :length, :length] += ds
                dsl = low(ds)
                a = product(dsl, jnp.where(mine, k2, zero))
                b = dot_tn(dsl, jnp.where(mine, q2, zero))
                c = dot_tn(p, jnp.where(mine, go2, zero))
                gq = a if gq is None else gq + a
                gk = b if gk is None else gk + b
                gv = c if gv is None else gv + c
            gq_ref[rows, lanes] = low(gq)
            gk_ref[rows, lanes] = low(gk)
            gv_ref[rows, lanes] = low(gv)
        return carry

    lax.fori_loop(0, pairs, pair, 0, unroll=2)


def small_kernel(
    buckets, ds_ref, lookup_ref, in_ref, mid_ref, final_ref, loss_ref, out_ref, diag_ref, wide_s
):
    heads, plen, _ = ds_ref.shape
    out_ref[...] = jnp.zeros_like(out_ref)
    out_ref[0:1, :] = in_ref[...]
    out_ref[1:2, :] = mid_ref[...]
    out_ref[2:3, :] = final_ref[...]
    out_ref[3:4, :128] = loss_ref[...]
    width = 2 * plen
    wide_s[...] = jnp.full((1, width), -1, jnp.int32)
    wide_s[:, : lookup_ref.shape[1]] = lookup_ref[...]
    for head in range(heads):
        block = ds_ref[head]
        wide_block = jnp.concatenate([block, jnp.zeros_like(block)], axis=1)
        rows = plen
        while rows > 8:
            rows //= 2
            wide_block = wide_block[:rows] + pltpu.roll(wide_block[rows:], width - rows, 1)
        at = lax.broadcasted_iota(jnp.int32, (8, width), 0)
        for bit in (4, 2, 1):
            moved = pltpu.roll(wide_block, width - bit, 1)
            wide_block = jnp.where((at & bit) != 0, moved, wide_block)
        rolled = pltpu.roll(wide_block, plen - 1, 1)
        diag_ref[head : head + 1, :] = jnp.sum(rolled, axis=0, keepdims=True)
    onehot = (
        lax.broadcasted_iota(jnp.int32, (buckets, width), 0)
        == jnp.broadcast_to(wide_s[...], (buckets, width))
    ).astype(F32)
    out_ref[4 : 4 + heads, :buckets] = dot_nt(diag_ref[...], onehot, HIGHEST)


def segment_table(seg_ref, first):
    rows, length = PACK, seg_ref.shape[1]
    slot = lax.broadcasted_iota(jnp.int32, (rows, length), 0)
    return (slot == jnp.broadcast_to(seg_ref[...], (rows, length)) + first).astype(F32)


def pool_kernel(
    x_ref, gain_ref, qseg_ref, pseg_ref, label_ref, wp_ref, packed_ref, vec_ref, e_ref, pooled_ref
):
    qlen = qseg_ref.shape[1]
    x = x_ref[...]
    z = x * lax.rsqrt(jnp.mean(x * x, axis=-1, keepdims=True) + EPSILON) * gain_ref[...]
    qt, pt = segment_table(qseg_ref, 0), segment_table(pseg_ref, QSEGS)
    sizes = jnp.sum(qt, axis=1, keepdims=True) + jnp.sum(pt, axis=1, keepdims=True)
    sums = jnp.dot(qt, z[:qlen], precision=HIGHEST, preferred_element_type=F32) + jnp.dot(
        pt, z[qlen:], precision=HIGHEST, preferred_element_type=F32
    )
    pooled = low(sums / jnp.maximum(sizes, 1.0))
    pooled_ref[...] = pooled
    e = product(pooled, wp_ref[...])
    e_ref[...] = e
    vec = e * lax.rsqrt(jnp.sum(e * e, axis=-1, keepdims=True) + EPSILON)
    vec_ref[...] = vec
    at = lax.broadcasted_iota(jnp.int32, vec.shape, 1)
    row = lax.broadcasted_iota(jnp.int32, vec.shape, 0)
    code = jnp.zeros(vec.shape, F32)
    for i in range(QSEGS):
        label = label_ref[i]
        high = lax.shift_right_logical(label, 5).astype(F32)
        rest = (label & 31).astype(F32)
        code = jnp.where(at == i, high, jnp.where(at == QSEGS + i, rest, code))
    packed_ref[...] = low(jnp.where(row == PACK - 1, code, vec))


SLOPE = 0.7978845608028654
CUBE = 0.044715
SAVED = ("h", "q", "k", "v", "pp", "pq", "o", "x_mid", "normed", "da", "db", "u")


def unit_scale(x):
    return lax.rsqrt(jnp.mean(x * x, axis=-1, keepdims=True) + EPSILON)


def gated_parts(a, b):
    square = a * a
    th = jnp.tanh(a * (SLOPE + (SLOPE * CUBE) * square))
    half = 0.5 + 0.5 * th
    value = a * half
    slope = half + (0.5 * a) * (1.0 - th * th) * (SLOPE + (3.0 * SLOPE * CUBE) * square)
    return low(value * b), low(b * slope), low(value)


def forward_kernel(qlen, plen, n_tiles, *refs):
    (qx_ref, px_ref, lookup_ref, grid_ref, qseg_ref, pseg_ref, gains_ref, label_ref), refs = refs[:8], refs[8:]
    hbm, refs = refs[:8], refs[8:]
    packed_ref, vec_ref, e_ref, pooled_ref, x_mid_out, x_out = refs[:6]
    refs = refs[6:]
    outs = [dict(zip(SAVED, refs[n * len(SAVED) : (n + 1) * len(SAVED)])) for n in range(LAYERS)]
    refs = refs[LAYERS * len(SAVED) :]
    held, refs = refs[:8], refs[8:]
    keep, refs = dict(zip(SAVED, refs[: len(SAVED)])), refs[len(SAVED) :]
    x_s, pbias_s, qbias_s, wide_s, short_s, in_sem, out_sem, x_sem = refs
    wq_s, wk_s, wv_s, wo_s, wg_s, wu_s, wd_s, wp_s = held
    fetch = [pltpu.make_async_copy(a, b, in_sem.at[i]) for i, (a, b) in enumerate(zip(hbm, held))]
    for c in fetch:
        c.start()
    x_s[0, :qlen] = qx_ref[...].astype(F32)
    x_s[0, qlen:] = px_ref[...].astype(F32)
    bias_kernel(qlen, plen, lookup_ref, grid_ref, qseg_ref, pseg_ref, pbias_s, qbias_s, wide_s, short_s)

    def write(n, name):
        i = n * len(SAVED) + SAVED.index(name)
        return pltpu.make_async_copy(keep[name].at[n], outs[n][name], out_sem.at[i])

    def send(layer, *names):
        for n in range(LAYERS):

            @pl.when(layer == n)
            def _():
                for name in names:
                    write(n, name).start()

    def arrive(layer, *ids):
        @pl.when(layer == 0)
        def _():
            for i in ids:
                fetch[i].wait()

    def layer_step(layer, carry):
        x = x_s[layer]
        h = low(x * unit_scale(x) * gains_ref[0:1, :])
        keep["h"][layer] = h
        for i, (name, w) in enumerate((("q", wq_s), ("k", wk_s), ("v", wv_s))):
            arrive(layer, i)
            keep[name][layer] = low(product(h, w[...]))
        send(layer, "h", "q", "k", "v")
        at = {name: keep[name].at[layer] for name in SAVED}
        attend_kernel(qlen, at["q"], at["k"], at["v"], pbias_s, qbias_s, at["o"], at["pp"], at["pq"])
        send(layer, "o", "pp", "pq")
        arrive(layer, 3)
        x_mid = x_s[layer] + product(at["o"][...], wo_s[...])
        at["x_mid"][...] = x_mid
        normed = low(x_mid * unit_scale(x_mid) * gains_ref[1:2, :])
        at["normed"][...] = normed
        send(layer, "x_mid", "normed")
        arrive(layer, 4, 5)
        size = wg_s.shape[1] // n_tiles
        for t in range(n_tiles):
            lanes = slice(t * size, (t + 1) * size)
            a = product(normed, wg_s[:, lanes])
            b = product(normed, wu_s[:, lanes])
            u, da, db = gated_parts(a, b)
            at["u"][:, lanes] = u
            at["da"][:, lanes] = da
            at["db"][:, lanes] = db
        send(layer, "u", "da", "db")
        arrive(layer, 6)
        x_s[layer + 1] = at["x_mid"][...] + product(at["u"][...], wd_s[...])
        return carry

    lax.fori_loop(0, LAYERS, layer_step, 0)
    inner = pltpu.make_async_copy(x_s.at[1], x_mid_out, x_sem.at[0])
    outer = pltpu.make_async_copy(x_s.at[LAYERS], x_out, x_sem.at[1])
    inner.start()
    outer.start()
    fetch[7].wait()
    pool_kernel(
        x_s.at[LAYERS], gains_ref.at[2:3], qseg_ref, pseg_ref, label_ref, wp_s, packed_ref, vec_ref, e_ref, pooled_ref
    )
    for n in range(LAYERS):
        for name in SAVED:
            write(n, name).wait()
    inner.wait()
    outer.wait()


def saved_shapes(total, qlen, plen, feat, hidden, heads):
    tok, ff = ((total, feat), BF), ((total, hidden), BF)
    kinds = dict(h=tok, q=tok, k=tok, v=tok, o=tok, normed=tok, da=ff, db=ff, u=ff)
    kinds["pp"], kinds["pq"] = ((heads, plen, plen), BF), ((heads, qlen, qlen), BF)
    kinds["x_mid"] = ((total, feat), F32)
    return [kinds[name] for name in SAVED]


def forward(qx, px, lookup, grid, qseg, pseg, gains, labels, matrices):
    qlen, feat = qx.shape
    plen, heads, hidden = px.shape[0], grid.shape[0], matrices[4].shape[1]
    total = qlen + plen
    kinds = saved_shapes(total, qlen, plen, feat, hidden, heads)
    small = (PACK, feat)
    shapes = [(small, BF), (small, F32), (small, F32), (small, BF), ((total, feat), F32), ((total, feat), F32)]
    shapes += kinds * LAYERS
    anywhere = pl.BlockSpec(memory_space=pltpu.HBM)
    smem = pl.BlockSpec(memory_space=pltpu.SMEM)
    weights = sum(m.size for m in matrices)
    outs = pl.pallas_call(
        functools.partial(forward_kernel, qlen, plen, 4),
        out_shape=tuple(jax.ShapeDtypeStruct(*s) for s in shapes),
        in_specs=[whole()] * 7 + [smem] + [anywhere] * 8,
        out_specs=(whole(),) * 4 + (anywhere,) * (2 + LAYERS * len(SAVED)),
        scratch_shapes=[pltpu.VMEM(m.shape, BF) for m in matrices]
        + [pltpu.VMEM((LAYERS,) + shape, dtype) for shape, dtype in kinds]
        + [
            pltpu.VMEM((LAYERS + 1, total, feat), F32),
            pltpu.VMEM((heads, plen, plen), F32),
            pltpu.VMEM((heads, qlen, qlen), F32),
            pltpu.VMEM((1, 2 * plen), jnp.int32),
            pltpu.VMEM((1, 128), jnp.int32),
            pltpu.SemaphoreType.DMA((8,)),
            pltpu.SemaphoreType.DMA((LAYERS * len(SAVED),)),
            pltpu.SemaphoreType.DMA((2,)),
        ],
        name="forward",
        compiler_params=pltpu.CompilerParams(vmem_limit_bytes=56 << 20),
        cost_estimate=pl.CostEstimate(
            flops=2 * LAYERS * total * weights, bytes_accessed=2 * weights, transcendentals=LAYERS * total * hidden
        ),
    )(qx, px, lookup[None], grid, qseg, pseg, gains, labels, *matrices)
    saved = [dict(zip(SAVED, outs[6 + n * len(SAVED) : 6 + (n + 1) * len(SAVED)])) for n in range(LAYERS)]
    return outs[:6], saved


def loss_kernel(
    narrow, stages, me_ref, sharp_ref, here_ref, there_ref, e_ref, x_ref, gain_ref,
    qseg_ref, pseg_ref, wp_ref, gx_ref, ggain_ref, loss_ref, ge_ref, flat_s,
):
    half = here_ref.shape[0]
    flat_s[:half, :] = here_ref[...]
    flat_s[half:, :] = there_ref[...]
    size = 2 * half
    tile = min(size, 256)
    sharp = sharp_ref[0]
    lane = lax.broadcasted_iota(jnp.int32, (1, size), 1)
    block, slot = lax.shift_right_logical(lane, 3), lane & (PACK - 1)
    dw, dn = jnp.zeros_like(block), jnp.zeros_like(block)
    for k, (axis, bit) in enumerate(stages):
        on = (lax.shift_right_logical(block, k) & 1) * bit
        dw, dn = (dw + on, dn) if axis == "wide" else (dw, dn + on)
    device = (dw ^ me_ref[0]) * narrow + (dn ^ me_ref[1])
    is_passage = (slot >= QSEGS) & (slot < QSEGS + PSEGS)
    document = jnp.where(is_passage, device * PSEGS + slot - QSEGS, -2)
    row = lax.broadcasted_iota(jnp.int32, (tile, 1), 0)
    row_slot = row & (PACK - 1)
    is_query = row_slot < QSEGS
    across = lax.broadcasted_iota(jnp.int32, (tile, tile), 1)
    source = low((across == row - row_slot + PACK - 1).astype(F32))
    place = lax.broadcasted_iota(jnp.int32, (tile, 128), 1)
    weigh = jnp.where(place == row_slot, 32.0, 0.0) + jnp.where(place == row_slot + QSEGS, 1.0, 0.0)
    mine = lax.broadcasted_iota(jnp.int32, (1, 128), 1) < PACK
    grad = None
    for t in range(size // tile):
        rows = flat_s[t * tile : (t + 1) * tile, :]
        match = dot_nt(rows, flat_s[...]) / sharp
        match = jnp.where(is_passage, match, MASKED)
        label = jnp.sum(product(source, rows[:, :128]) * weigh, axis=1, keepdims=True)
        hit = (label.astype(jnp.int32) == document) & is_query
        top = jnp.max(match, axis=1, keepdims=True)
        ex = jnp.exp(match - top)
        line = jnp.sum(ex, axis=1, keepdims=True)
        g = (ex / line - hit.astype(F32)) / sharp
        g = low(jnp.where(is_query & is_passage, g, 0.0))
        back = dot_tn(jnp.where(mine, g[:, :128], jnp.zeros_like(g[:, :128])), rows)[:PACK]
        if t == 0:
            part = jnp.sum(jnp.where(hit, match, 0.0), axis=1, keepdims=True)
            part = jnp.where(is_query & (row < PACK), top + jnp.log(line) - part, 0.0)
            loss_ref[...] = jnp.broadcast_to(jnp.sum(part, axis=0, keepdims=True), loss_ref.shape)
            grad = product(g[:16], flat_s[...])[:PACK]
        grad = grad + back
    e = e_ref[...]
    scale = lax.rsqrt(jnp.sum(e * e, axis=-1, keepdims=True) + EPSILON)
    vec = e * scale
    ge = low((grad - vec * jnp.sum(vec * grad, axis=-1, keepdims=True)) * scale)
    ge_ref[...] = ge
    qt, pt = segment_table(qseg_ref, 0), segment_table(pseg_ref, QSEGS)
    sizes = jnp.sum(qt, axis=1, keepdims=True) + jnp.sum(pt, axis=1, keepdims=True)
    pooled = dot_nt(ge, wp_ref[...]) / jnp.maximum(sizes, 1.0)
    qlen = qseg_ref.shape[1]
    gain = gain_ref[...]
    total = None
    for table, start, count in ((qt, 0, qlen), (pt, qlen, pseg_ref.shape[1])):
        gz = dot_tn(table, pooled, HIGHEST)
        x = x_ref[start : start + count, :]
        r = lax.rsqrt(jnp.mean(x * x, axis=-1, keepdims=True) + EPSILON)
        unit = x * r
        scaled = gz * gain
        gx_ref[start : start + count, :] = r * (
            scaled - unit * jnp.mean(unit * scaled, axis=-1, keepdims=True)
        )
        part = jnp.sum(gz * unit, axis=0, keepdims=True)
        total = part if total is None else total + part
    ggain_ref[...] = total


PAIRED = ("grad_f", "ga", "grad_f1", "ga1")
BACK = ("grad_f", "ga", "gb", "gy", "gq", "gk", "gv", "ds", "grad_f1", "ga1", "gb1", "grad_x")


def through_norm(x, gain, grad):
    r = unit_scale(x)
    unit = x * r
    scaled = grad * gain
    back = r * (scaled - unit * jnp.mean(unit * scaled, axis=-1, keepdims=True))
    return back, jnp.sum(grad * unit, axis=0, keepdims=True)


def back_kernel(narrow, stages, qlen, n_tiles, n_held, names, jobs, job_rows, *refs):
    me_ref, sharp_ref, here_ref, there_ref, e_ref, gains_ref, qseg_ref, pseg_ref = refs[:8]
    refs = refs[8:]
    n_fetch = n_held + (4 if jobs else 0)
    hbm, refs = refs[:n_fetch], refs[n_fetch:]
    ggain_ref, loss_ref, ge_ref, gmid_ref, gin_ref = refs[:5]
    outs, refs = dict(zip(names, refs[5 : 5 + len(names)])), refs[5 + len(names) :]
    if jobs:
        (keep_ref, send_ref), refs = refs[:2], refs[2:]
    held, refs = list(refs[: n_held - 4]), refs[n_held - 4 :]
    singles = [n for n in BACK if n not in PAIRED and n != "grad_x"]
    keep, refs = dict(zip(singles, refs[: len(singles)])), refs[len(singles) :]
    gf_s, ga_s, wide_s, row_s, flat_s, gx_s, go_s, in_sem, out_sem = refs[:9]
    total = gx_s.shape[0]
    keep["grad_x"] = gx_s
    halves = [buf.at[i * total : (i + 1) * total] for buf in (wide_s, row_s) for i in range(2)]
    held = held[:3] + halves[:2] + held[3:7] + halves[2:] + held[7:] + halves
    for i, (name, buf) in enumerate((("grad_f1", gf_s), ("ga1", ga_s), ("grad_f", gf_s), ("ga", ga_s))):
        keep[name] = buf.at[i // 2 * total : (i // 2 + 1) * total]
    fetch = [pltpu.make_async_copy(a, b, in_sem.at[i]) for i, (a, b) in enumerate(zip(hbm, held))]
    for c in fetch[:21]:
        c.start()
    (x2_s, wp_s, wd_s, da_s, db_s, wg_s, wu_s, xm_s, wo_s, v_s, o_s, pp_s, k_s, q_s, pq_s) = held[:15]
    wq_s, wk_s, wv_s, x_s, da1_s, db1_s = held[15:21]

    def write(name):
        return pltpu.make_async_copy(keep[name], outs[name], out_sem.at[names.index(name)])

    def send(*ready):
        for name in ready:
            if name in outs:
                write(name).start()

    fetch[0].wait()
    fetch[1].wait()
    loss_kernel(
        narrow, stages, me_ref, sharp_ref, here_ref, there_ref, e_ref, x2_s, gains_ref.at[2:3],
        qseg_ref, pseg_ref, wp_s, gx_s, ggain_ref, loss_ref, ge_ref, flat_s,
    )

    def gated_back(x_ref, da, db, made):
        grad_f = low(x_ref[...])
        keep[made[0]][...] = grad_f
        size = da.shape[1] // n_tiles
        for t in range(n_tiles):
            lanes = slice(t * size, (t + 1) * size)
            gu = dot_nt(grad_f, wd_s[lanes, :])
            keep[made[1]][:, lanes] = low(gu * da[:, lanes].astype(F32))
            keep[made[2]][:, lanes] = low(gu * db[:, lanes].astype(F32))
        send(*made)

    for i in (2, 3, 4):
        fetch[i].wait()
    gated_back(gx_s, da_s, db_s, BACK[:3])
    for c in fetch[21:23]:
        c.start()
    for i in (5, 6, 7):
        fetch[i].wait()
    grad = dot_nt(keep["ga"][...], wg_s[...]) + dot_nt(keep["gb"][...], wu_s[...])
    back, gmid_ref[...] = through_norm(xm_s[...], gains_ref[1:2, :], grad)
    grad_mid = gx_s[...] + back
    gx_s[...] = grad_mid
    gy = low(grad_mid)
    keep["gy"][...] = gy
    send("gy")
    fetch[8].wait()
    go_s[...] = low(dot_nt(gy, wo_s[...]))
    for i in range(9, 15):
        fetch[i].wait()
    attend_back_kernel(
        qlen, q_s, k_s, v_s, o_s, go_s, pp_s, pq_s, None, keep["gq"], keep["gk"], keep["gv"], keep["ds"]
    )
    send("gq", "gk", "gv", "ds")
    for c in fetch[23:]:
        c.start()
    for i in range(15, 19):
        fetch[i].wait()
    grad = dot_nt(keep["gq"][...], wq_s[...]) + dot_nt(keep["gk"][...], wk_s[...])
    grad = grad + dot_nt(keep["gv"][...], wv_s[...])
    back, gin_ref[...] = through_norm(x_s[...], gains_ref[0:1, :], grad)
    gx_s[...] = gx_s[...] + back
    send("grad_x")
    fetch[19].wait()
    fetch[20].wait()
    gated_back(gx_s, da1_s, db1_s, BACK[8:11])
    if jobs:
        for i in range(21, 25):
            fetch[i].wait()
        turned_s, keep_s, send_s, block_sem = refs[9:]
        first_row, moves = 0, []
        for i, (job, rows) in enumerate(zip(jobs, job_rows)):
            weight_products(
                [job], (gf_s, wide_s, row_s, ga_s), lambda g: None, me_ref, keep_s, send_s, turned_s
            )
            span = pl.ds(first_row, rows)
            for j, (a, b) in enumerate(((send_s, send_ref), (keep_s, keep_ref))):
                move = pltpu.make_async_copy(a.at[:, span], b.at[:, span], block_sem.at[2 * i + j])
                move.start()
                moves.append(move)
            first_row += rows
        for move in moves:
            move.wait()
    for name in names:
        write(name).wait()


def loss_and_back(me, narrow, stages, sharp, here, there, e, gains, qseg, pseg, x_last, x_in, first, second, matrices, wide, jobs, job_rows):
    wq, wk, wv, wo, wg, wu, wd, wp = matrices
    total, feat = x_last.shape
    qlen, plen = qseg.shape[1], pseg.shape[1]
    heads, hidden = second["pp"].shape[0], wd.shape[0]
    size = 2 * here.shape[0]
    t = second
    fetched = [x_last, wp, wd, t["da"], t["db"], wg, wu, t["x_mid"], wo, t["v"], t["o"], t["pp"], t["k"], t["q"], t["pq"]]
    fetched += [wq, wk, wv, x_in, first["da"], first["db"]]
    tok, ff = ((total, feat), BF), ((total, hidden), BF)
    kinds = [tok, ff, ff, tok, tok, tok, tok, ((heads, plen, plen), F32), tok, ff, ff, ((total, feat), F32)]
    kinds = dict(zip(BACK, kinds))
    names = [n for n in BACK if not (jobs and n in ("grad_f", "ga", "grad_f1"))]
    held = [pltpu.VMEM(a.shape, a.dtype) for i, a in enumerate(fetched) if i not in (3, 4, 9, 10)]
    n_held = len(fetched)
    blocks, late = [], []
    if jobs:
        fetched += [first["u"], second["u"], first["normed"], second["normed"]]
        blocks = [((wide * narrow // 2, sum(job_rows), 128), BF)] * 2
        late = [pltpu.VMEM((384, 2 * total), BF)] + [pltpu.VMEM(*b) for b in blocks]
        late.append(pltpu.SemaphoreType.DMA((4,)))
        widths = (feat, hidden, feat, hidden)
        jobs = with_blocks(jobs, lambda g: widths[g], wide, narrow)
    small = [((1, feat), F32), ((1, 128), F32), ((PACK, feat), BF), ((1, feat), F32), ((1, feat), F32)]
    anywhere = pl.BlockSpec(memory_space=pltpu.HBM)
    smem = pl.BlockSpec(memory_space=pltpu.SMEM)
    weights = sum(m.size for m in matrices)
    outs = pl.pallas_call(
        functools.partial(back_kernel, narrow, stages, qlen, 4, n_held, names, jobs, job_rows),
        out_shape=tuple(jax.ShapeDtypeStruct(*s) for s in small + [kinds[n] for n in names] + blocks),
        in_specs=[smem, smem] + [whole()] * 6 + [anywhere] * len(fetched),
        out_specs=(whole(),) * 5 + (anywhere,) * len(names) + (anywhere,) * len(blocks),
        scratch_shapes=held
        + [pltpu.VMEM(*kinds[n]) for n in BACK if n not in PAIRED and n != "grad_x"]
        + [
            pltpu.VMEM((2 * total, feat), BF),
            pltpu.VMEM((2 * total, hidden), BF),
            pltpu.VMEM((2 * total, hidden), BF),
            pltpu.VMEM((2 * total, feat), BF),
            pltpu.VMEM((size, feat), BF),
            pltpu.VMEM((total, feat), F32),
            pltpu.VMEM((total, feat), BF),
            pltpu.SemaphoreType.DMA((len(fetched),)),
            pltpu.SemaphoreType.DMA((len(names),)),
        ]
        + late,
        name="loss_and_back",
        compiler_params=pltpu.CompilerParams(vmem_limit_bytes=(54 if jobs else 56) << 20),
        cost_estimate=pl.CostEstimate(
            flops=3 * total * weights, bytes_accessed=2 * weights, transcendentals=0
        ),
    )(me, sharp, here, there, e, gains, qseg, pseg, *fetched)
    return outs[:5], dict(zip(names, outs[5:])), outs[5 + len(names) :]


REST = ("gy", "gq", "gk", "gv", "grad_x")


def rest_kernel(qlen, buckets, n_held, *refs):
    gains_ref, lookup_ref, gin_ref, gmid_ref, gfin_ref, loss_ref = refs[:6]
    refs = refs[6:]
    hbm, refs = refs[:n_held], refs[n_held:]
    sums_ref, outs, refs = refs[0], dict(zip(REST, refs[1:6])), refs[6:]
    held, refs = refs[:n_held], refs[n_held:]
    keep, refs = dict(zip(REST, refs[:5])), refs[5:]
    go_s, row_s, diag_s, wide_s, in_sem, out_sem = refs
    (ga_s, wg_s, gb_s, wu_s, xm_s, gx_s, wo_s, q_s, k_s, v_s, o_s, pp_s, pq_s, ds_s) = held[:14]
    wq_s, wk_s, wv_s, qx_s, px_s = held[14:]
    fetch = [pltpu.make_async_copy(a, b, in_sem.at[i]) for i, (a, b) in enumerate(zip(hbm, held))]
    for c in fetch:
        c.start()

    def arrive(first, last):
        for i in range(first, last):
            fetch[i].wait()

    def write(name):
        return pltpu.make_async_copy(keep[name], outs[name], out_sem.at[REST.index(name)])

    arrive(0, 2)
    grad = dot_nt(ga_s[...], wg_s[...])
    arrive(2, 6)
    grad = grad + dot_nt(gb_s[...], wu_s[...])
    back, part = through_norm(xm_s[...], gains_ref[1:2, :], grad)
    row_s[1:2, :] = gmid_ref[...] + part
    grad_mid = gx_s[...] + back
    gx_s[...] = grad_mid
    gy = low(grad_mid)
    keep["gy"][...] = gy
    write("gy").start()
    arrive(6, 7)
    go_s[...] = low(dot_nt(gy, wo_s[...]))
    arrive(7, 14)
    attend_back_kernel(
        qlen, q_s, k_s, v_s, o_s, go_s, pp_s, pq_s, ds_s, keep["gq"], keep["gk"], keep["gv"], ds_s
    )
    for name in REST[1:4]:
        write(name).start()
    arrive(14, 19)
    grad = dot_nt(keep["gq"][...], wq_s[...]) + dot_nt(keep["gk"][...], wk_s[...])
    grad = grad + dot_nt(keep["gv"][...], wv_s[...])
    x = jnp.concatenate([qx_s[...], px_s[...]], axis=0).astype(F32)
    back, part = through_norm(x, gains_ref[0:1, :], grad)
    row_s[0:1, :] = gin_ref[...] + part
    keep["grad_x"][...] = gx_s[...] + back
    write("grad_x").start()
    small_kernel(
        buckets, ds_s, lookup_ref, row_s.at[0:1], row_s.at[1:2], gfin_ref, loss_ref, sums_ref, diag_s, wide_s
    )
    for name in REST:
        write(name).wait()


def rest_back(gains, lookup, buckets, small, ga, gb, gx, acc, first, matrices, qx, px):
    wq, wk, wv, wo, wg, wu = matrices[:6]
    total, feat = gx.shape
    heads, plen, _ = acc.shape
    qlen = qx.shape[0]
    t = first
    fetched = [ga, wg, gb, wu, t["x_mid"], gx, wo, t["q"], t["k"], t["v"], t["o"], t["pp"], t["pq"], acc]
    fetched += [wq, wk, wv, qx, px]
    kinds = [((total, feat), BF)] * 4 + [((total, feat), F32)]
    anywhere = pl.BlockSpec(memory_space=pltpu.HBM)
    weights = sum(m.size for m in matrices[:6])
    outs = pl.pallas_call(
        functools.partial(rest_kernel, qlen, buckets, len(fetched)),
        out_shape=tuple(jax.ShapeDtypeStruct(*k) for k in [((4 + heads, feat), F32)] + kinds),
        in_specs=[whole()] * 6 + [anywhere] * len(fetched),
        out_specs=(whole(),) + (anywhere,) * len(kinds),
        scratch_shapes=[pltpu.VMEM(a.shape, a.dtype) for a in fetched]
        + [pltpu.VMEM(*k) for k in kinds]
        + [
            pltpu.VMEM((total, feat), BF),
            pltpu.VMEM((8, feat), F32),
            pltpu.VMEM((heads, 2 * plen), F32),
            pltpu.VMEM((1, 2 * plen), jnp.int32),
            pltpu.SemaphoreType.DMA((len(fetched),)),
            pltpu.SemaphoreType.DMA((len(kinds),)),
        ],
        name="rest_back",
        compiler_params=pltpu.CompilerParams(vmem_limit_bytes=50 << 20),
        cost_estimate=pl.CostEstimate(
            flops=3 * total * weights, bytes_accessed=2 * weights, transcendentals=0
        ),
    )(gains, lookup[None], *small, *fetched)
    return outs


def join_kernel(*refs):
    ins, out_ref = refs[:-1], refs[-1]
    rows = ins[0].shape[0]
    for i, ref in enumerate(ins):
        out_ref[i * rows : (i + 1) * rows, :] = ref[...]


def join(*parts):
    a = parts[0]
    return pl.pallas_call(
        join_kernel,
        out_shape=jax.ShapeDtypeStruct((len(parts) * a.shape[0], a.shape[1]), a.dtype),
        in_specs=[whole()] * len(parts),
        out_specs=whole(),
        name="join",
        compiler_params=pltpu.CompilerParams(vmem_limit_bytes=4 << 20),
    )(*parts)


def stage_orders(wide, narrow):
    wbits = [1 << i for i in range(wide.bit_length() - 1)]
    nbits = [1 << i for i in range(narrow.bit_length() - 1)]
    w = lambda bits: [("wide", b) for b in bits]
    n = [("narrow", b) for b in nbits]
    tail = w(wbits[2:])
    return (w(wbits[:1]) + w(wbits[1:2]) + n + tail, w(wbits[:1]) + n + w(wbits[1:2]) + tail)


def place_of(order, dw, dn):
    place = 0
    for axis, bit in order:
        own = dw if axis == "wide" else dn
        place = place * 2 + (own // bit) % 2
    return place


def traced_place(order, dw, dn):
    place = 0
    for axis, bit in order:
        own = dw if axis == "wide" else dn
        place = place * 2 + (lax.shift_right_logical(own, bit.bit_length() - 1) & 1)
    return place


def weight_products(jobs, held, arrive, me_ref, keep_ref, send_ref, turned_s):
    me_w, me_n = me_ref[0], me_ref[1]
    half = keep_ref.shape[0]

    def store(acc, job, w_first, n_first):
        row_axis, block_rows, block_lanes, targets = job[2:]
        blocks = [
            (bi, bj)
            for bi in range(acc.shape[0] // block_rows)
            for bj in range(acc.shape[1] // block_lanes)
        ]
        bases = [traced_place(t[0], w_first ^ me_w, n_first ^ me_n) for t in targets]
        for core in range(2):

            @pl.when((me_w & 1) == core)
            def _():
                for bi, bj in blocks:
                    w, n = (bi, bj) if row_axis == "wide" else (bj, bi)
                    out_ref = keep_ref if (w & 1) == core else send_ref
                    for (order, first, count, offset), base in zip(targets, bases):
                        at = (base ^ place_of(order, w, n)) & (half - 1)
                        for k in range(block_lanes // 128):
                            lane = bj * block_lanes + k * 128
                            row = bi * block_rows + first
                            out_ref[at, offset + k * count : offset + (k + 1) * count, :] = acc[
                                row : row + count, lane : lane + 128
                            ]

    for job in jobs:
        rg, lg, row_axis, block_rows, block_lanes, targets = job
        arrive(rg)
        arrive(lg)
        row_s, lane_s = held[rg], held[lg]
        depth, rows, lanes = row_s.shape[0], row_s.shape[1], lane_s.shape[1]
        tile_rows = 384
        tile_lanes = block_lanes
        while tile_lanes < 512 and lanes % (2 * tile_lanes) == 0:
            tile_lanes *= 2
        per_row, per_lane = tile_rows // block_rows, tile_lanes // block_lanes

        def row_step(rt, carry):
            mine = row_s[:, pl.ds(pl.multiple_of(rt * tile_rows, 128), tile_rows)]
            if depth > 16:
                turned_s[...] = mine.T

            def lane_step(lt, inner):
                part = lane_s[:, pl.ds(pl.multiple_of(lt * tile_lanes, 128), tile_lanes)]
                acc = product(turned_s[...], part) if depth > 16 else dot_tn(mine, part)
                if row_axis == "wide":
                    store(low(acc), job, rt * per_row, lt * per_lane)
                else:
                    store(low(acc), job, lt * per_lane, rt * per_row)
                return inner

            if lanes == tile_lanes:
                return lane_step(0, carry)
            return lax.fori_loop(0, lanes // tile_lanes, lane_step, carry)

        lax.fori_loop(0, rows // tile_rows, row_step, 0)


def wgrad_kernel(jobs, groups, n_ops, me_ref, *refs):
    ops, (keep_ref, send_ref) = refs[:n_ops], refs[n_ops : n_ops + 2]
    held = refs[n_ops + 2 : n_ops + 2 + len(groups)]
    turned_s, sems = refs[-2:]
    copies = []
    for ids, buf in zip(groups, held):
        first, own = 0, []
        for i in ids:
            count = ops[i].shape[0]
            sem = sems.at[sum(len(c) for c in copies) + len(own)]
            own.append(pltpu.make_async_copy(ops[i], buf.at[first : first + count], sem))
            first += count
        copies.append(own)
    for own in copies:
        for c in own:
            c.start()
    ready = set()

    def arrive(g):
        if g not in ready:
            for c in copies[g]:
                c.wait()
            ready.add(g)

    weight_products(jobs, held, arrive, me_ref, keep_ref, send_ref, turned_s)


def with_blocks(jobs, width, wide, narrow):
    full = []
    for rg, lg, row_axis, targets in jobs:
        split = (wide, narrow) if row_axis == "wide" else (narrow, wide)
        full.append((rg, lg, row_axis, width(rg) // split[0], width(lg) // split[1], targets))
    return full


def wgrad(me, ops, groups, jobs, total_rows, wide, narrow, vmem):
    half = wide * narrow // 2
    width = lambda g: ops[groups[g][0]].shape[1]
    depth = [sum(ops[i].shape[0] for i in g) for g in groups]
    full = with_blocks(jobs, width, wide, narrow)
    flops = sum(2 * depth[j[0]] * width(j[0]) * width(j[1]) for j in full)
    return pl.pallas_call(
        functools.partial(wgrad_kernel, full, groups, len(ops)),
        out_shape=(jax.ShapeDtypeStruct((half, total_rows, 128), BF),) * 2,
        in_specs=[pl.BlockSpec(memory_space=pltpu.SMEM)]
        + [pl.BlockSpec(memory_space=pltpu.HBM)] * len(ops),
        out_specs=(whole(),) * 2,
        scratch_shapes=[pltpu.VMEM((d, width(g)), BF) for g, d in enumerate(depth)]
        + [pltpu.VMEM((384, max(depth)), BF), pltpu.SemaphoreType.DMA((sum(map(len, groups)),))],
        name="wgrad",
        compiler_params=pltpu.CompilerParams(vmem_limit_bytes=vmem << 20),
        cost_estimate=pl.CostEstimate(flops=flops, bytes_accessed=flops // 256, transcendentals=0),
    )(me, *ops)


def swap(a, *stage):
    dw = sum(bit for axis, bit in stage if axis == "wide")
    dn = sum(bit for axis, bit in stage if axis == "narrow")
    wide, narrow = lax.axis_size("wide"), lax.axis_size("narrow")
    if not dn:
        return lax.ppermute(a, "wide", [(i, i ^ dw) for i in range(wide)])
    if not dw:
        return lax.ppermute(a, "narrow", [(i, i ^ dn) for i in range(narrow)])
    pairs = [(i * narrow + j, (i ^ dw) * narrow + (j ^ dn)) for i in range(wide) for j in range(narrow)]
    return lax.ppermute(a, AXES, pairs)


def relatives(stage):
    if len(stage) == 1:
        return [stage]
    return [(stage[1],), (stage[0],), tuple(stage)]


def grouped(order, direct):
    if not direct:
        return [(s,) for s in order]
    return [(s,) for s in order[:-2]] + [tuple(order[-2:])]


class Chunk:
    def __init__(self, keep, send, split, orders, finals, direct=False):
        self.rows, self.split, self.finals = keep.shape[1], split, finals
        self.orders = [grouped(order, direct) for order in orders]
        self.stage, self.parts = 0, [(keep, send)]
        self.done = False

    def spans(self, stage):
        if self.orders[0][stage] == self.orders[1][stage] and (
            stage == 0 or self.orders[0][stage:] == self.orders[1][stage:]
        ):
            return [(0, self.rows, self.orders[0])]
        return [(0, self.split, self.orders[0]), (self.split, self.rows, self.orders[1])]

    def start(self):
        return [
            [swap(a, *to) for a, to in zip(part[1:], relatives(order[self.stage]))]
            for part, (_, _, order) in zip(self.parts, self.spans(self.stage))
        ]


def doubled(value, stages):
    for stage in stages:
        value = value + swap(value, stage)
    return value


def advance(flows):
    operands, shapes, steps = [], [], []
    for f in flows:
        now = f.spans(f.stage)
        last = f.stage == len(f.orders[0]) - 1
        first_in, first_out = len(operands), len(shapes)
        for part, got in zip(f.parts, f.got):
            operands += [part[0]] + got
        half = f.parts[0][0].shape[0] // 2
        if last:
            for kind, offset, rows, lanes in f.finals:
                shapes.append(jax.ShapeDtypeStruct((rows, lanes), F32))
            steps.append(("final", first_in, first_out, f.finals, len(f.got[0])))
        else:
            later = f.spans(f.stage + 1)
            ways = 2 ** len(f.orders[0][f.stage + 1])
            for lo, hi, _ in later:
                shapes += [jax.ShapeDtypeStruct((2 * half // ways, hi - lo, 128), BF)] * ways
            steps.append(
                ("halve", first_in, first_out, [n[:2] for n in now], [n[:2] for n in later], ways)
            )

    def whole_sum(ins, i, count, pick):
        total = pick(ins[i]) + pick(ins[i + 1])
        return total if count == 1 else total + (pick(ins[i + 2]) + pick(ins[i + 3]))

    def body(*refs):
        ins, outs = refs[: len(operands)], refs[len(operands) :]
        for step in steps:
            kind, i, o = step[:3]
            if kind == "final":
                for n, (_, offset, rows, lanes) in enumerate(step[3]):
                    for k in range(lanes // 128):
                        span = pl.ds(offset + k * rows, rows)
                        value = whole_sum(ins, i, step[4], lambda ref: ref[0, span, :].astype(F32))
                        outs[o + n][:, k * 128 : (k + 1) * 128] = value
            else:
                ways = step[5]
                for p, (lo, hi) in enumerate(step[3]):
                    for q, (lo2, hi2) in enumerate(step[4]):
                        a, b = max(lo, lo2), min(hi, hi2)
                        if a >= b:
                            continue
                        keep_ref, got_ref = ins[i + 2 * p], ins[i + 2 * p + 1]
                        count = keep_ref.shape[0] // ways
                        for side in range(ways):
                            out_ref = outs[o + ways * q + side]

                            def block(n, carry):
                                src = pl.ds(a - lo, b - a)
                                value = keep_ref[side * count + n, src, :].astype(F32)
                                value = value + got_ref[side * count + n, src, :].astype(F32)
                                out_ref[n, a - lo2 : b - lo2, :] = low(value)
                                return carry

                            if count == 1:
                                block(0, 0)
                            else:
                                lax.fori_loop(0, count, block, 0)

    room = (1 << 20) + sum(a.size * a.dtype.itemsize for a in operands + shapes)
    outs = pl.pallas_call(
        body,
        out_shape=tuple(shapes),
        in_specs=[whole()] * len(operands),
        out_specs=(whole(),) * len(shapes),
        name="advance",
        compiler_params=pltpu.CompilerParams(vmem_limit_bytes=room),
    )(*operands)
    at = 0
    for f, step in zip(flows, steps):
        f.stage += 1
        if step[0] == "final":
            f.result = [
                out.T if final[0] == "turn" else out
                for out, final in zip(outs[at : at + len(step[3])], step[3])
            ]
            at += len(step[3])
            f.done = True
        else:
            ways = step[5]
            f.parts = [tuple(outs[at + ways * q : at + ways * (q + 1)]) for q in range(len(step[4]))]
            at += ways * len(step[4])


def exchange(begin, compute, inputs):
    sent, inputs = lax.optimization_barrier(([f.parts for f in begin], inputs))
    for f, value in zip(begin, sent):
        f.parts = value
    for f in begin:
        f.got = f.start()
    got, made = lax.optimization_barrier(([f.got for f in begin], compute(*inputs)))
    for f, value in zip(begin, got):
        f.got = value
    advance(begin)
    return made


def gather_stages(order):
    far, near = order[3:], order[1:3]
    return [far[i : i + 2] for i in range(0, len(far), 2)] + [near] + [order[:1]]


def gather_all(rows, stages):
    for stage in stages[:-1]:
        got = [swap(rows, *to) for to in ([stage] if len(stage) == 1 else [stage[:1], stage[1:], stage])]
        rows = join(rows, *got)
    return rows, swap(rows, *stages[-1])


def local(
    wide,
    narrow,
    query_x,
    query_seg,
    passage_x,
    passage_seg,
    labels,
    lookup,
    softness,
    bias_grid,
    gains,
    wq,
    wk,
    wv,
    wo,
    wg,
    wu,
    wd,
    wp,
):
    qrows, qlen, feat = query_x.shape
    prows, plen, _ = passage_x.shape
    buckets, heads = bias_grid.shape
    order_a, order_b = stage_orders(wide, narrow)
    me_w, me_n = lax.axis_index("wide"), lax.axis_index("narrow")
    me = jnp.stack([me_w, me_n]).astype(jnp.int32)

    hidden = wd.shape[0]
    block, cols, ff_block, ff_cols = feat // wide, feat // narrow, hidden // wide, hidden // narrow
    matrices = (wq, wk, wv, wo, wg, wu, wd, wp)
    (packed, vectors, e, pooled, x_between, x_last), (first, second) = forward(
        query_x.reshape(-1, feat),
        passage_x.reshape(-1, feat),
        lookup,
        bias_grid.T,
        query_seg,
        passage_seg,
        gains,
        labels,
        matrices,
    )
    down_rows, att_rows = block * ff_cols // 128, block * cols // 128
    jobs = None
    if not (cols % 128 or ff_block % 128 or block % 16):
        jobs = [
            (0, 1, "wide", [(order_a, 0, block, 0)]),
            (2, 3, "narrow", [(order_b, 0, cols, down_rows)]),
        ]
    groups = gather_stages(order_a)
    stages = [bit for group in groups for bit in group]
    here, there = gather_all(packed, groups)
    (gain_final, loss_part, grad_e, gain_mid, gain_in), back, parts = loss_and_back(
        me, narrow, stages, softness, here, there, e, gains, query_seg, passage_seg,
        x_last, x_between, first, second, matrices, wide, jobs, (down_rows, cols),
    )
    grad_b, grad_b_2 = back["gb1"], back["gb"]
    att_2 = (back["gy"], back["gq"], back["gk"], back["gv"])
    h, o, normed, u = (first[name] for name in ("h", "o", "normed", "u"))
    h_2, o_2, normed_2, u_2 = (second[name] for name in ("h", "o", "normed", "u"))

    def split_sums(value):
        return value[:3], value[4 : 4 + heads, :buckets], value[3, :1]

    def finish(grad_a, grad_b):
        return rest_back(
            gains, lookup, buckets, (gain_in, gain_mid, gain_final, loss_part), grad_a, grad_b,
            back["grad_x"], back["ds"], first, matrices, query_x.reshape(-1, feat), passage_x.reshape(-1, feat),
        )

    if jobs is None:
        grad_f, grad_a = back["grad_f1"], back["ga1"]
        ffn_2 = (back["grad_f"], back["ga"], grad_b_2)
        sums, grad_y, grad_q, grad_k, grad_v, grad_x = finish(grad_a, grad_b)
        outs = split_sums(doubled(sums, order_a))

        def scatter(*pairs):
            full = low(sum(dot_tn(left, right) for left, right in pairs))
            full = lax.psum_scatter(full, "wide", scatter_dimension=1, tiled=True)
            return lax.psum_scatter(full, "narrow", scatter_dimension=0, tiled=True).astype(F32)

        grad_query = scatter((h, grad_q), (h_2, att_2[1]))
        grad_key = scatter((h, grad_k), (h_2, att_2[2]))
        grad_value = scatter((h, grad_v), (h_2, att_2[3]))
        grad_out = scatter((o, grad_y), (o_2, att_2[0]))
        grad_gate = scatter((normed, grad_a), (normed_2, ffn_2[1]))
        grad_up = scatter((normed, grad_b), (normed_2, ffn_2[2]))
        grad_down = scatter((u, grad_f), (u_2, ffn_2[0]))
        grad_proj = scatter((pooled, grad_e))
    else:
        orders = (order_a, order_b)
        finals = [("turn", 0, block, ff_cols), ("keep", down_rows, cols, ff_block)]
        ffn = Chunk(*parts, down_rows, orders, finals)

        cut = (cols + att_rows) // 2 // 16 * 16

        def make_up(grad_b, grad_b_2):
            return wgrad(
                me,
                [normed, normed_2, grad_b, grad_b_2, grad_e, pooled],
                [(0, 1), (2, 3), (4,), (5,)],
                [
                    (2, 3, "wide", [(order_b, 0, block, cols)]),
                    (0, 1, "narrow", [(order_a, 0, cut, 0), (order_b, cut, cols - cut, cut)]),
                ],
                cols + att_rows,
                wide,
                narrow,
                52,
            )

        parts = exchange([ffn], make_up, (grad_b, grad_b_2))
        finals = [("keep", 0, cols, ff_block), ("turn", cols, block, cols)]
        up = Chunk(*parts, cut, orders, finals)

        sums, *grads, grad_x = exchange([ffn, up], finish, (back["ga1"], grad_b))

        def make_rest(sums, grad_y, grad_q, grad_k, grad_v):
            got = swap(sums, order_a[-2])
            parts = wgrad(
                me,
                [grad_y, att_2[0], o, o_2, grad_q, att_2[1], h, h_2, grad_k, att_2[2], grad_v, att_2[3]],
                [(0, 1), (2, 3), (4, 5), (6, 7), (8, 9), (10, 11)],
                [
                    (0, 1, "wide", [(order_a, 0, block, 0)]),
                    (2, 3, "wide", [(order_a, 0, block, att_rows)]),
                    (4, 3, "wide", [(order_b, 0, block, 2 * att_rows)]),
                    (5, 3, "wide", [(order_b, 0, block, 3 * att_rows)]),
                ],
                4 * att_rows,
                wide,
                narrow,
                12,
            )
            got, parts = lax.optimization_barrier((got, parts))
            return parts, sums + got

        parts, sums = exchange([ffn, up], make_rest, (sums, *grads))
        att = Chunk(*parts, 2 * att_rows, orders, [("turn", i * att_rows, block, cols) for i in range(4)], True)
        for stage in order_a[-1:] + order_a[:2]:
            live = [f for f in (att, up, ffn) if not f.done]
            sums = exchange(live, lambda value: doubled(value, [stage]), (sums,))
        outs = exchange([att], lambda value: split_sums(doubled(value, order_a[2:-2])), (sums,))
        grad_down, grad_gate = ffn.result
        grad_up, grad_proj = up.result
        grad_out, grad_query, grad_key, grad_value = att.result
    gain_total, bucket_total, loss_total = outs
    mean_loss = loss_total / (qrows * QSEGS * wide * narrow)
    return (
        mean_loss,
        vectors[:QSEGS],
        vectors[QSEGS : QSEGS + PSEGS],
        grad_x[:qlen].reshape(1, qlen, feat),
        grad_x[qlen:].reshape(1, plen, feat),
        gain_total,
        bucket_total.T,
        grad_query,
        grad_key,
        grad_value,
        grad_out,
        grad_gate,
        grad_up,
        grad_down,
        grad_proj,
    )


def solution(mesh):
    rows3, rows2, rows1 = P(AXES, None, None), P(AXES, None), P(AXES)
    return jax.shard_map(
        functools.partial(local, mesh.shape["wide"], mesh.shape["narrow"]),
        mesh=mesh,
        in_specs=(rows3, rows2, rows3, rows2, rows1) + (P(),) * 12,
        out_specs=(P(), rows2, rows2, rows3, rows3, P(), P()) + (P("narrow", "wide"),) * 8,
        check_vma=False,
    )
```

```python
import functools

import jax
import jax.numpy as jnp
from jax import lax
from jax.experimental import pallas as pl
from jax.experimental.pallas import tpu as pltpu
from jax.sharding import PartitionSpec as P

LAYERS = 2
QSEGS = 3
PSEGS = 4
HDIM = 64
PACK = 8

HIGHEST = lax.Precision.HIGHEST
EPSILON = 1e-06
MASKED = -1000000000.0
BF = jnp.bfloat16
F32 = jnp.float32
AXES = ("wide", "narrow")


def low(a):
    return a.astype(BF)


def product(a, b):
    return jnp.dot(a, b, preferred_element_type=F32)


def dot_tn(a, b, precision=None):
    return lax.dot_general(
        a, b, (((0,), (0,)), ((), ())), preferred_element_type=F32, precision=precision
    )


def dot_nt(a, b, precision=None):
    return lax.dot_general(
        a, b, (((1,), (1,)), ((), ())), preferred_element_type=F32, precision=precision
    )


def whole():
    return pl.BlockSpec(memory_space=pltpu.VMEM)


def bias_kernel(qlen, plen, lookup_ref, grid_ref, qseg_ref, pseg_ref, pbias_ref, qbias_ref, wide_s, short_s):
    heads, buckets = grid_ref.shape
    width = 2 * plen
    wide_s[...] = jnp.full((1, width), -1, jnp.int32)
    wide_s[:, : lookup_ref.shape[1]] = lookup_ref[...]
    onehot = (
        lax.broadcasted_iota(jnp.int32, (buckets, width), 0)
        == jnp.broadcast_to(wide_s[...], (buckets, width))
    ).astype(F32)
    table = jnp.dot(grid_ref[...], onehot, precision=HIGHEST, preferred_element_type=F32)
    pcol = jnp.transpose(jnp.broadcast_to(pseg_ref[...], (plen, plen)))
    psame = pcol == jnp.broadcast_to(pseg_ref[...], (plen, plen))
    short_s[...] = jnp.full((1, 128), -1, jnp.int32)
    short_s[:, :qlen] = qseg_ref[...]
    qcol = jnp.transpose(jnp.broadcast_to(short_s[...], (128, 128)))
    qsame = (qcol == jnp.broadcast_to(short_s[...], (128, 128)))[:qlen, :qlen]
    for head in range(heads):
        rows = jnp.broadcast_to(table[head : head + 1, :], (plen, width))
        rolled = pltpu.roll(rows, width - (plen - 1), 1, stride=1, stride_axis=0)
        block = rolled[:, :plen]
        pbias_ref[head] = jnp.where(psame, block, MASKED)
        qbias_ref[head] = jnp.where(qsame, block[:qlen, :qlen], MASKED)


def half_mask(lanes, side):
    return (lax.broadcasted_iota(jnp.int32, (1, lanes), 1) // HDIM) == side


def attend_kernel(qlen, q_ref, k_ref, v_ref, pbias_ref, qbias_ref, o_ref, pp_ref, pq_ref):
    pairs = q_ref.shape[1] // 128
    spans = ((0, qlen, qbias_ref, pq_ref), (qlen, q_ref.shape[0] - qlen, pbias_ref, pp_ref))

    def pair(i, carry):
        lanes = pl.ds(pl.multiple_of(i * 128, 128), 128)
        for start, length, bias_ref, keep_ref in spans:
            rows = pl.ds(start, length)
            q2, k2, v2 = q_ref[rows, lanes], k_ref[rows, lanes], v_ref[rows, lanes]
            total = None
            for side in range(2):
                mine = half_mask(128, side)
                zero = jnp.zeros_like(k2)
                s = dot_nt(q2, jnp.where(mine, k2, zero)) + bias_ref[2 * i + side]
                top = jnp.max(s, axis=-1, keepdims=True)
                e = jnp.exp(s - top)
                p = low(e * (1.0 / jnp.sum(e, axis=-1, keepdims=True)))
                keep_ref[2 * i + side] = p
                part = product(p, jnp.where(mine, v2, zero))
                total = part if total is None else total + part
            o_ref[rows, lanes] = low(total)
        return carry

    lax.fori_loop(0, pairs, pair, 0, unroll=3)


def attend_back_kernel(
    qlen, q_ref, k_ref, v_ref, o_ref, go_ref, pp_ref, pq_ref, acc_ref, gq_ref, gk_ref, gv_ref, ds_ref
):
    pairs = q_ref.shape[1] // 128
    plen = q_ref.shape[0] - qlen

    def pair(i, carry):
        lanes = pl.ds(pl.multiple_of(i * 128, 128), 128)
        for start, length, keep_ref in ((qlen, plen, pp_ref), (0, qlen, pq_ref)):
            rows = pl.ds(start, length)
            q2, k2, v2 = q_ref[rows, lanes], k_ref[rows, lanes], v_ref[rows, lanes]
            o2, go2 = o_ref[rows, lanes], go_ref[rows, lanes]
            prod = o2.astype(F32) * go2.astype(F32)
            gq, gk, gv = None, None, None
            for side in range(2):
                mine = half_mask(128, side)
                zero = jnp.zeros_like(k2)
                p = keep_ref[2 * i + side]
                gp = dot_nt(go2, jnp.where(mine, v2, zero))
                delta = jnp.sum(jnp.where(mine, prod, 0.0), axis=-1, keepdims=True)
                ds = p.astype(F32) * (gp - delta)
                if start == qlen:
                    if acc_ref is None:
                        ds_ref[2 * i + side] = ds
                    else:
                        ds_ref[2 * i + side] = ds + acc_ref[2 * i + side]
                else:
                    ds_ref[2 * i + side, :length, :length] += ds
                dsl = low(ds)
                a = product(dsl, jnp.where(mine, k2, zero))
                b = dot_tn(dsl, jnp.where(mine, q2, zero))
                c = dot_tn(p, jnp.where(mine, go2, zero))
                gq = a if gq is None else gq + a
                gk = b if gk is None else gk + b
                gv = c if gv is None else gv + c
            gq_ref[rows, lanes] = low(gq)
            gk_ref[rows, lanes] = low(gk)
            gv_ref[rows, lanes] = low(gv)
        return carry

    lax.fori_loop(0, pairs, pair, 0, unroll=2)


def small_kernel(
    buckets, ds_ref, lookup_ref, in_ref, mid_ref, final_ref, loss_ref, out_ref, diag_ref, wide_s
):
    heads, plen, _ = ds_ref.shape
    out_ref[...] = jnp.zeros_like(out_ref)
    out_ref[0:1, :] = in_ref[...]
    out_ref[1:2, :] = mid_ref[...]
    out_ref[2:3, :] = final_ref[...]
    out_ref[3:4, :128] = loss_ref[...]
    width = 2 * plen
    wide_s[...] = jnp.full((1, width), -1, jnp.int32)
    wide_s[:, : lookup_ref.shape[1]] = lookup_ref[...]
    for head in range(heads):
        block = ds_ref[head]
        wide_block = jnp.concatenate([block, jnp.zeros_like(block)], axis=1)
        rows = plen
        while rows > 8:
            rows //= 2
            wide_block = wide_block[:rows] + pltpu.roll(wide_block[rows:], width - rows, 1)
        at = lax.broadcasted_iota(jnp.int32, (8, width), 0)
        for bit in (4, 2, 1):
            moved = pltpu.roll(wide_block, width - bit, 1)
            wide_block = jnp.where((at & bit) != 0, moved, wide_block)
        rolled = pltpu.roll(wide_block, plen - 1, 1)
        diag_ref[head : head + 1, :] = jnp.sum(rolled, axis=0, keepdims=True)
    onehot = (
        lax.broadcasted_iota(jnp.int32, (buckets, width), 0)
        == jnp.broadcast_to(wide_s[...], (buckets, width))
    ).astype(F32)
    out_ref[4 : 4 + heads, :buckets] = dot_nt(diag_ref[...], onehot, HIGHEST)


def segment_table(seg_ref, first):
    rows, length = PACK, seg_ref.shape[1]
    slot = lax.broadcasted_iota(jnp.int32, (rows, length), 0)
    return (slot == jnp.broadcast_to(seg_ref[...], (rows, length)) + first).astype(F32)


def pool_kernel(
    x_ref, gain_ref, qseg_ref, pseg_ref, label_ref, wp_ref, packed_ref, vec_ref, e_ref, pooled_ref
):
    qlen = qseg_ref.shape[1]
    x = x_ref[...]
    z = x * lax.rsqrt(jnp.mean(x * x, axis=-1, keepdims=True) + EPSILON) * gain_ref[...]
    qt, pt = segment_table(qseg_ref, 0), segment_table(pseg_ref, QSEGS)
    sizes = jnp.sum(qt, axis=1, keepdims=True) + jnp.sum(pt, axis=1, keepdims=True)
    sums = jnp.dot(qt, z[:qlen], precision=HIGHEST, preferred_element_type=F32) + jnp.dot(
        pt, z[qlen:], precision=HIGHEST, preferred_element_type=F32
    )
    pooled = low(sums / jnp.maximum(sizes, 1.0))
    pooled_ref[...] = pooled
    e = product(pooled, wp_ref[...])
    e_ref[...] = e
    vec = e * lax.rsqrt(jnp.sum(e * e, axis=-1, keepdims=True) + EPSILON)
    vec_ref[...] = vec
    at = lax.broadcasted_iota(jnp.int32, vec.shape, 1)
    row = lax.broadcasted_iota(jnp.int32, vec.shape, 0)
    code = jnp.zeros(vec.shape, F32)
    for i in range(QSEGS):
        label = label_ref[i]
        high = lax.shift_right_logical(label, 5).astype(F32)
        rest = (label & 31).astype(F32)
        code = jnp.where(at == i, high, jnp.where(at == QSEGS + i, rest, code))
    packed_ref[...] = low(jnp.where(row == PACK - 1, code, vec))


SLOPE = 0.7978845608028654
CUBE = 0.044715
SAVED = ("h", "q", "k", "v", "pp", "pq", "o", "x_mid", "normed", "da", "db", "u")


def unit_scale(x):
    return lax.rsqrt(jnp.mean(x * x, axis=-1, keepdims=True) + EPSILON)


def gated_parts(a, b):
    square = a * a
    th = jnp.tanh(a * (SLOPE + (SLOPE * CUBE) * square))
    half = 0.5 + 0.5 * th
    value = a * half
    slope = half + (0.5 * a) * (1.0 - th * th) * (SLOPE + (3.0 * SLOPE * CUBE) * square)
    return low(value * b), low(b * slope), low(value)


def forward_kernel(qlen, plen, n_tiles, *refs):
    (qx_ref, px_ref, lookup_ref, grid_ref, qseg_ref, pseg_ref, gains_ref, label_ref), refs = refs[:8], refs[8:]
    hbm, refs = refs[:8], refs[8:]
    packed_ref, vec_ref, e_ref, pooled_ref, x_mid_out, x_out = refs[:6]
    refs = refs[6:]
    outs = [dict(zip(SAVED, refs[n * len(SAVED) : (n + 1) * len(SAVED)])) for n in range(LAYERS)]
    refs = refs[LAYERS * len(SAVED) :]
    held, refs = refs[:8], refs[8:]
    keep, refs = dict(zip(SAVED, refs[: len(SAVED)])), refs[len(SAVED) :]
    x_s, pbias_s, qbias_s, wide_s, short_s, in_sem, out_sem, x_sem = refs
    wq_s, wk_s, wv_s, wo_s, wg_s, wu_s, wd_s, wp_s = held
    fetch = [pltpu.make_async_copy(a, b, in_sem.at[i]) for i, (a, b) in enumerate(zip(hbm, held))]
    for c in fetch:
        c.start()
    x_s[0, :qlen] = qx_ref[...].astype(F32)
    x_s[0, qlen:] = px_ref[...].astype(F32)
    bias_kernel(qlen, plen, lookup_ref, grid_ref, qseg_ref, pseg_ref, pbias_s, qbias_s, wide_s, short_s)

    def write(n, name):
        i = n * len(SAVED) + SAVED.index(name)
        return pltpu.make_async_copy(keep[name].at[n], outs[n][name], out_sem.at[i])

    def send(layer, *names):
        for n in range(LAYERS):

            @pl.when(layer == n)
            def _():
                for name in names:
                    write(n, name).start()

    def arrive(layer, *ids):
        @pl.when(layer == 0)
        def _():
            for i in ids:
                fetch[i].wait()

    def layer_step(layer, carry):
        x = x_s[layer]
        h = low(x * unit_scale(x) * gains_ref[0:1, :])
        keep["h"][layer] = h
        for i, (name, w) in enumerate((("q", wq_s), ("k", wk_s), ("v", wv_s))):
            arrive(layer, i)
            keep[name][layer] = low(product(h, w[...]))
        send(layer, "h", "q", "k", "v")
        at = {name: keep[name].at[layer] for name in SAVED}
        attend_kernel(qlen, at["q"], at["k"], at["v"], pbias_s, qbias_s, at["o"], at["pp"], at["pq"])
        send(layer, "o", "pp", "pq")
        arrive(layer, 3)
        x_mid = x_s[layer] + product(at["o"][...], wo_s[...])
        at["x_mid"][...] = x_mid
        normed = low(x_mid * unit_scale(x_mid) * gains_ref[1:2, :])
        at["normed"][...] = normed
        send(layer, "x_mid", "normed")
        arrive(layer, 4, 5)
        size = wg_s.shape[1] // n_tiles
        for t in range(n_tiles):
            lanes = slice(t * size, (t + 1) * size)
            a = product(normed, wg_s[:, lanes])
            b = product(normed, wu_s[:, lanes])
            u, da, db = gated_parts(a, b)
            at["u"][:, lanes] = u
            at["da"][:, lanes] = da
            at["db"][:, lanes] = db
        send(layer, "u", "da", "db")
        arrive(layer, 6)
        x_s[layer + 1] = at["x_mid"][...] + product(at["u"][...], wd_s[...])
        return carry

    lax.fori_loop(0, LAYERS, layer_step, 0)
    inner = pltpu.make_async_copy(x_s.at[1], x_mid_out, x_sem.at[0])
    outer = pltpu.make_async_copy(x_s.at[LAYERS], x_out, x_sem.at[1])
    inner.start()
    outer.start()
    fetch[7].wait()
    pool_kernel(
        x_s.at[LAYERS], gains_ref.at[2:3], qseg_ref, pseg_ref, label_ref, wp_s, packed_ref, vec_ref, e_ref, pooled_ref
    )
    for n in range(LAYERS):
        for name in SAVED:
            write(n, name).wait()
    inner.wait()
    outer.wait()


def saved_shapes(total, qlen, plen, feat, hidden, heads):
    tok, ff = ((total, feat), BF), ((total, hidden), BF)
    kinds = dict(h=tok, q=tok, k=tok, v=tok, o=tok, normed=tok, da=ff, db=ff, u=ff)
    kinds["pp"], kinds["pq"] = ((heads, plen, plen), BF), ((heads, qlen, qlen), BF)
    kinds["x_mid"] = ((total, feat), F32)
    return [kinds[name] for name in SAVED]


def forward(qx, px, lookup, grid, qseg, pseg, gains, labels, matrices):
    qlen, feat = qx.shape
    plen, heads, hidden = px.shape[0], grid.shape[0], matrices[4].shape[1]
    total = qlen + plen
    kinds = saved_shapes(total, qlen, plen, feat, hidden, heads)
    small = (PACK, feat)
    shapes = [(small, BF), (small, F32), (small, F32), (small, BF), ((total, feat), F32), ((total, feat), F32)]
    shapes += kinds * LAYERS
    anywhere = pl.BlockSpec(memory_space=pltpu.HBM)
    smem = pl.BlockSpec(memory_space=pltpu.SMEM)
    weights = sum(m.size for m in matrices)
    outs = pl.pallas_call(
        functools.partial(forward_kernel, qlen, plen, 4),
        out_shape=tuple(jax.ShapeDtypeStruct(*s) for s in shapes),
        in_specs=[whole()] * 7 + [smem] + [anywhere] * 8,
        out_specs=(whole(),) * 4 + (anywhere,) * (2 + LAYERS * len(SAVED)),
        scratch_shapes=[pltpu.VMEM(m.shape, BF) for m in matrices]
        + [pltpu.VMEM((LAYERS,) + shape, dtype) for shape, dtype in kinds]
        + [
            pltpu.VMEM((LAYERS + 1, total, feat), F32),
            pltpu.VMEM((heads, plen, plen), F32),
            pltpu.VMEM((heads, qlen, qlen), F32),
            pltpu.VMEM((1, 2 * plen), jnp.int32),
            pltpu.VMEM((1, 128), jnp.int32),
            pltpu.SemaphoreType.DMA((8,)),
            pltpu.SemaphoreType.DMA((LAYERS * len(SAVED),)),
            pltpu.SemaphoreType.DMA((2,)),
        ],
        name="forward",
        compiler_params=pltpu.CompilerParams(vmem_limit_bytes=56 << 20),
        cost_estimate=pl.CostEstimate(
            flops=2 * LAYERS * total * weights, bytes_accessed=2 * weights, transcendentals=LAYERS * total * hidden
        ),
    )(qx, px, lookup[None], grid, qseg, pseg, gains, labels, *matrices)
    saved = [dict(zip(SAVED, outs[6 + n * len(SAVED) : 6 + (n + 1) * len(SAVED)])) for n in range(LAYERS)]
    return outs[:6], saved


def loss_kernel(
    narrow, stages, me_ref, sharp_ref, here_ref, there_ref, e_ref, x_ref, gain_ref,
    qseg_ref, pseg_ref, wp_ref, gx_ref, ggain_ref, loss_ref, ge_ref, flat_s,
):
    half = here_ref.shape[0]
    flat_s[:half, :] = here_ref[...]
    flat_s[half:, :] = there_ref[...]
    size = 2 * half
    tile = min(size, 256)
    sharp = sharp_ref[0]
    lane = lax.broadcasted_iota(jnp.int32, (1, size), 1)
    block, slot = lax.shift_right_logical(lane, 3), lane & (PACK - 1)
    dw, dn = jnp.zeros_like(block), jnp.zeros_like(block)
    for k, (axis, bit) in enumerate(stages):
        on = (lax.shift_right_logical(block, k) & 1) * bit
        dw, dn = (dw + on, dn) if axis == "wide" else (dw, dn + on)
    device = (dw ^ me_ref[0]) * narrow + (dn ^ me_ref[1])
    is_passage = (slot >= QSEGS) & (slot < QSEGS + PSEGS)
    document = jnp.where(is_passage, device * PSEGS + slot - QSEGS, -2)
    row = lax.broadcasted_iota(jnp.int32, (tile, 1), 0)
    row_slot = row & (PACK - 1)
    is_query = row_slot < QSEGS
    across = lax.broadcasted_iota(jnp.int32, (tile, tile), 1)
    source = low((across == row - row_slot + PACK - 1).astype(F32))
    place = lax.broadcasted_iota(jnp.int32, (tile, 128), 1)
    weigh = jnp.where(place == row_slot, 32.0, 0.0) + jnp.where(place == row_slot + QSEGS, 1.0, 0.0)
    mine = lax.broadcasted_iota(jnp.int32, (1, 128), 1) < PACK
    grad = None
    for t in range(size // tile):
        rows = flat_s[t * tile : (t + 1) * tile, :]
        match = dot_nt(rows, flat_s[...]) / sharp
        match = jnp.where(is_passage, match, MASKED)
        label = jnp.sum(product(source, rows[:, :128]) * weigh, axis=1, keepdims=True)
        hit = (label.astype(jnp.int32) == document) & is_query
        top = jnp.max(match, axis=1, keepdims=True)
        ex = jnp.exp(match - top)
        line = jnp.sum(ex, axis=1, keepdims=True)
        g = (ex / line - hit.astype(F32)) / sharp
        g = low(jnp.where(is_query & is_passage, g, 0.0))
        back = dot_tn(jnp.where(mine, g[:, :128], jnp.zeros_like(g[:, :128])), rows)[:PACK]
        if t == 0:
            part = jnp.sum(jnp.where(hit, match, 0.0), axis=1, keepdims=True)
            part = jnp.where(is_query & (row < PACK), top + jnp.log(line) - part, 0.0)
            loss_ref[...] = jnp.broadcast_to(jnp.sum(part, axis=0, keepdims=True), loss_ref.shape)
            grad = product(g[:16], flat_s[...])[:PACK]
        grad = grad + back
    e = e_ref[...]
    scale = lax.rsqrt(jnp.sum(e * e, axis=-1, keepdims=True) + EPSILON)
    vec = e * scale
    ge = low((grad - vec * jnp.sum(vec * grad, axis=-1, keepdims=True)) * scale)
    ge_ref[...] = ge
    qt, pt = segment_table(qseg_ref, 0), segment_table(pseg_ref, QSEGS)
    sizes = jnp.sum(qt, axis=1, keepdims=True) + jnp.sum(pt, axis=1, keepdims=True)
    pooled = dot_nt(ge, wp_ref[...]) / jnp.maximum(sizes, 1.0)
    qlen = qseg_ref.shape[1]
    gain = gain_ref[...]
    total = None
    for table, start, count in ((qt, 0, qlen), (pt, qlen, pseg_ref.shape[1])):
        gz = dot_tn(table, pooled, HIGHEST)
        x = x_ref[start : start + count, :]
        r = lax.rsqrt(jnp.mean(x * x, axis=-1, keepdims=True) + EPSILON)
        unit = x * r
        scaled = gz * gain
        gx_ref[start : start + count, :] = r * (
            scaled - unit * jnp.mean(unit * scaled, axis=-1, keepdims=True)
        )
        part = jnp.sum(gz * unit, axis=0, keepdims=True)
        total = part if total is None else total + part
    ggain_ref[...] = total


PAIRED = ("grad_f", "ga", "grad_f1", "ga1")
BACK = ("grad_f", "ga", "gb", "gy", "gq", "gk", "gv", "ds", "grad_f1", "ga1", "gb1", "grad_x")


def through_norm(x, gain, grad):
    r = unit_scale(x)
    unit = x * r
    scaled = grad * gain
    back = r * (scaled - unit * jnp.mean(unit * scaled, axis=-1, keepdims=True))
    return back, jnp.sum(grad * unit, axis=0, keepdims=True)


def back_kernel(narrow, stages, qlen, n_tiles, n_held, names, jobs, job_rows, *refs):
    me_ref, sharp_ref, here_ref, there_ref, e_ref, gains_ref, qseg_ref, pseg_ref = refs[:8]
    refs = refs[8:]
    n_fetch = n_held + (4 if jobs else 0)
    hbm, refs = refs[:n_fetch], refs[n_fetch:]
    ggain_ref, loss_ref, ge_ref, gmid_ref, gin_ref = refs[:5]
    outs, refs = dict(zip(names, refs[5 : 5 + len(names)])), refs[5 + len(names) :]
    if jobs:
        (keep_ref, send_ref), refs = refs[:2], refs[2:]
    held, refs = list(refs[: n_held - 4]), refs[n_held - 4 :]
    singles = [n for n in BACK if n not in PAIRED and n != "grad_x"]
    keep, refs = dict(zip(singles, refs[: len(singles)])), refs[len(singles) :]
    gf_s, ga_s, wide_s, row_s, flat_s, gx_s, go_s, in_sem, out_sem = refs[:9]
    total = gx_s.shape[0]
    keep["grad_x"] = gx_s
    halves = [buf.at[i * total : (i + 1) * total] for buf in (wide_s, row_s) for i in range(2)]
    held = held[:3] + halves[:2] + held[3:7] + halves[2:] + held[7:] + halves
    for i, (name, buf) in enumerate((("grad_f1", gf_s), ("ga1", ga_s), ("grad_f", gf_s), ("ga", ga_s))):
        keep[name] = buf.at[i // 2 * total : (i // 2 + 1) * total]
    fetch = [pltpu.make_async_copy(a, b, in_sem.at[i]) for i, (a, b) in enumerate(zip(hbm, held))]
    for c in fetch[:21]:
        c.start()
    (x2_s, wp_s, wd_s, da_s, db_s, wg_s, wu_s, xm_s, wo_s, v_s, o_s, pp_s, k_s, q_s, pq_s) = held[:15]
    wq_s, wk_s, wv_s, x_s, da1_s, db1_s = held[15:21]

    def write(name):
        return pltpu.make_async_copy(keep[name], outs[name], out_sem.at[names.index(name)])

    def send(*ready):
        for name in ready:
            if name in outs:
                write(name).start()

    fetch[0].wait()
    fetch[1].wait()
    loss_kernel(
        narrow, stages, me_ref, sharp_ref, here_ref, there_ref, e_ref, x2_s, gains_ref.at[2:3],
        qseg_ref, pseg_ref, wp_s, gx_s, ggain_ref, loss_ref, ge_ref, flat_s,
    )

    def gated_back(x_ref, da, db, made):
        grad_f = low(x_ref[...])
        keep[made[0]][...] = grad_f
        size = da.shape[1] // n_tiles
        for t in range(n_tiles):
            lanes = slice(t * size, (t + 1) * size)
            gu = dot_nt(grad_f, wd_s[lanes, :])
            keep[made[1]][:, lanes] = low(gu * da[:, lanes].astype(F32))
            keep[made[2]][:, lanes] = low(gu * db[:, lanes].astype(F32))
        send(*made)

    for i in (2, 3, 4):
        fetch[i].wait()
    gated_back(gx_s, da_s, db_s, BACK[:3])
    for c in fetch[21:23]:
        c.start()
    for i in (5, 6, 7):
        fetch[i].wait()
    grad = dot_nt(keep["ga"][...], wg_s[...]) + dot_nt(keep["gb"][...], wu_s[...])
    back, gmid_ref[...] = through_norm(xm_s[...], gains_ref[1:2, :], grad)
    grad_mid = gx_s[...] + back
    gx_s[...] = grad_mid
    gy = low(grad_mid)
    keep["gy"][...] = gy
    send("gy")
    fetch[8].wait()
    go_s[...] = low(dot_nt(gy, wo_s[...]))
    for i in range(9, 15):
        fetch[i].wait()
    attend_back_kernel(
        qlen, q_s, k_s, v_s, o_s, go_s, pp_s, pq_s, None, keep["gq"], keep["gk"], keep["gv"], keep["ds"]
    )
    send("gq", "gk", "gv", "ds")
    for c in fetch[23:]:
        c.start()
    for i in range(15, 19):
        fetch[i].wait()
    grad = dot_nt(keep["gq"][...], wq_s[...]) + dot_nt(keep["gk"][...], wk_s[...])
    grad = grad + dot_nt(keep["gv"][...], wv_s[...])
    back, gin_ref[...] = through_norm(x_s[...], gains_ref[0:1, :], grad)
    gx_s[...] = gx_s[...] + back
    send("grad_x")
    fetch[19].wait()
    fetch[20].wait()
    gated_back(gx_s, da1_s, db1_s, BACK[8:11])
    if jobs:
        for i in range(21, 25):
            fetch[i].wait()
        turned_s, keep_s, send_s, block_sem = refs[9:]
        first_row, moves = 0, []
        for i, (job, rows) in enumerate(zip(jobs, job_rows)):
            weight_products(
                [job], (gf_s, wide_s, row_s, ga_s), lambda g: None, me_ref, keep_s, send_s, turned_s
            )
            span = pl.ds(first_row, rows)
            for j, (a, b) in enumerate(((send_s, send_ref), (keep_s, keep_ref))):
                move = pltpu.make_async_copy(a.at[:, span], b.at[:, span], block_sem.at[2 * i + j])
                move.start()
                moves.append(move)
            first_row += rows
        for move in moves:
            move.wait()
    for name in names:
        write(name).wait()


def loss_and_back(me, narrow, stages, sharp, here, there, e, gains, qseg, pseg, x_last, x_in, first, second, matrices, wide, jobs, job_rows):
    wq, wk, wv, wo, wg, wu, wd, wp = matrices
    total, feat = x_last.shape
    qlen, plen = qseg.shape[1], pseg.shape[1]
    heads, hidden = second["pp"].shape[0], wd.shape[0]
    size = 2 * here.shape[0]
    t = second
    fetched = [x_last, wp, wd, t["da"], t["db"], wg, wu, t["x_mid"], wo, t["v"], t["o"], t["pp"], t["k"], t["q"], t["pq"]]
    fetched += [wq, wk, wv, x_in, first["da"], first["db"]]
    tok, ff = ((total, feat), BF), ((total, hidden), BF)
    kinds = [tok, ff, ff, tok, tok, tok, tok, ((heads, plen, plen), F32), tok, ff, ff, ((total, feat), F32)]
    kinds = dict(zip(BACK, kinds))
    names = [n for n in BACK if not (jobs and n in ("grad_f", "ga", "grad_f1"))]
    held = [pltpu.VMEM(a.shape, a.dtype) for i, a in enumerate(fetched) if i not in (3, 4, 9, 10)]
    n_held = len(fetched)
    blocks, late = [], []
    if jobs:
        fetched += [first["u"], second["u"], first["normed"], second["normed"]]
        blocks = [((wide * narrow // 2, sum(job_rows), 128), BF)] * 2
        late = [pltpu.VMEM((384, 2 * total), BF)] + [pltpu.VMEM(*b) for b in blocks]
        late.append(pltpu.SemaphoreType.DMA((4,)))
        widths = (feat, hidden, feat, hidden)
        jobs = with_blocks(jobs, lambda g: widths[g], wide, narrow)
    small = [((1, feat), F32), ((1, 128), F32), ((PACK, feat), BF), ((1, feat), F32), ((1, feat), F32)]
    anywhere = pl.BlockSpec(memory_space=pltpu.HBM)
    smem = pl.BlockSpec(memory_space=pltpu.SMEM)
    weights = sum(m.size for m in matrices)
    outs = pl.pallas_call(
        functools.partial(back_kernel, narrow, stages, qlen, 4, n_held, names, jobs, job_rows),
        out_shape=tuple(jax.ShapeDtypeStruct(*s) for s in small + [kinds[n] for n in names] + blocks),
        in_specs=[smem, smem] + [whole()] * 6 + [anywhere] * len(fetched),
        out_specs=(whole(),) * 5 + (anywhere,) * len(names) + (anywhere,) * len(blocks),
        scratch_shapes=held
        + [pltpu.VMEM(*kinds[n]) for n in BACK if n not in PAIRED and n != "grad_x"]
        + [
            pltpu.VMEM((2 * total, feat), BF),
            pltpu.VMEM((2 * total, hidden), BF),
            pltpu.VMEM((2 * total, hidden), BF),
            pltpu.VMEM((2 * total, feat), BF),
            pltpu.VMEM((size, feat), BF),
            pltpu.VMEM((total, feat), F32),
            pltpu.VMEM((total, feat), BF),
            pltpu.SemaphoreType.DMA((len(fetched),)),
            pltpu.SemaphoreType.DMA((len(names),)),
        ]
        + late,
        name="loss_and_back",
        compiler_params=pltpu.CompilerParams(vmem_limit_bytes=(54 if jobs else 56) << 20),
        cost_estimate=pl.CostEstimate(
            flops=3 * total * weights, bytes_accessed=2 * weights, transcendentals=0
        ),
    )(me, sharp, here, there, e, gains, qseg, pseg, *fetched)
    return outs[:5], dict(zip(names, outs[5:])), outs[5 + len(names) :]


REST = ("gy", "gq", "gk", "gv", "grad_x")


def rest_kernel(qlen, buckets, n_held, *refs):
    gains_ref, lookup_ref, gin_ref, gmid_ref, gfin_ref, loss_ref = refs[:6]
    refs = refs[6:]
    hbm, refs = refs[:n_held], refs[n_held:]
    sums_ref, outs, refs = refs[0], dict(zip(REST, refs[1:6])), refs[6:]
    held, refs = refs[:n_held], refs[n_held:]
    keep, refs = dict(zip(REST, refs[:5])), refs[5:]
    go_s, row_s, diag_s, wide_s, in_sem, out_sem = refs
    (ga_s, wg_s, gb_s, wu_s, xm_s, gx_s, wo_s, q_s, k_s, v_s, o_s, pp_s, pq_s, ds_s) = held[:14]
    wq_s, wk_s, wv_s, qx_s, px_s = held[14:]
    fetch = [pltpu.make_async_copy(a, b, in_sem.at[i]) for i, (a, b) in enumerate(zip(hbm, held))]
    for c in fetch:
        c.start()

    def arrive(first, last):
        for i in range(first, last):
            fetch[i].wait()

    def write(name):
        return pltpu.make_async_copy(keep[name], outs[name], out_sem.at[REST.index(name)])

    arrive(0, 2)
    grad = dot_nt(ga_s[...], wg_s[...])
    arrive(2, 6)
    grad = grad + dot_nt(gb_s[...], wu_s[...])
    back, part = through_norm(xm_s[...], gains_ref[1:2, :], grad)
    row_s[1:2, :] = gmid_ref[...] + part
    grad_mid = gx_s[...] + back
    gx_s[...] = grad_mid
    gy = low(grad_mid)
    keep["gy"][...] = gy
    write("gy").start()
    arrive(6, 7)
    go_s[...] = low(dot_nt(gy, wo_s[...]))
    arrive(7, 14)
    attend_back_kernel(
        qlen, q_s, k_s, v_s, o_s, go_s, pp_s, pq_s, ds_s, keep["gq"], keep["gk"], keep["gv"], ds_s
    )
    for name in REST[1:4]:
        write(name).start()
    arrive(14, 19)
    grad = dot_nt(keep["gq"][...], wq_s[...]) + dot_nt(keep["gk"][...], wk_s[...])
    grad = grad + dot_nt(keep["gv"][...], wv_s[...])
    x = jnp.concatenate([qx_s[...], px_s[...]], axis=0).astype(F32)
    back, part = through_norm(x, gains_ref[0:1, :], grad)
    row_s[0:1, :] = gin_ref[...] + part
    keep["grad_x"][...] = gx_s[...] + back
    write("grad_x").start()
    small_kernel(
        buckets, ds_s, lookup_ref, row_s.at[0:1], row_s.at[1:2], gfin_ref, loss_ref, sums_ref, diag_s, wide_s
    )
    for name in REST:
        write(name).wait()


def rest_back(gains, lookup, buckets, small, ga, gb, gx, acc, first, matrices, qx, px):
    wq, wk, wv, wo, wg, wu = matrices[:6]
    total, feat = gx.shape
    heads, plen, _ = acc.shape
    qlen = qx.shape[0]
    t = first
    fetched = [ga, wg, gb, wu, t["x_mid"], gx, wo, t["q"], t["k"], t["v"], t["o"], t["pp"], t["pq"], acc]
    fetched += [wq, wk, wv, qx, px]
    kinds = [((total, feat), BF)] * 4 + [((total, feat), F32)]
    anywhere = pl.BlockSpec(memory_space=pltpu.HBM)
    weights = sum(m.size for m in matrices[:6])
    outs = pl.pallas_call(
        functools.partial(rest_kernel, qlen, buckets, len(fetched)),
        out_shape=tuple(jax.ShapeDtypeStruct(*k) for k in [((4 + heads, feat), F32)] + kinds),
        in_specs=[whole()] * 6 + [anywhere] * len(fetched),
        out_specs=(whole(),) + (anywhere,) * len(kinds),
        scratch_shapes=[pltpu.VMEM(a.shape, a.dtype) for a in fetched]
        + [pltpu.VMEM(*k) for k in kinds]
        + [
            pltpu.VMEM((total, feat), BF),
            pltpu.VMEM((8, feat), F32),
            pltpu.VMEM((heads, 2 * plen), F32),
            pltpu.VMEM((1, 2 * plen), jnp.int32),
            pltpu.SemaphoreType.DMA((len(fetched),)),
            pltpu.SemaphoreType.DMA((len(kinds),)),
        ],
        name="rest_back",
        compiler_params=pltpu.CompilerParams(vmem_limit_bytes=50 << 20),
        cost_estimate=pl.CostEstimate(
            flops=3 * total * weights, bytes_accessed=2 * weights, transcendentals=0
        ),
    )(gains, lookup[None], *small, *fetched)
    return outs


def join_kernel(*refs):
    ins, out_ref = refs[:-1], refs[-1]
    rows = ins[0].shape[0]
    for i, ref in enumerate(ins):
        out_ref[i * rows : (i + 1) * rows, :] = ref[...]


def join(*parts):
    a = parts[0]
    return pl.pallas_call(
        join_kernel,
        out_shape=jax.ShapeDtypeStruct((len(parts) * a.shape[0], a.shape[1]), a.dtype),
        in_specs=[whole()] * len(parts),
        out_specs=whole(),
        name="join",
        compiler_params=pltpu.CompilerParams(vmem_limit_bytes=4 << 20),
    )(*parts)


def stage_orders(wide, narrow):
    wbits = [1 << i for i in range(wide.bit_length() - 1)]
    nbits = [1 << i for i in range(narrow.bit_length() - 1)]
    w = lambda bits: [("wide", b) for b in bits]
    n = [("narrow", b) for b in nbits]
    tail = w(wbits[2:])
    return (w(wbits[:1]) + w(wbits[1:2]) + n + tail, w(wbits[:1]) + n + w(wbits[1:2]) + tail)


def place_of(order, dw, dn):
    place = 0
    for axis, bit in order:
        own = dw if axis == "wide" else dn
        place = place * 2 + (own // bit) % 2
    return place


def traced_place(order, dw, dn):
    place = 0
    for axis, bit in order:
        own = dw if axis == "wide" else dn
        place = place * 2 + (lax.shift_right_logical(own, bit.bit_length() - 1) & 1)
    return place


def weight_products(jobs, held, arrive, me_ref, keep_ref, send_ref, turned_s):
    me_w, me_n = me_ref[0], me_ref[1]
    half = keep_ref.shape[0]

    def store(acc, job, w_first, n_first):
        row_axis, block_rows, block_lanes, targets = job[2:]
        blocks = [
            (bi, bj)
            for bi in range(acc.shape[0] // block_rows)
            for bj in range(acc.shape[1] // block_lanes)
        ]
        bases = [traced_place(t[0], w_first ^ me_w, n_first ^ me_n) for t in targets]
        for core in range(2):

            @pl.when((me_w & 1) == core)
            def _():
                for bi, bj in blocks:
                    w, n = (bi, bj) if row_axis == "wide" else (bj, bi)
                    out_ref = keep_ref if (w & 1) == core else send_ref
                    for (order, first, count, offset), base in zip(targets, bases):
                        at = (base ^ place_of(order, w, n)) & (half - 1)
                        for k in range(block_lanes // 128):
                            lane = bj * block_lanes + k * 128
                            row = bi * block_rows + first
                            out_ref[at, offset + k * count : offset + (k + 1) * count, :] = acc[
                                row : row + count, lane : lane + 128
                            ]

    for job in jobs:
        rg, lg, row_axis, block_rows, block_lanes, targets = job
        arrive(rg)
        arrive(lg)
        row_s, lane_s = held[rg], held[lg]
        depth, rows, lanes = row_s.shape[0], row_s.shape[1], lane_s.shape[1]
        tile_rows = 384
        tile_lanes = block_lanes
        while tile_lanes < 512 and lanes % (2 * tile_lanes) == 0:
            tile_lanes *= 2
        per_row, per_lane = tile_rows // block_rows, tile_lanes // block_lanes

        def row_step(rt, carry):
            mine = row_s[:, pl.ds(pl.multiple_of(rt * tile_rows, 128), tile_rows)]
            if depth > 16:
                turned_s[...] = mine.T

            def lane_step(lt, inner):
                part = lane_s[:, pl.ds(pl.multiple_of(lt * tile_lanes, 128), tile_lanes)]
                acc = product(turned_s[...], part) if depth > 16 else dot_tn(mine, part)
                if row_axis == "wide":
                    store(low(acc), job, rt * per_row, lt * per_lane)
                else:
                    store(low(acc), job, lt * per_lane, rt * per_row)
                return inner

            if lanes == tile_lanes:
                return lane_step(0, carry)
            return lax.fori_loop(0, lanes // tile_lanes, lane_step, carry)

        lax.fori_loop(0, rows // tile_rows, row_step, 0)


def wgrad_kernel(jobs, groups, n_ops, me_ref, *refs):
    ops, (keep_ref, send_ref) = refs[:n_ops], refs[n_ops : n_ops + 2]
    held = refs[n_ops + 2 : n_ops + 2 + len(groups)]
    turned_s, sems = refs[-2:]
    copies = []
    for ids, buf in zip(groups, held):
        first, own = 0, []
        for i in ids:
            count = ops[i].shape[0]
            sem = sems.at[sum(len(c) for c in copies) + len(own)]
            own.append(pltpu.make_async_copy(ops[i], buf.at[first : first + count], sem))
            first += count
        copies.append(own)
    for own in copies:
        for c in own:
            c.start()
    ready = set()

    def arrive(g):
        if g not in ready:
            for c in copies[g]:
                c.wait()
            ready.add(g)

    weight_products(jobs, held, arrive, me_ref, keep_ref, send_ref, turned_s)


def with_blocks(jobs, width, wide, narrow):
    full = []
    for rg, lg, row_axis, targets in jobs:
        split = (wide, narrow) if row_axis == "wide" else (narrow, wide)
        full.append((rg, lg, row_axis, width(rg) // split[0], width(lg) // split[1], targets))
    return full


def wgrad(me, ops, groups, jobs, total_rows, wide, narrow, vmem):
    half = wide * narrow // 2
    width = lambda g: ops[groups[g][0]].shape[1]
    depth = [sum(ops[i].shape[0] for i in g) for g in groups]
    full = with_blocks(jobs, width, wide, narrow)
    flops = sum(2 * depth[j[0]] * width(j[0]) * width(j[1]) for j in full)
    return pl.pallas_call(
        functools.partial(wgrad_kernel, full, groups, len(ops)),
        out_shape=(jax.ShapeDtypeStruct((half, total_rows, 128), BF),) * 2,
        in_specs=[pl.BlockSpec(memory_space=pltpu.SMEM)]
        + [pl.BlockSpec(memory_space=pltpu.HBM)] * len(ops),
        out_specs=(whole(),) * 2,
        scratch_shapes=[pltpu.VMEM((d, width(g)), BF) for g, d in enumerate(depth)]
        + [pltpu.VMEM((384, max(depth)), BF), pltpu.SemaphoreType.DMA((sum(map(len, groups)),))],
        name="wgrad",
        compiler_params=pltpu.CompilerParams(vmem_limit_bytes=vmem << 20),
        cost_estimate=pl.CostEstimate(flops=flops, bytes_accessed=flops // 256, transcendentals=0),
    )(me, *ops)


def swap(a, *stage):
    dw = sum(bit for axis, bit in stage if axis == "wide")
    dn = sum(bit for axis, bit in stage if axis == "narrow")
    wide, narrow = lax.axis_size("wide"), lax.axis_size("narrow")
    if not dn:
        return lax.ppermute(a, "wide", [(i, i ^ dw) for i in range(wide)])
    if not dw:
        return lax.ppermute(a, "narrow", [(i, i ^ dn) for i in range(narrow)])
    pairs = [(i * narrow + j, (i ^ dw) * narrow + (j ^ dn)) for i in range(wide) for j in range(narrow)]
    return lax.ppermute(a, AXES, pairs)


def relatives(stage):
    if len(stage) == 1:
        return [stage]
    return [(stage[1],), (stage[0],), tuple(stage)]


def grouped(order, direct):
    if not direct:
        return [(s,) for s in order]
    return [(s,) for s in order[:-2]] + [tuple(order[-2:])]


class Chunk:
    def __init__(self, keep, send, split, orders, finals, direct=False):
        self.rows, self.split, self.finals = keep.shape[1], split, finals
        self.orders = [grouped(order, direct) for order in orders]
        self.stage, self.parts = 0, [(keep, send)]
        self.done = False

    def spans(self, stage):
        if self.orders[0][stage] == self.orders[1][stage] and (
            stage == 0 or self.orders[0][stage:] == self.orders[1][stage:]
        ):
            return [(0, self.rows, self.orders[0])]
        return [(0, self.split, self.orders[0]), (self.split, self.rows, self.orders[1])]

    def start(self):
        return [
            [swap(a, *to) for a, to in zip(part[1:], relatives(order[self.stage]))]
            for part, (_, _, order) in zip(self.parts, self.spans(self.stage))
        ]


def doubled(value, stages):
    for stage in stages:
        value = value + swap(value, stage)
    return value


def advance(flows):
    operands, shapes, steps = [], [], []
    for f in flows:
        now = f.spans(f.stage)
        last = f.stage == len(f.orders[0]) - 1
        first_in, first_out = len(operands), len(shapes)
        for part, got in zip(f.parts, f.got):
            operands += [part[0]] + got
        half = f.parts[0][0].shape[0] // 2
        if last:
            for kind, offset, rows, lanes in f.finals:
                shapes.append(jax.ShapeDtypeStruct((rows, lanes), F32))
            steps.append(("final", first_in, first_out, f.finals, len(f.got[0])))
        else:
            later = f.spans(f.stage + 1)
            ways = 2 ** len(f.orders[0][f.stage + 1])
            for lo, hi, _ in later:
                shapes += [jax.ShapeDtypeStruct((2 * half // ways, hi - lo, 128), BF)] * ways
            steps.append(
                ("halve", first_in, first_out, [n[:2] for n in now], [n[:2] for n in later], ways)
            )

    def whole_sum(ins, i, count, pick):
        total = pick(ins[i]) + pick(ins[i + 1])
        return total if count == 1 else total + (pick(ins[i + 2]) + pick(ins[i + 3]))

    def body(*refs):
        ins, outs = refs[: len(operands)], refs[len(operands) :]
        for step in steps:
            kind, i, o = step[:3]
            if kind == "final":
                for n, (_, offset, rows, lanes) in enumerate(step[3]):
                    for k in range(lanes // 128):
                        span = pl.ds(offset + k * rows, rows)
                        value = whole_sum(ins, i, step[4], lambda ref: ref[0, span, :].astype(F32))
                        outs[o + n][:, k * 128 : (k + 1) * 128] = value
            else:
                ways = step[5]
                for p, (lo, hi) in enumerate(step[3]):
                    for q, (lo2, hi2) in enumerate(step[4]):
                        a, b = max(lo, lo2), min(hi, hi2)
                        if a >= b:
                            continue
                        keep_ref, got_ref = ins[i + 2 * p], ins[i + 2 * p + 1]
                        count = keep_ref.shape[0] // ways
                        for side in range(ways):
                            out_ref = outs[o + ways * q + side]

                            def block(n, carry):
                                src = pl.ds(a - lo, b - a)
                                value = keep_ref[side * count + n, src, :].astype(F32)
                                value = value + got_ref[side * count + n, src, :].astype(F32)
                                out_ref[n, a - lo2 : b - lo2, :] = low(value)
                                return carry

                            if count == 1:
                                block(0, 0)
                            else:
                                lax.fori_loop(0, count, block, 0)

    room = (1 << 20) + sum(a.size * a.dtype.itemsize for a in operands + shapes)
    outs = pl.pallas_call(
        body,
        out_shape=tuple(shapes),
        in_specs=[whole()] * len(operands),
        out_specs=(whole(),) * len(shapes),
        name="advance",
        compiler_params=pltpu.CompilerParams(vmem_limit_bytes=room),
    )(*operands)
    at = 0
    for f, step in zip(flows, steps):
        f.stage += 1
        if step[0] == "final":
            f.result = [
                out.T if final[0] == "turn" else out
                for out, final in zip(outs[at : at + len(step[3])], step[3])
            ]
            at += len(step[3])
            f.done = True
        else:
            ways = step[5]
            f.parts = [tuple(outs[at + ways * q : at + ways * (q + 1)]) for q in range(len(step[4]))]
            at += ways * len(step[4])


def exchange(begin, compute, inputs):
    sent, inputs = lax.optimization_barrier(([f.parts for f in begin], inputs))
    for f, value in zip(begin, sent):
        f.parts = value
    for f in begin:
        f.got = f.start()
    got, made = lax.optimization_barrier(([f.got for f in begin], compute(*inputs)))
    for f, value in zip(begin, got):
        f.got = value
    advance(begin)
    return made


def gather_stages(order):
    far, near = order[3:], order[1:3]
    return [far[i : i + 2] for i in range(0, len(far), 2)] + [near] + [order[:1]]


def gather_all(rows, stages):
    for stage in stages[:-1]:
        got = [swap(rows, *to) for to in ([stage] if len(stage) == 1 else [stage[:1], stage[1:], stage])]
        rows = join(rows, *got)
    return rows, swap(rows, *stages[-1])


def local(
    wide,
    narrow,
    query_x,
    query_seg,
    passage_x,
    passage_seg,
    labels,
    lookup,
    softness,
    bias_grid,
    gains,
    wq,
    wk,
    wv,
    wo,
    wg,
    wu,
    wd,
    wp,
):
    qrows, qlen, feat = query_x.shape
    prows, plen, _ = passage_x.shape
    buckets, heads = bias_grid.shape
    order_a, order_b = stage_orders(wide, narrow)
    me_w, me_n = lax.axis_index("wide"), lax.axis_index("narrow")
    me = jnp.stack([me_w, me_n]).astype(jnp.int32)

    hidden = wd.shape[0]
    block, cols, ff_block, ff_cols = feat // wide, feat // narrow, hidden // wide, hidden // narrow
    matrices = (wq, wk, wv, wo, wg, wu, wd, wp)
    (packed, vectors, e, pooled, x_between, x_last), (first, second) = forward(
        query_x.reshape(-1, feat),
        passage_x.reshape(-1, feat),
        lookup,
        bias_grid.T,
        query_seg,
        passage_seg,
        gains,
        labels,
        matrices,
    )
    down_rows, att_rows = block * ff_cols // 128, block * cols // 128
    jobs = None
    if not (cols % 128 or ff_block % 128 or block % 16):
        jobs = [
            (0, 1, "wide", [(order_a, 0, block, 0)]),
            (2, 3, "narrow", [(order_b, 0, cols, down_rows)]),
        ]
    groups = gather_stages(order_a)
    stages = [bit for group in groups for bit in group]
    here, there = gather_all(packed, groups)
    (gain_final, loss_part, grad_e, gain_mid, gain_in), back, parts = loss_and_back(
        me, narrow, stages, softness, here, there, e, gains, query_seg, passage_seg,
        x_last, x_between, first, second, matrices, wide, jobs, (down_rows, cols),
    )
    grad_b, grad_b_2 = back["gb1"], back["gb"]
    att_2 = (back["gy"], back["gq"], back["gk"], back["gv"])
    h, o, normed, u = (first[name] for name in ("h", "o", "normed", "u"))
    h_2, o_2, normed_2, u_2 = (second[name] for name in ("h", "o", "normed", "u"))

    def split_sums(value):
        return value[:3], value[4 : 4 + heads, :buckets], value[3, :1]

    def finish(grad_a, grad_b):
        return rest_back(
            gains, lookup, buckets, (gain_in, gain_mid, gain_final, loss_part), grad_a, grad_b,
            back["grad_x"], back["ds"], first, matrices, query_x.reshape(-1, feat), passage_x.reshape(-1, feat),
        )

    if jobs is None:
        grad_f, grad_a = back["grad_f1"], back["ga1"]
        ffn_2 = (back["grad_f"], back["ga"], grad_b_2)
        sums, grad_y, grad_q, grad_k, grad_v, grad_x = finish(grad_a, grad_b)
        outs = split_sums(doubled(sums, order_a))

        def scatter(*pairs):
            full = low(sum(dot_tn(left, right) for left, right in pairs))
            full = lax.psum_scatter(full, "wide", scatter_dimension=1, tiled=True)
            return lax.psum_scatter(full, "narrow", scatter_dimension=0, tiled=True).astype(F32)

        grad_query = scatter((h, grad_q), (h_2, att_2[1]))
        grad_key = scatter((h, grad_k), (h_2, att_2[2]))
        grad_value = scatter((h, grad_v), (h_2, att_2[3]))
        grad_out = scatter((o, grad_y), (o_2, att_2[0]))
        grad_gate = scatter((normed, grad_a), (normed_2, ffn_2[1]))
        grad_up = scatter((normed, grad_b), (normed_2, ffn_2[2]))
        grad_down = scatter((u, grad_f), (u_2, ffn_2[0]))
        grad_proj = scatter((pooled, grad_e))
    else:
        orders = (order_a, order_b)
        finals = [("turn", 0, block, ff_cols), ("keep", down_rows, cols, ff_block)]
        ffn = Chunk(*parts, down_rows, orders, finals)

        cut = (cols + att_rows) // 2 // 16 * 16

        def make_up(grad_b, grad_b_2):
            return wgrad(
                me,
                [normed, normed_2, grad_b, grad_b_2, grad_e, pooled],
                [(0, 1), (2, 3), (4,), (5,)],
                [
                    (2, 3, "wide", [(order_b, 0, block, cols)]),
                    (0, 1, "narrow", [(order_a, 0, cut, 0), (order_b, cut, cols - cut, cut)]),
                ],
                cols + att_rows,
                wide,
                narrow,
                52,
            )

        parts = exchange([ffn], make_up, (grad_b, grad_b_2))
        finals = [("keep", 0, cols, ff_block), ("turn", cols, block, cols)]
        up = Chunk(*parts, cut, orders, finals)

        sums, *grads, grad_x = exchange([ffn, up], finish, (back["ga1"], grad_b))

        def make_rest(sums, grad_y, grad_q, grad_k, grad_v):
            got = swap(sums, order_a[-2])
            parts = wgrad(
                me,
                [grad_y, att_2[0], o, o_2, grad_q, att_2[1], h, h_2, grad_k, att_2[2], grad_v, att_2[3]],
                [(0, 1), (2, 3), (4, 5), (6, 7), (8, 9), (10, 11)],
                [
                    (0, 1, "wide", [(order_a, 0, block, 0)]),
                    (2, 3, "wide", [(order_a, 0, block, att_rows)]),
                    (4, 3, "wide", [(order_b, 0, block, 2 * att_rows)]),
                    (5, 3, "wide", [(order_b, 0, block, 3 * att_rows)]),
                ],
                4 * att_rows,
                wide,
                narrow,
                12,
            )
            got, parts = lax.optimization_barrier((got, parts))
            return parts, sums + got

        parts, sums = exchange([ffn, up], make_rest, (sums, *grads))
        att = Chunk(*parts, 2 * att_rows, orders, [("turn", i * att_rows, block, cols) for i in range(4)], True)
        for stage in order_a[-1:] + order_a[:2]:
            live = [f for f in (att, up, ffn) if not f.done]
            sums = exchange(live, lambda value: doubled(value, [stage]), (sums,))
        outs = exchange([att], lambda value: split_sums(doubled(value, order_a[2:-2])), (sums,))
        grad_down, grad_gate = ffn.result
        grad_up, grad_proj = up.result
        grad_out, grad_query, grad_key, grad_value = att.result
    gain_total, bucket_total, loss_total = outs
    mean_loss = loss_total / (qrows * QSEGS * wide * narrow)
    return (
        mean_loss,
        vectors[:QSEGS],
        vectors[QSEGS : QSEGS + PSEGS],
        grad_x[:qlen].reshape(1, qlen, feat),
        grad_x[qlen:].reshape(1, plen, feat),
        gain_total,
        bucket_total.T,
        grad_query,
        grad_key,
        grad_value,
        grad_out,
        grad_gate,
        grad_up,
        grad_down,
        grad_proj,
    )


def solution(mesh):
    rows3, rows2, rows1 = P(AXES, None, None), P(AXES, None), P(AXES)
    return jax.shard_map(
        functools.partial(local, mesh.shape["wide"], mesh.shape["narrow"]),
        mesh=mesh,
        in_specs=(rows3, rows2, rows3, rows2, rows1) + (P(),) * 12,
        out_specs=(P(), rows2, rows2, rows3, rows3, P(), P()) + (P("narrow", "wide"),) * 8,
        check_vma=False,
    )
```
